32 devices in a mesh: grp: 8 (over z, x), dev: 4 (over y, core).
Axes of the slice: x: 2, y: 2, z: 4, core: 2. Of those that a mesh axis runs over, the one named last changes fastest.
Arguments:
- node_src: bfloat16 [4096, 1024], P(('grp', 'dev'))
- hub_feat: bfloat16 [4096, 1024], P(('grp', 'dev'))
- w_query: bfloat16 [1024, 1024], replicated, may hold values from -0.1875 to 0.1875
- w_key: bfloat16 [1024, 1024], replicated, may hold values from -0.1875 to 0.1875
- w_value: bfloat16 [1024, 1024], replicated, may hold values from -0.1875 to 0.1875
- w_out: bfloat16 [1024, 1024], replicated, may hold values from -0.75 to 0.75
- w_att: bfloat16 [16, 16, 64, 64], replicated, may hold values from -0.75 to 0.75
- w_msg: bfloat16 [16, 16, 64, 64], replicated, may hold values from -0.75 to 0.75
- relation_prior: float32 [16, 16], replicated, may hold values from 0.5 to 2
- block_src: int32 [32, 40], P(('grp', 'dev')), may hold values from 0 to 7
- block_dst: int32 [32, 40], P(('grp', 'dev')), may hold values from 0 to 3
- block_type: int32 [32, 40], P(('grp', 'dev')), may hold values from 0 to 15
- block_count: int32 [32], P(('grp', 'dev')), may hold values from 20 to 40, as said below
Outputs:
- hub_out: bfloat16 [4096, 1024], P(('grp', 'dev'))
The draws below stay inside these ranges and needn't reach their ends.
Inputs may be any that keep to these rules, and one draw needn't show every extreme that they name: `block_count`: some device uses all 40 slots; every hub tile of a group is the target of some used block of that group.
All inputs are finite; a program needn't handle non-finite values.
Results may differ from the reference program's by a relative error of at most 0.018.
The reference program's roundings to bfloat16 on the way (of `queries`, `keyval`, `weight_half` and `aggregate`) count: a program that leaves them out, or rounds other values in their place, can miss the bound.
Values may be sent and summed in bfloat16 or wider, within the bound.
No kernel may reach another device: no remote copies, remote signals or barrier semaphores. Data moves between devices by JAX's collectives and lax.ppermute only.
A program may use at most 128 MiB of HBM per device.

```python
import math
import jax
import jax.numpy as jnp
from jax import lax

D = 1024
HEADS = 16
RELATIONS = 16
TILE = 128
BLK_DEV = 40
HEAD_DIM = 64
GROUPS = 8
OWNERS = 4
HUBS = 4096
SOURCES = 4096


def block_lists(key):
    base = jax.random.fold_in(key, 11)
    keys = jax.random.split(base, 8)
    total = GROUPS * OWNERS
    first = jax.random.randint(keys[0], (total,), BLK_DEV // 2, BLK_DEV + 1)
    second = jax.random.randint(keys[1], (total,), BLK_DEV // 2, BLK_DEV + 1)
    counts = jnp.minimum(first, second)
    chosen = jax.random.randint(keys[2], (), 0, total)
    flat = jnp.arange(total)
    counts = jnp.where(flat == chosen, BLK_DEV, counts)
    sources = jax.random.randint(keys[3], (total, BLK_DEV), 0, GROUPS)
    dests = jnp.minimum(jax.random.randint(keys[4], (total, BLK_DEV), 0, OWNERS), jax.random.randint(keys[5], (total, BLK_DEV), 0, OWNERS))
    shifts = jax.random.randint(keys[6], (GROUPS,), 0, OWNERS)
    cover = (flat % OWNERS + shifts[flat // OWNERS]) % OWNERS
    dests = dests.at[:, 0].set(cover)
    types = jax.random.randint(keys[7], (total, BLK_DEV), 0, RELATIONS)
    return (sources.astype(jnp.int32), dests.astype(jnp.int32), types.astype(jnp.int32), counts.astype(jnp.int32))


def feature_rows(key, total_rows):
    values = jax.random.normal(jax.random.fold_in(key, 5), (total_rows, D), jnp.float32)
    values = jnp.clip(values, -6.0, 6.0)
    return values.astype(jnp.bfloat16)


def draw_node_src(key, part):
    return feature_rows(jax.random.fold_in(key, 21), SOURCES)


def draw_hub_feat(key, part):
    return feature_rows(jax.random.fold_in(key, 23), HUBS)


def draw_block_src(key, part):
    return block_lists(key)[0]


def draw_block_dst(key, part):
    return block_lists(key)[1]


def draw_block_type(key, part):
    return block_lists(key)[2]


def draw_block_count(key, part):
    return block_lists(key)[3]


def bell_draw(key, extent, width, most, dtype=jnp.bfloat16):
    return jnp.clip(width * jax.random.normal(key, extent, jnp.float32), -most, most).astype(dtype)


def setup_inputs(seed: int = 0) -> dict:
    splits = jax.random.split(jax.random.key(seed), 14)
    return {
        "node_src": draw_node_src(jax.random.fold_in(splits[13], 71), 0),
        "hub_feat": draw_hub_feat(jax.random.fold_in(splits[13], 71), 0),
        "w_query": bell_draw(splits[2], (D, D), D ** -0.5, 0.1875),
        "w_key": bell_draw(splits[3], (D, D), D ** -0.5, 0.1875),
        "w_value": bell_draw(splits[4], (D, D), D ** -0.5, 0.1875),
        "w_out": bell_draw(splits[5], (D, D), (D // 16) ** -0.5, 0.75),
        "w_att": bell_draw(splits[6], (RELATIONS, HEADS, HEAD_DIM, HEAD_DIM), HEAD_DIM ** -0.5, 0.75),
        "w_msg": bell_draw(splits[7], (RELATIONS, HEADS, HEAD_DIM, HEAD_DIM), HEAD_DIM ** -0.5, 0.75),
        "relation_prior": jnp.clip(jnp.exp(jax.random.uniform(splits[8], (RELATIONS, HEADS), jnp.float32, math.log(0.5), math.log(2.0))), 0.5, 2.0),
        "block_src": draw_block_src(jax.random.fold_in(splits[13], 71), 0),
        "block_dst": draw_block_dst(jax.random.fold_in(splits[13], 71), 0),
        "block_type": draw_block_type(jax.random.fold_in(splits[13], 71), 0),
        "block_count": draw_block_count(jax.random.fold_in(splits[13], 71), 0),
    }


def key_map(keyval, src_tile, w_att, rtype):
    rows = lax.dynamic_slice_in_dim(keyval, (src_tile * TILE).astype(jnp.int32), TILE, 0)
    keys = rows[:, :D].reshape(TILE, HEADS, HEAD_DIM).astype(jnp.float32)
    return jnp.einsum('shd,hde->she', keys, w_att[rtype].astype(jnp.float32)).astype(jnp.bfloat16)

def msg_map(keyval, src_tile, w_msg, rtype):
    rows = lax.dynamic_slice_in_dim(keyval, (src_tile * TILE).astype(jnp.int32), TILE, 0)
    values = rows[:, D:].reshape(TILE, HEADS, HEAD_DIM).astype(jnp.float32)
    return jnp.einsum('shd,hde->she', values, w_msg[rtype].astype(jnp.float32)).astype(jnp.bfloat16)

def block_scores(queries, dst_tile, key_rel, prior_row):
    tile_q = lax.dynamic_slice_in_dim(queries, (dst_tile * TILE).astype(jnp.int32), TILE, 0)
    tile_q = tile_q.reshape(TILE, HEADS, HEAD_DIM).astype(jnp.float32)
    scores = jnp.einsum('thd,shd->hts', tile_q, key_rel.astype(jnp.float32))
    return scores * (prior_row / jnp.sqrt(jnp.float32(HEAD_DIM)))[:, None, None]

def reference(node_src, hub_feat, w_query, w_key, w_value, w_out, w_att, w_msg, relation_prior, block_src, block_dst, block_type, block_count):
    queries = jnp.dot(hub_feat, w_query, preferred_element_type=jnp.float32).astype(jnp.bfloat16)
    keyval = jnp.dot(node_src, jnp.concatenate([w_key, w_value], axis=1), preferred_element_type=jnp.float32).astype(jnp.bfloat16)
    flat = jnp.arange(GROUPS * OWNERS).astype(jnp.int32)
    group = flat // OWNERS
    member = flat % OWNERS
    src_tiles = (block_src * OWNERS + member[:, None]).reshape(-1).astype(jnp.int32)
    dst_tiles = (group[:, None] * OWNERS + block_dst).reshape(-1).astype(jnp.int32)
    types = block_type.reshape(-1).astype(jnp.int32)
    valid = (jnp.arange(BLK_DEV).astype(jnp.int32)[None, :] < block_count[:, None]).reshape(-1)

    def first_pass(highest, item):
        src_tile, dst_tile, rtype, used = item
        key_rel = key_map(keyval, src_tile, w_att, rtype)
        scores = block_scores(queries, dst_tile, key_rel, relation_prior[rtype])
        block_top = jnp.where(used, scores.max(axis=2).T, jnp.float32(-1e+30))
        start = (dst_tile * TILE).astype(jnp.int32)
        old = lax.dynamic_slice_in_dim(highest, start, TILE, 0)
        return (lax.dynamic_update_slice_in_dim(highest, jnp.maximum(old, block_top), start, 0), None)
    highest0 = jnp.full((HUBS, HEADS), -1e+30, jnp.float32)
    highest, _ = lax.scan(first_pass, highest0, (src_tiles, dst_tiles, types, valid))

    def second_pass(carry, item):
        denom, total = carry
        src_tile, dst_tile, rtype, used = item
        key_rel = key_map(keyval, src_tile, w_att, rtype)
        message = msg_map(keyval, src_tile, w_msg, rtype)
        scores = block_scores(queries, dst_tile, key_rel, relation_prior[rtype])
        start = (dst_tile * TILE).astype(jnp.int32)
        tile_top = lax.dynamic_slice_in_dim(highest, start, TILE, 0)
        weight = jnp.where(used, jnp.exp(scores - tile_top.T[:, :, None]), jnp.float32(0.0))
        weight_half = weight.astype(jnp.bfloat16).astype(jnp.float32)
        summed = jnp.einsum('hts,she->the', weight_half, message.astype(jnp.float32)).reshape(TILE, D)
        old_d = lax.dynamic_slice_in_dim(denom, start, TILE, 0)
        old_t = lax.dynamic_slice_in_dim(total, start, TILE, 0)
        denom = lax.dynamic_update_slice_in_dim(denom, old_d + weight.sum(axis=2).T, start, 0)
        total = lax.dynamic_update_slice_in_dim(total, old_t + summed, start, 0)
        return ((denom, total), None)
    init = (jnp.zeros((HUBS, HEADS), jnp.float32), jnp.zeros((HUBS, D), jnp.float32))
    (denom, total), _ = lax.scan(second_pass, init, (src_tiles, dst_tiles, types, valid))
    aggregate = (total / jnp.repeat(denom, HEAD_DIM, axis=1)).astype(jnp.bfloat16)
    return jnp.dot(aggregate, w_out, preferred_element_type=jnp.float32).astype(jnp.bfloat16)
```

```python
import functools

import jax
import jax.numpy as jnp
from jax import lax
from jax.experimental import pallas as pl
from jax.experimental.pallas import tpu as pltpu
from jax.sharding import PartitionSpec as P

BF = jnp.bfloat16
F32 = jnp.float32
LOG2E = 1.4426950408889634
EMPTY = -1e30
LANES = 128
UNROLL = 4


def pair_diag(w):
    zero = jnp.zeros_like(w[:, 0::2])
    upper = jnp.concatenate([w[:, 0::2], zero], axis=3)
    lower = jnp.concatenate([zero, w[:, 1::2]], axis=3)
    return jnp.concatenate([upper, lower], axis=2)


def split3(x):
    hi = x.astype(BF)
    rest = x - hi.astype(F32)
    mid = rest.astype(BF)
    lo = (rest - mid.astype(F32)).astype(BF)
    return hi, mid, lo


def attend(
    owners,
    heads,
    tile,
    head_dim,
    info,
    b_src,
    b_dst,
    b_type,
    prior,
    src,
    hub,
    wq,
    wk,
    wv,
    watt,
    wmsg,
    *rest,
):
    outs = rest[:owners]
    w_both, keys, values_t, queries_t, acc, top, den, stats = rest[owners:]
    step = pl.program_id(0)
    count = info[0]
    groups = src.shape[0] // tile
    width = 2 * head_dim

    w_both[:, :width] = wk[...]
    w_both[:, width:] = wv[...]

    def project(g, _):
        rows = pl.ds(pl.multiple_of(g * tile, tile), tile)
        kv = jnp.dot(src[rows, :], w_both[...], preferred_element_type=F32)
        keys[g] = kv[:, :width].astype(BF)
        values_t[g] = kv[:, width:].T.astype(BF)
        return 0

    lax.fori_loop(0, groups, project, 0)

    def project_q(t, _):
        rows = pl.ds(pl.multiple_of(t * tile, tile), tile)
        q = jnp.dot(hub[rows, :], wq[...], preferred_element_type=F32)
        queries_t[t] = q.T.astype(BF)
        acc[t] = jnp.zeros((width, tile), F32)
        top[t] = jnp.full((2, tile), EMPTY, F32)
        den[t] = jnp.zeros((2, tile), F32)
        return 0

    lax.fori_loop(0, owners, project_q, 0)

    lane = lax.broadcasted_iota(jnp.int32, (tile, width), 1)
    first = lane < head_dim

    def some_blocks(c, _):
        done = []
        for u in range(UNROLL):
            j = c * UNROLL + u
            valid = j < count
            jj = jnp.where(valid, j, 0)
            s_tile, d_tile, rtype = b_src[0, jj], b_dst[0, jj], b_type[0, jj]
            key_rel = jnp.dot(keys[s_tile], watt[rtype, 0], preferred_element_type=F32).astype(BF)
            zero = jnp.zeros_like(key_rel)
            stacked = jnp.concatenate(
                [jnp.where(first, key_rel, zero), jnp.where(first, zero, key_rel)], axis=0
            )
            scores = jnp.dot(stacked, queries_t[d_tile], preferred_element_type=F32)
            message_t = jnp.dot(
                wmsg[rtype, 0], values_t[s_tile], preferred_element_type=F32
            ).astype(BF)
            tops, sums, parts = [], [], []
            for i in range(2):
                scale = prior[rtype, 2 * step + i] * (LOG2E / float(head_dim) ** 0.5)
                s = scores[i * tile : (i + 1) * tile, :] * scale
                m = jnp.max(s, axis=0, keepdims=True)
                p = jnp.exp2(s - m)
                sums.append(jnp.sum(p, axis=0, keepdims=True))
                tops.append(m)
                parts.append(
                    jnp.dot(
                        message_t[i * head_dim : (i + 1) * head_dim, :],
                        p.astype(BF),
                        preferred_element_type=F32,
                    )
                )
            done.append((valid, d_tile, tops, sums, parts))
        for valid, d_tile, tops, sums, parts in done:
            for i in range(2):
                old = top[d_tile, i : i + 1, :]
                new = jnp.where(valid, jnp.maximum(old, tops[i]), old)
                keep = jnp.exp2(old - new)
                take = jnp.where(valid, jnp.exp2(tops[i] - new), 0.0)
                top[d_tile, i : i + 1, :] = new
                den[d_tile, i : i + 1, :] = den[d_tile, i : i + 1, :] * keep + sums[i] * take
                rows = pl.ds(i * head_dim, head_dim)
                acc[d_tile, rows, :] = acc[d_tile, rows, :] * keep + parts[i] * take
        return 0

    lax.fori_loop(0, (count + UNROLL - 1) // UNROLL, some_blocks, 0)

    for t in range(owners):
        for i in range(2):
            total = den[t, i : i + 1, :]
            some = total > 0.0
            safe = jnp.where(some, total, 1.0)
            lse = jnp.where(some, top[t, i : i + 1, :] + jnp.log(safe) * LOG2E, EMPTY)
            stats[t, pl.ds(2 * step + i, 1), :] = lse
            rows = pl.ds(pl.multiple_of((2 * step + i) * head_dim, head_dim), head_dim)
            outs[t][rows, :] = (acc[t, pl.ds(i * head_dim, head_dim), :] * (1.0 / safe)).astype(BF)

    @pl.when(step == pl.num_programs(0) - 1)
    def _():
        for t in range(owners):
            parts = split3(stats[t])
            for k in range(3):
                outs[t][pl.ds(heads * head_dim + k * heads, heads), :] = parts[k]


def combine(owners, heads, head_dim, *refs):
    parts, w_out, out, agg = refs[:owners], refs[owners], refs[owners + 1], refs[owners + 2]
    base = heads * head_dim
    lse = []
    for r in parts:
        hi, mid, lo = (
            r[pl.ds(base + k * heads, heads), :].astype(F32) for k in range(3)
        )
        lse.append((hi + mid) + lo)
    best = functools.reduce(jnp.maximum, lse)
    weights = [jnp.exp2(v - best) for v in lse]
    whole = functools.reduce(jnp.add, weights)
    weights = [w / whole for w in weights]
    for h in range(heads):
        rows = pl.ds(h * head_dim, head_dim)
        total = functools.reduce(
            jnp.add,
            [r[rows, :].astype(F32) * w[h : h + 1, :] for r, w in zip(parts, weights)],
        )
        agg[:, h * head_dim : (h + 1) * head_dim] = total.T.astype(BF)
    out[...] = jnp.dot(agg[...], w_out[...], preferred_element_type=F32).astype(BF)


def body(
    node_src,
    hub_feat,
    w_query,
    w_key,
    w_value,
    w_out,
    w_att,
    w_msg,
    relation_prior,
    block_src,
    block_dst,
    block_type,
    block_count,
):
    groups = lax.axis_size("grp")
    owners = lax.axis_size("dev")
    tile, width = hub_feat.shape
    relations, heads = relation_prior.shape
    head_dim = width // heads
    pair = 2 * head_dim
    slots = block_src.shape[1]
    my_grp = lax.axis_index("grp")
    my_dev = lax.axis_index("dev")

    all_src = [node_src]
    all_hub = [hub_feat]
    for k in range(1, owners):
        all_hub.append(lax.ppermute(hub_feat, "dev", [(i, i ^ k) for i in range(owners)]))
    swap = [(i, i ^ 1) for i in range(groups)]
    all_src = {0: node_src, 1: lax.ppermute(node_src, "grp", swap)}
    order = [2, 6, 4] if groups == 8 else list(range(2, groups, 2))
    for k in order:
        all_src[k] = lax.ppermute(node_src, "grp", [(i, i ^ k) for i in range(groups)])
    for k in order:
        all_src[k + 1] = lax.ppermute(all_src[k], "grp", swap)
    src = jnp.concatenate([all_src[k] for k in range(groups)], axis=0)
    hub = jnp.concatenate(all_hub, axis=0)

    att = pair_diag(w_att)
    msg = pair_diag(jnp.swapaxes(w_msg, 2, 3))
    rows_out = width + 3 * heads
    whole = lambda shape: pl.BlockSpec(shape, lambda h, *_: (0,) * len(shape))
    column = pl.BlockSpec((width, pair), lambda h, *_: (0, h))
    maps = pl.BlockSpec((relations, 1, pair, pair), lambda h, *_: (0, h, 0, 0))
    blocks = slots * heads
    tiles = pl.pallas_call(
        functools.partial(attend, owners, heads, tile, head_dim),
        grid_spec=pltpu.PrefetchScalarGridSpec(
            num_scalar_prefetch=5,
            grid=(heads // 2,),
            in_specs=[whole(src.shape), whole(hub.shape), column, column, column, maps, maps],
            out_specs=[whole((rows_out, tile))] * owners,
            scratch_shapes=[
                pltpu.VMEM((width, 2 * pair), BF),
                pltpu.VMEM((groups, tile, pair), BF),
                pltpu.VMEM((groups, pair, tile), BF),
                pltpu.VMEM((owners, pair, tile), BF),
                pltpu.VMEM((owners, pair, tile), F32),
                pltpu.VMEM((owners, 2, tile), F32),
                pltpu.VMEM((owners, 2, tile), F32),
                pltpu.VMEM((owners, heads, tile), F32),
            ],
        ),
        out_shape=[jax.ShapeDtypeStruct((rows_out, tile), BF)] * owners,
        cost_estimate=pl.CostEstimate(
            flops=blocks * tile * tile * head_dim * 8, bytes_accessed=1 << 24, transcendentals=0
        ),
        name="attend",
    )(
        block_count,
        block_src ^ my_grp,
        block_dst ^ my_dev,
        block_type,
        relation_prior,
        src,
        hub,
        w_query,
        w_key,
        w_value,
        att,
        msg,
    )
    parts = [tiles[0]]
    for k in range(1, owners):
        parts.append(lax.ppermute(tiles[k], "dev", [(i, i ^ k) for i in range(owners)]))
    return pl.pallas_call(
        functools.partial(combine, owners, heads, head_dim),
        out_shape=jax.ShapeDtypeStruct((tile, width), BF),
        scratch_shapes=[pltpu.VMEM((tile, width), BF)],
        name="combine",
    )(*parts, w_out)


def solution(mesh):
    rows = P(("grp", "dev"), None)
    placed = (rows, rows) + (P(),) * 7 + (rows,) * 3 + (P(("grp", "dev")),)
    return jax.shard_map(body, mesh=mesh, in_specs=placed, out_specs=rows, check_vma=False)
```

```python
import functools

import jax
import jax.numpy as jnp
from jax import lax
from jax.experimental import pallas as pl
from jax.experimental.pallas import tpu as pltpu
from jax.sharding import PartitionSpec as P

BF = jnp.bfloat16
F32 = jnp.float32
LOG2E = 1.4426950408889634
EMPTY = -1e30
BLOCKS = 2
LAGS = (4, 8, 12)
LIMIT = 16 << 20


def split3(x):
    hi = x.astype(BF)
    rest = x - hi.astype(F32)
    mid = rest.astype(BF)
    lo = (rest - mid.astype(F32)).astype(BF)
    return hi, mid, lo


def prepare(att, msg, att_out, msg_out):
    kinds, pairs, pair, head_dim = att.shape
    row = lax.broadcasted_iota(jnp.int32, (pair, head_dim), 0)
    col = lax.broadcasted_iota(jnp.int32, (pair, head_dim), 1)
    twice = jnp.where((row & (head_dim - 1)) == col, 1.0, 0.0).astype(BF)
    r2 = lax.broadcasted_iota(jnp.int32, (pair, pair), 0)
    c2 = lax.broadcasted_iota(jnp.int32, (pair, pair), 1)
    same = (r2 < head_dim) == (c2 < head_dim)
    dims = (((1,), (1,)), ((), ()))
    for r in range(kinds):
        for h in range(pairs):
            a = lax.dot_general(att[r, h], twice, dims, preferred_element_type=F32)
            att_out[r, h] = jnp.where(same, a, 0.0).astype(BF)
            m = lax.dot_general(twice, msg[r, h], dims, preferred_element_type=F32)
            msg_out[r, h] = jnp.where(same, m, 0.0).astype(BF)


def run_blocks(
    owners, heads, tile, head_dim, slots, count, b_src, b_dst, b_type, prior, tiles, wk, wv, att, msg,
    queries, acc, top, den, order, src, keys, values,
):
    width = heads * head_dim
    pair, quad = 2 * head_dim, 4 * head_dim
    quads = heads // 4
    for i, ref in enumerate(tiles):
        src[i * tile : (i + 1) * tile, :] = ref[...]
    for q in range(quads):
        cols = slice(q * quad, (q + 1) * quad)
        k = jnp.dot(src[...], wk[:, cols], preferred_element_type=F32)
        v = jnp.dot(src[...], wv[:, cols], preferred_element_type=F32)
        for i in range(len(slots)):
            rows = slice(i * tile, (i + 1) * tile)
            keys[i, q] = k[rows, :].astype(BF)
            values[i, q] = v[rows, :].T.astype(BF)

    def pick(j, n):
        s = b_src[0, j]
        which = jnp.int32(0)
        hit = s == slots[0]
        for i in range(1, len(slots)):
            here = s == slots[i]
            which = jnp.where(here, i, which)
            hit = hit | here
        order[0, n] = j
        order[1, n] = which
        return n + hit.astype(jnp.int32)

    total = lax.fori_loop(0, count[0], pick, jnp.int32(0))
    lane = lax.broadcasted_iota(jnp.int32, (tile, pair), 1)
    left = lane < head_dim
    none = jnp.zeros((pair, pair), BF)

    def diag(w, r, q):
        upper = jnp.concatenate([w[r, 2 * q], none], axis=1)
        lower = jnp.concatenate([none, w[r, 2 * q + 1]], axis=1)
        return jnp.concatenate([upper, lower], axis=0)

    def some_blocks(c, _):
        blocks = []
        for u in range(BLOCKS):
            n = c * BLOCKS + u
            valid = n < total
            j = jnp.where(valid, order[0, n], 0)
            s = jnp.where(valid, order[1, n], 0)
            blocks.append((valid, s, b_dst[0, j], b_type[0, j]))

        def maps(u, q):
            _, s, _, r = blocks[u]
            key_rel = jnp.dot(keys[s, q], diag(att, r, q), preferred_element_type=F32).astype(BF)
            message = jnp.dot(diag(msg, r, q), values[s, q], preferred_element_type=F32).astype(BF)
            return key_rel, message

        def scores(u, h, key_rel):
            _, _, d, _ = blocks[u]
            k = key_rel[:, (h % 2) * pair : (h % 2 + 1) * pair]
            zero = jnp.zeros_like(k)
            both = jnp.concatenate([jnp.where(left, k, zero), jnp.where(left, zero, k)], axis=0)
            q = queries[d, h * pair : (h + 1) * pair, :]
            return jnp.dot(both, q, preferred_element_type=F32)

        def weigh(u, h, s):
            _, _, _, r = blocks[u]
            found = []
            for i in range(2):
                scale = prior[r, 2 * h + i] * (LOG2E / float(head_dim) ** 0.5)
                x = s[i * tile : (i + 1) * tile, :] * scale
                m = jnp.max(x, axis=0, keepdims=True)
                p = jnp.exp2(x - m)
                found.append((m, jnp.sum(p, axis=0, keepdims=True), p.astype(BF)))
            return found

        def gather(u, h, message, found):
            valid, _, d, _ = blocks[u]
            for i in range(2):
                row = (h % 2) * pair + i * head_dim
                m, total_w, p = found[i]
                part = jnp.dot(message[row : row + head_dim, :], p, preferred_element_type=F32)
                head = 2 * h + i
                one = slice(head, head + 1)
                rows = slice(head * head_dim, (head + 1) * head_dim)
                old = top[d, one, :]
                new = jnp.where(valid, jnp.maximum(old, m), old)
                keep = jnp.exp2(old - new)
                add = jnp.where(valid, jnp.exp2(m - new), 0.0)
                top[d, one, :] = new
                den[d, one, :] = den[d, one, :] * keep + total_w * add
                acc[d, rows, :] = acc[d, rows, :] * keep + part * add

        items = [(u, h) for u in range(BLOCKS) for h in range(heads // 2)]
        mapped, scored, weighed = {}, {}, {}
        a, b, d = LAGS
        for t in range(len(items) + d):
            if t < len(items) and items[t][1] % 2 == 0:
                u, h = items[t]
                mapped[u, h // 2] = maps(u, h // 2)
            if 0 <= t - a < len(items):
                u, h = items[t - a]
                scored[u, h] = scores(u, h, mapped[u, h // 2][0])
            if 0 <= t - b < len(items):
                u, h = items[t - b]
                weighed[u, h] = weigh(u, h, scored.pop((u, h)))
            if 0 <= t - d < len(items):
                u, h = items[t - d]
                gather(u, h, mapped[u, h // 2][1], weighed.pop((u, h)))
        return 0

    lax.fori_loop(0, (total + BLOCKS - 1) // BLOCKS, some_blocks, 0)


def first_phase(shape, slots, *refs):
    owners, heads, tile, head_dim = shape
    n = len(slots)
    count, b_src, b_dst, b_type, prior = refs[:5]
    tiles = refs[5 : 5 + n]
    wk, wv, att, msg, wq = refs[5 + n : 10 + n]
    hubs = refs[10 + n : 10 + n + owners]
    queries, acc, top, den, order, src, keys, values = refs[10 + n + owners :]
    quad = 4 * head_dim
    acc[...] = jnp.zeros(acc.shape, F32)
    top[...] = jnp.full(top.shape, EMPTY, F32)
    den[...] = jnp.zeros(den.shape, F32)
    for lo in range(0, owners, n):
        some = range(lo, min(lo + n, owners))
        for i, t in enumerate(some):
            src[i * tile : (i + 1) * tile, :] = hubs[t][...]
        for c in range(0, heads * head_dim, quad):
            q = jnp.dot(src[...], wq[:, c : c + quad], preferred_element_type=F32)
            for i, t in enumerate(some):
                queries[t, c : c + quad, :] = q[i * tile : (i + 1) * tile, :].T.astype(BF)
    run_blocks(
        *shape, slots, count, b_src, b_dst, b_type, prior, tiles, wk, wv, att, msg,
        queries, acc, top, den, order, src, keys, values,
    )


def later_phase(shape, slots, last, *refs):
    owners, heads, tile, head_dim = shape
    n = len(slots)
    count, b_src, b_dst, b_type, prior = refs[:5]
    tiles = refs[5 : 5 + n]
    wk, wv, att, msg, queries = refs[5 + n : 10 + n]
    given = refs[10 + n : 13 + n]
    rest = refs[13 + n :]
    if last:
        outs, rest = rest[:owners], rest[owners:]
        order, src, keys, values = rest
        acc, top, den = given
    else:
        acc, top, den, order, src, keys, values = rest
        acc[...], top[...], den[...] = (g[...] for g in given)
    run_blocks(
        *shape, slots, count, b_src, b_dst, b_type, prior, tiles, wk, wv, att, msg,
        queries, acc, top, den, order, src, keys, values,
    )
    if last:
        for t in range(owners):
            total = den[t]
            some = total > 0.0
            safe = jnp.where(some, total, 1.0)
            lse = jnp.where(some, top[t] + jnp.log(safe) * LOG2E, EMPTY)
            inverse = 1.0 / safe
            for h in range(heads):
                rows = slice(h * head_dim, (h + 1) * head_dim)
                outs[t][rows, :] = (acc[t, rows, :] * inverse[h : h + 1, :]).astype(BF)
            parts = split3(lse)
            for k in range(3):
                base = heads * head_dim + k * heads
                outs[t][base : base + heads, :] = parts[k]


def combine(owners, heads, head_dim, *refs):
    parts, w_out, out, agg = refs[:owners], refs[owners], refs[owners + 1], refs[owners + 2]
    base = heads * head_dim
    lse = []
    for r in parts:
        hi, mid, lo = (r[base + k * heads : base + (k + 1) * heads, :].astype(F32) for k in range(3))
        lse.append((hi + mid) + lo)
    best = functools.reduce(jnp.maximum, lse)
    weights = [jnp.exp2(v - best) for v in lse]
    whole = functools.reduce(jnp.add, weights)
    weights = [w / whole for w in weights]
    for h in range(heads):
        rows = slice(h * head_dim, (h + 1) * head_dim)
        total = functools.reduce(
            jnp.add,
            [r[rows, :].astype(F32) * w[h : h + 1, :] for r, w in zip(parts, weights)],
        )
        agg[:, rows] = total.T.astype(BF)
    out[...] = jnp.dot(agg[...], w_out[...], preferred_element_type=F32).astype(BF)


def body(
    node_src,
    hub_feat,
    w_query,
    w_key,
    w_value,
    w_out,
    w_att,
    w_msg,
    relation_prior,
    block_src,
    block_dst,
    block_type,
    block_count,
):
    groups = lax.axis_size("grp")
    owners = lax.axis_size("dev")
    tile, width = hub_feat.shape
    relations, heads = relation_prior.shape
    head_dim = width // heads
    pair, pairs = 2 * head_dim, heads // 2
    quads = heads // 4
    length = block_src.shape[1]
    shape = (owners, heads, tile, head_dim)
    smem = pl.BlockSpec(memory_space=pltpu.SMEM)
    keep = lambda x: pltpu.with_memory_space_constraint(x, pltpu.VMEM)
    w_query, w_key, w_value, w_out = (keep(w) for w in (w_query, w_key, w_value, w_out))
    vmem = pl.BlockSpec(memory_space=pltpu.VMEM)

    def move(x, axis, size, k):
        return lax.ppermute(x, axis, [(i, i ^ k) for i in range(size)])

    hubs = {0: hub_feat}
    for k in range(1, owners):
        far = k > 1 and k % 2 == 1
        hubs[k] = move(hubs[k - 1] if far else hub_feat, "dev", owners, 1 if far else k)
    srcs = {0: node_src}
    if groups == 8:
        steps = [(0, 1), (2, 3), (6, 4), (7, 5)]
        for k in (1, 2, 3, 6, 4):
            srcs[k] = move(node_src, "grp", groups, k)
    else:
        steps = [(k, k + 1) for k in range(0, groups, 2)]
        for k in range(1, groups):
            srcs[k] = move(node_src, "grp", groups, k)

    kinds = 4
    wide = pl.BlockSpec((kinds, pairs, pair, head_dim), lambda r: (r, 0, 0, 0))
    square = pl.BlockSpec((kinds, pairs, pair, pair), lambda r: (r, 0, 0, 0))
    att, msg = pl.pallas_call(
        prepare,
        grid=(relations // kinds,),
        in_specs=[wide, wide],
        out_specs=[square, square],
        out_shape=[jax.ShapeDtypeStruct((relations, pairs, pair, pair), BF)] * 2,
        name="prepare",
        compiler_params=pltpu.CompilerParams(vmem_limit_bytes=LIMIT),
    )(w_att.reshape(relations, pairs, pair, head_dim), w_msg.reshape(relations, pairs, pair, head_dim))

    att, msg = keep(att), keep(msg)
    lists = (
        block_count,
        block_src ^ lax.axis_index("grp"),
        block_dst ^ lax.axis_index("dev"),
        block_type,
        relation_prior,
    )
    state = [
        pltpu.VMEM((owners, width, tile), F32),
        pltpu.VMEM((owners, heads, tile), F32),
        pltpu.VMEM((owners, heads, tile), F32),
    ]
    rows_out = width + 3 * heads
    sent = [pltpu.VMEM((rows_out, tile), BF)] * owners
    for i, slots in enumerate(steps):
        n = len(slots)
        if groups == 8 and i == 2:
            carry = list(carry)
            held = lax.optimization_barrier((srcs[6], srcs[4], carry[2]))
            srcs[6], srcs[4], carry[2] = held
            for k in (7, 5):
                srcs[k] = move(srcs[k - 1], "grp", groups, 1)
        scratch = [
            pltpu.SMEM((2, length + 2), jnp.int32),
            pltpu.VMEM((n * tile, width), BF),
            pltpu.VMEM((n, quads, tile, 2 * pair), BF),
            pltpu.VMEM((n, quads, 2 * pair, tile), BF),
        ]
        cost = pl.CostEstimate(flops=9 * 10**9, bytes_accessed=1 << 20, transcendentals=0)
        tiles = [keep(srcs[k]) for k in slots]
        if i == 0:
            queries, *carry = pl.pallas_call(
                functools.partial(first_phase, shape, slots),
                in_specs=[smem] * 5 + [vmem] * (n + 5 + owners),
                out_specs=[vmem] * 4,
                out_shape=[pltpu.VMEM((owners, width, tile), BF)] + state,
                scratch_shapes=scratch,
                cost_estimate=cost,
            compiler_params=pltpu.CompilerParams(vmem_limit_bytes=LIMIT),
                name="phase0",
            )(*lists, *tiles, w_key, w_value, att, msg, w_query, *[keep(hubs[k]) for k in range(owners)])
            continue
        last = i == len(steps) - 1
        base = 10 + n
        aliases = {} if last else {base + k: k for k in range(3)}
        carry = pl.pallas_call(
            functools.partial(later_phase, shape, slots, last),
            in_specs=[smem] * 5 + [vmem] * (n + 8),
            out_specs=[vmem] * (owners if last else 3),
            out_shape=sent if last else state,
            scratch_shapes=scratch,
            input_output_aliases=aliases,
            cost_estimate=cost,
            compiler_params=pltpu.CompilerParams(vmem_limit_bytes=LIMIT),
            name="phase%d" % i,
        )(*lists, *tiles, w_key, w_value, att, msg, queries, *carry)
    parts = [carry[0]] + [move(carry[k], "dev", owners, k) for k in range(1, owners)]
    return pl.pallas_call(
        functools.partial(combine, owners, heads, head_dim),
        out_shape=jax.ShapeDtypeStruct((tile, width), BF),
        scratch_shapes=[pltpu.VMEM((tile, width), BF)],
        compiler_params=pltpu.CompilerParams(vmem_limit_bytes=LIMIT),
        name="combine",
    )(*[keep(p) for p in parts], w_out)


def solution(mesh):
    rows = P(("grp", "dev"), None)
    placed = (rows, rows) + (P(),) * 7 + (rows,) * 3 + (P(("grp", "dev")),)
    return jax.shard_map(body, mesh=mesh, in_specs=placed, out_specs=rows, check_vma=False)
```

```python
import functools

import jax
import jax.numpy as jnp
from jax import lax
from jax.experimental import pallas as pl
from jax.experimental.pallas import tpu as pltpu
from jax.sharding import PartitionSpec as P

BF = jnp.bfloat16
F32 = jnp.float32
LOG2E = 1.4426950408889634
EMPTY = -1e30
BLOCKS = 2
LAGS = (4, 8, 12)
LIMIT = 16 << 20
COST = 10**6


def split3(x):
    hi = x.astype(BF)
    rest = x - hi.astype(F32)
    mid = rest.astype(BF)
    lo = (rest - mid.astype(F32)).astype(BF)
    return hi, mid, lo


def prepare(att, msg, att_out, msg_out):
    kinds, pairs, pair, head_dim = att.shape
    row = lax.broadcasted_iota(jnp.int32, (pair, head_dim), 0)
    col = lax.broadcasted_iota(jnp.int32, (pair, head_dim), 1)
    twice = jnp.where((row & (head_dim - 1)) == col, 1.0, 0.0).astype(BF)
    r2 = lax.broadcasted_iota(jnp.int32, (pair, 2 * pair), 0)
    c2 = lax.broadcasted_iota(jnp.int32, (pair, 2 * pair), 1)
    same = (r2 < head_dim) == ((c2 & (pair - 1)) < head_dim)
    none = jnp.zeros((head_dim, head_dim), BF)
    for r in range(kinds):
        for h in range(pairs):
            upper = jnp.concatenate([att[r, h, :head_dim, :], none], axis=1)
            lower = jnp.concatenate([none, att[r, h, head_dim:, :]], axis=1)
            att_out[r, h] = jnp.concatenate([upper, lower], axis=0)
        for h in range(0, pairs, 2):
            both = msg[r, h : h + 2].reshape(2 * pair, head_dim)
            m = lax.dot_general(twice, both, (((1,), (1,)), ((), ())), preferred_element_type=F32)
            m = jnp.where(same, m, 0.0).astype(BF)
            msg_out[r, h] = m[:, :pair]
            msg_out[r, h + 1] = m[:, pair:]


def run_blocks(
    owners, heads, tile, head_dim, slots, count, b_src, b_dst, b_type, prior, tiles, wk, wv, att, msg,
    queries, acc, top, den, order, src, keys, values,
):
    width = heads * head_dim
    pair, quad = 2 * head_dim, 4 * head_dim
    quads = heads // 4
    for i, ref in enumerate(tiles):
        src[i * tile : (i + 1) * tile, :] = ref[...]
    for q in range(quads):
        cols = slice(q * quad, (q + 1) * quad)
        k = jnp.dot(src[...], wk[:, cols], preferred_element_type=F32)
        v = jnp.dot(src[...], wv[:, cols], preferred_element_type=F32)
        for i in range(len(slots)):
            rows = slice(i * tile, (i + 1) * tile)
            keys[i, q] = k[rows, :].astype(BF)
            values[i, q] = v[rows, :].T.astype(BF)

    def pick(j, n):
        s = b_src[0, j]
        which = jnp.int32(0)
        hit = s == slots[0]
        for i in range(1, len(slots)):
            here = s == slots[i]
            which = jnp.where(here, i, which)
            hit = hit | here
        order[0, n] = j
        order[1, n] = which
        return n + hit.astype(jnp.int32)

    total = lax.fori_loop(0, count[0], pick, jnp.int32(0))
    lane = lax.broadcasted_iota(jnp.int32, (tile, pair), 1)
    left = lane < head_dim
    none = jnp.zeros((pair, pair), BF)

    def diag(w, r, q):
        upper = jnp.concatenate([w[r, 2 * q], none], axis=1)
        lower = jnp.concatenate([none, w[r, 2 * q + 1]], axis=1)
        return jnp.concatenate([upper, lower], axis=0)

    def some_blocks(c, _):
        blocks = []
        for u in range(BLOCKS):
            n = c * BLOCKS + u
            valid = n < total
            j = jnp.where(valid, order[0, n], 0)
            s = jnp.where(valid, order[1, n], 0)
            blocks.append((valid, s, b_dst[0, j], b_type[0, j]))

        def maps(u, q):
            _, s, _, r = blocks[u]
            key_rel = jnp.dot(keys[s, q], diag(att, r, q), preferred_element_type=F32).astype(BF)
            message = jnp.dot(diag(msg, r, q), values[s, q], preferred_element_type=F32).astype(BF)
            return key_rel, message

        def scores(u, h, key_rel):
            _, _, d, _ = blocks[u]
            k = key_rel[:, (h % 2) * pair : (h % 2 + 1) * pair]
            zero = jnp.zeros_like(k)
            both = jnp.concatenate([jnp.where(left, k, zero), jnp.where(left, zero, k)], axis=0)
            q = queries[d, h * pair : (h + 1) * pair, :]
            return jnp.dot(both, q, preferred_element_type=F32)

        def weigh(u, h, s):
            _, _, _, r = blocks[u]
            found = []
            for i in range(2):
                scale = prior[r, 2 * h + i] * (LOG2E / float(head_dim) ** 0.5)
                x = s[i * tile : (i + 1) * tile, :] * scale
                m = jnp.max(x, axis=0, keepdims=True)
                p = jnp.exp2(x - m)
                found.append((m, jnp.sum(p, axis=0, keepdims=True), p.astype(BF)))
            return found

        def gather(u, h, message, found):
            valid, _, d, _ = blocks[u]
            for i in range(2):
                row = (h % 2) * pair + i * head_dim
                m, total_w, p = found[i]
                part = jnp.dot(message[row : row + head_dim, :], p, preferred_element_type=F32)
                head = 2 * h + i
                one = slice(head, head + 1)
                rows = slice(head * head_dim, (head + 1) * head_dim)
                old = top[d, one, :]
                new = jnp.where(valid, jnp.maximum(old, m), old)
                keep = jnp.exp2(old - new)
                add = jnp.where(valid, jnp.exp2(m - new), 0.0)
                top[d, one, :] = new
                den[d, one, :] = den[d, one, :] * keep + total_w * add
                acc[d, rows, :] = acc[d, rows, :] * keep + part * add

        items = [(u, h) for u in range(BLOCKS) for h in range(heads // 2)]
        mapped, scored, weighed = {}, {}, {}
        a, b, d = LAGS
        for t in range(len(items) + d):
            if t < len(items) and items[t][1] % 2 == 0:
                u, h = items[t]
                mapped[u, h // 2] = maps(u, h // 2)
            if 0 <= t - a < len(items):
                u, h = items[t - a]
                scored[u, h] = scores(u, h, mapped[u, h // 2][0])
            if 0 <= t - b < len(items):
                u, h = items[t - b]
                weighed[u, h] = weigh(u, h, scored.pop((u, h)))
            if 0 <= t - d < len(items):
                u, h = items[t - d]
                gather(u, h, mapped[u, h // 2][1], weighed.pop((u, h)))
        return 0

    lax.fori_loop(0, (total + BLOCKS - 1) // BLOCKS, some_blocks, 0)


def first_phase(shape, slots, *refs):
    owners, heads, tile, head_dim = shape
    n = len(slots)
    count, b_src, b_dst, b_type, prior = refs[:5]
    tiles = refs[5 : 5 + n]
    wk, wv, att, msg, wq = refs[5 + n : 10 + n]
    hubs = refs[10 + n : 10 + n + owners]
    queries, acc, top, den, order, src, keys, values = refs[10 + n + owners :]
    quad = 4 * head_dim
    acc[...] = jnp.zeros(acc.shape, F32)
    top[...] = jnp.full(top.shape, EMPTY, F32)
    den[...] = jnp.zeros(den.shape, F32)
    for lo in range(0, owners, n):
        some = range(lo, min(lo + n, owners))
        for i, t in enumerate(some):
            src[i * tile : (i + 1) * tile, :] = hubs[t][...]
        for c in range(0, heads * head_dim, quad):
            q = jnp.dot(src[...], wq[:, c : c + quad], preferred_element_type=F32)
            for i, t in enumerate(some):
                queries[t, c : c + quad, :] = q[i * tile : (i + 1) * tile, :].T.astype(BF)
    run_blocks(
        *shape, slots, count, b_src, b_dst, b_type, prior, tiles, wk, wv, att, msg,
        queries, acc, top, den, order, src, keys, values,
    )


def later_phase(shape, slots, last, *refs):
    owners, heads, tile, head_dim = shape
    n = len(slots)
    count, b_src, b_dst, b_type, prior = refs[:5]
    tiles = refs[5 : 5 + n]
    wk, wv, att, msg, queries = refs[5 + n : 10 + n]
    given = refs[10 + n : 13 + n]
    rest = refs[13 + n :]
    if last:
        outs, rest = rest[:owners], rest[owners:]
        order, src, keys, values = rest
        acc, top, den = given
    else:
        acc, top, den, order, src, keys, values = rest
        acc[...], top[...], den[...] = (g[...] for g in given)
    run_blocks(
        *shape, slots, count, b_src, b_dst, b_type, prior, tiles, wk, wv, att, msg,
        queries, acc, top, den, order, src, keys, values,
    )
    if last:
        for t in range(owners):
            total = den[t]
            some = total > 0.0
            safe = jnp.where(some, total, 1.0)
            lse = jnp.where(some, top[t] + jnp.log(safe) * LOG2E, EMPTY)
            inverse = 1.0 / safe
            for h in range(heads):
                rows = slice(h * head_dim, (h + 1) * head_dim)
                outs[t][rows, :] = (acc[t, rows, :] * inverse[h : h + 1, :]).astype(BF)
            parts = split3(lse)
            for k in range(3):
                base = heads * head_dim + k * heads
                outs[t][base : base + heads, :] = parts[k]


def combine(owners, heads, head_dim, *refs):
    parts, w_out, out, agg = refs[:owners], refs[owners], refs[owners + 1], refs[owners + 2]
    base = heads * head_dim
    lse = []
    for r in parts:
        hi, mid, lo = (r[base + k * heads : base + (k + 1) * heads, :].astype(F32) for k in range(3))
        lse.append((hi + mid) + lo)
    best = functools.reduce(jnp.maximum, lse)
    weights = [jnp.exp2(v - best) for v in lse]
    whole = functools.reduce(jnp.add, weights)
    weights = [w / whole for w in weights]
    for h in range(heads):
        rows = slice(h * head_dim, (h + 1) * head_dim)
        total = functools.reduce(
            jnp.add,
            [r[rows, :].astype(F32) * w[h : h + 1, :] for r, w in zip(parts, weights)],
        )
        agg[:, rows] = total.T.astype(BF)
    out[...] = jnp.dot(agg[...], w_out[...], preferred_element_type=F32).astype(BF)


def body(
    node_src,
    hub_feat,
    w_query,
    w_key,
    w_value,
    w_out,
    w_att,
    w_msg,
    relation_prior,
    block_src,
    block_dst,
    block_type,
    block_count,
):
    groups = lax.axis_size("grp")
    owners = lax.axis_size("dev")
    tile, width = hub_feat.shape
    relations, heads = relation_prior.shape
    head_dim = width // heads
    pair, pairs = 2 * head_dim, heads // 2
    quads = heads // 4
    length = block_src.shape[1]
    shape = (owners, heads, tile, head_dim)
    smem = pl.BlockSpec(memory_space=pltpu.SMEM)
    apart = lambda x: pltpu.with_memory_space_constraint(x, pltpu.HBM)
    keep = lambda x: pltpu.with_memory_space_constraint(x, pltpu.VMEM)
    w_query, w_key, w_value, w_out = (keep(w) for w in (w_query, w_key, w_value, w_out))
    vmem = pl.BlockSpec(memory_space=pltpu.VMEM)

    def move(x, axis, size, k):
        return lax.ppermute(x, axis, [(i, i ^ k) for i in range(size)])

    hubs = {0: hub_feat}
    for k in range(2, owners, 2):
        hubs[k] = move(hub_feat, "dev", owners, k)
    srcs = {0: node_src}
    if groups == 8:
        steps = [(0, 1), (2, 3), (6, 4), (7, 5)]
        for k in (1, 6, 2, 3):
            srcs[k] = move(node_src, "grp", groups, k)
    else:
        steps = [(k, k + 1) for k in range(0, groups, 2)]
        for k in range(1, groups):
            srcs[k] = move(node_src, "grp", groups, k)

    kinds = 4
    wide = pl.BlockSpec((kinds, pairs, pair, head_dim), lambda r: (r, 0, 0, 0))
    square = pl.BlockSpec((kinds, pairs, pair, pair), lambda r: (r, 0, 0, 0))
    att, msg = pl.pallas_call(
        prepare,
        grid=(relations // kinds,),
        in_specs=[wide, wide],
        out_specs=[square, square],
        out_shape=[jax.ShapeDtypeStruct((relations, pairs, pair, pair), BF)] * 2,
        name="prepare",
        compiler_params=pltpu.CompilerParams(vmem_limit_bytes=LIMIT),
    )(*[apart(w.reshape(relations, pairs, pair, head_dim)) for w in (w_att, w_msg)])
    held = lax.optimization_barrier((att, srcs[1], *[hubs[k] for k in range(0, owners, 2)]))
    att, srcs[1], near = held[0], held[1], held[2:]
    for k in range(0, owners, 2):
        hubs[k] = near[k // 2]
        hubs[k + 1] = move(hubs[k], "dev", owners, 1)
    if groups == 8:
        source, hubs[1] = lax.optimization_barrier((node_src, hubs[1]))
        srcs[4] = move(source, "grp", groups, 4)
    att, msg = keep(att), keep(msg)
    lists = (
        block_count,
        block_src ^ lax.axis_index("grp"),
        block_dst ^ lax.axis_index("dev"),
        block_type,
        relation_prior,
    )
    state = [
        pltpu.VMEM((owners, width, tile), F32),
        pltpu.VMEM((owners, heads, tile), F32),
        pltpu.VMEM((owners, heads, tile), F32),
    ]
    rows_out = width + 3 * heads
    sent = [pltpu.VMEM((rows_out, tile), BF)] * owners
    for i, slots in enumerate(steps):
        n = len(slots)
        if groups == 8 and i == 2:
            carry = list(carry)
            held = lax.optimization_barrier((srcs[6], srcs[4], carry[2]))
            srcs[6], srcs[4], carry[2] = held
            for k in (7, 5):
                srcs[k] = move(srcs[k - 1], "grp", groups, 1)
        scratch = [
            pltpu.SMEM((2, length + 2), jnp.int32),
            pltpu.VMEM((n * tile, width), BF),
            pltpu.VMEM((n, quads, tile, 2 * pair), BF),
            pltpu.VMEM((n, quads, 2 * pair, tile), BF),
        ]
        cost = pl.CostEstimate(flops=COST, bytes_accessed=1024, transcendentals=0)
        tiles = [keep(srcs[k]) for k in slots]
        if i == 0:
            queries, *carry = pl.pallas_call(
                functools.partial(first_phase, shape, slots),
                in_specs=[smem] * 5 + [vmem] * (n + 5 + owners),
                out_specs=[vmem] * 4,
                out_shape=[pltpu.VMEM((owners, width, tile), BF)] + state,
                scratch_shapes=scratch,
                cost_estimate=cost,
            compiler_params=pltpu.CompilerParams(vmem_limit_bytes=LIMIT),
                name="phase0",
            )(*lists, *tiles, w_key, w_value, att, msg, w_query, *[keep(hubs[k]) for k in range(owners)])
            continue
        last = i == len(steps) - 1
        base = 10 + n
        aliases = {} if last else {base + k: k for k in range(3)}
        carry = pl.pallas_call(
            functools.partial(later_phase, shape, slots, last),
            in_specs=[smem] * 5 + [vmem] * (n + 8),
            out_specs=[vmem] * (owners if last else 3),
            out_shape=sent if last else state,
            scratch_shapes=scratch,
            input_output_aliases=aliases,
            cost_estimate=cost,
            compiler_params=pltpu.CompilerParams(vmem_limit_bytes=LIMIT),
            name="phase%d" % i,
        )(*lists, *tiles, w_key, w_value, att, msg, queries, *carry)
    parts = [carry[0]] + [move(carry[k], "dev", owners, k) for k in range(1, owners)]
    return pl.pallas_call(
        functools.partial(combine, owners, heads, head_dim),
        out_shape=jax.ShapeDtypeStruct((tile, width), BF),
        scratch_shapes=[pltpu.VMEM((tile, width), BF)],
        compiler_params=pltpu.CompilerParams(vmem_limit_bytes=LIMIT),
        name="combine",
    )(*[keep(p) for p in parts], w_out)


def solution(mesh):
    rows = P(("grp", "dev"), None)
    placed = (rows, rows) + (P(),) * 7 + (rows,) * 3 + (P(("grp", "dev")),)
    return jax.shard_map(body, mesh=mesh, in_specs=placed, out_specs=rows, check_vma=False)
```

```python
import functools

import jax
import jax.numpy as jnp
from jax import lax
from jax.experimental import pallas as pl
from jax.experimental.pallas import tpu as pltpu
from jax.sharding import PartitionSpec as P

BF = jnp.bfloat16
F32 = jnp.float32
LOG2E = 1.4426950408889634
EMPTY = -1e30
BLOCKS = 2
LAGS = (4, 8, 12)
LIMIT = 16 << 20
COST = 10**6


def split3(x):
    hi = x.astype(BF)
    rest = x - hi.astype(F32)
    mid = rest.astype(BF)
    lo = (rest - mid.astype(F32)).astype(BF)
    return hi, mid, lo


def prepare(parts, att, msg, *refs):
    kinds, pairs, pair, head_dim = att.shape
    plain = (len(refs) - 6) // 2
    given, refs = refs[:plain], refs[plain:]
    att_out, msg_out, copies = refs[0], refs[1], refs[2 : 2 + plain]
    att_in, msg_in, sem, plain_sem = refs[2 + plain :]
    size = kinds // parts
    moves = []
    for k in range(parts):
        some = pl.ds(k * size, size)
        moves.append(pltpu.make_async_copy(att.at[some], att_in.at[some], sem.at[0, k]))
        moves.append(pltpu.make_async_copy(msg.at[some], msg_in.at[some], sem.at[1, k]))
    rest = [pltpu.make_async_copy(g, c, plain_sem.at[i]) for i, (g, c) in enumerate(zip(given, copies))]
    for m in moves + rest:
        m.start()
    row = lax.broadcasted_iota(jnp.int32, (pair, head_dim), 0)
    col = lax.broadcasted_iota(jnp.int32, (pair, head_dim), 1)
    twice = jnp.where((row & (head_dim - 1)) == col, 1.0, 0.0).astype(BF)
    r2 = lax.broadcasted_iota(jnp.int32, (pair, 2 * pair), 0)
    c2 = lax.broadcasted_iota(jnp.int32, (pair, 2 * pair), 1)
    same = (r2 < head_dim) == ((c2 & (pair - 1)) < head_dim)
    none = jnp.zeros((head_dim, head_dim), BF)
    for k in range(parts):
        moves[2 * k].wait()
        moves[2 * k + 1].wait()

        def one(i, _):
            r = k * size + i
            for h in range(pairs):
                upper = jnp.concatenate([att_in[r, h, :head_dim, :], none], axis=1)
                lower = jnp.concatenate([none, att_in[r, h, head_dim:, :]], axis=1)
                att_out[r, h] = jnp.concatenate([upper, lower], axis=0)
            for h in range(0, pairs, 2):
                both = msg_in[r, h : h + 2].reshape(2 * pair, head_dim)
                m = lax.dot_general(twice, both, (((1,), (1,)), ((), ())), preferred_element_type=F32)
                m = jnp.where(same, m, 0.0).astype(BF)
                msg_out[r, h] = m[:, :pair]
                msg_out[r, h + 1] = m[:, pair:]
            return 0

        lax.fori_loop(0, size, one, 0)
    for m in rest:
        m.wait()


def run_blocks(
    owners, heads, tile, head_dim, slots, count, b_src, b_dst, b_type, prior, tiles, wk, wv, att, msg,
    queries, acc, top, den, order, src, keys, values,
):
    width = heads * head_dim
    pair, quad = 2 * head_dim, 4 * head_dim
    quads = heads // 4
    for i, ref in enumerate(tiles):
        src[i * tile : (i + 1) * tile, :] = ref[...]
    for q in range(quads):
        cols = slice(q * quad, (q + 1) * quad)
        k = jnp.dot(src[...], wk[:, cols], preferred_element_type=F32)
        v = jnp.dot(src[...], wv[:, cols], preferred_element_type=F32)
        for i in range(len(slots)):
            rows = slice(i * tile, (i + 1) * tile)
            keys[i, q] = k[rows, :].astype(BF)
            values[i, q] = v[rows, :].T.astype(BF)

    my_grp, my_dev = lax.axis_index("grp"), lax.axis_index("dev")

    def pick(j, n):
        s = b_src[0, j] ^ my_grp
        which = jnp.int32(0)
        hit = s == slots[0]
        for i in range(1, len(slots)):
            here = s == slots[i]
            which = jnp.where(here, i, which)
            hit = hit | here
        order[0, n] = j
        order[1, n] = which
        return n + hit.astype(jnp.int32)

    total = lax.fori_loop(0, count[0], pick, jnp.int32(0))
    lane = lax.broadcasted_iota(jnp.int32, (tile, pair), 1)
    left = lane < head_dim
    none = jnp.zeros((pair, pair), BF)

    def diag(w, r, q):
        upper = jnp.concatenate([w[r, 2 * q], none], axis=1)
        lower = jnp.concatenate([none, w[r, 2 * q + 1]], axis=1)
        return jnp.concatenate([upper, lower], axis=0)

    def some_blocks(c, _):
        blocks = []
        for u in range(BLOCKS):
            n = c * BLOCKS + u
            valid = n < total
            j = jnp.where(valid, order[0, n], 0)
            s = jnp.where(valid, order[1, n], 0)
            blocks.append((valid, s, b_dst[0, j] ^ my_dev, b_type[0, j]))

        def maps(u, q):
            _, s, _, r = blocks[u]
            key_rel = jnp.dot(keys[s, q], diag(att, r, q), preferred_element_type=F32).astype(BF)
            message = jnp.dot(diag(msg, r, q), values[s, q], preferred_element_type=F32).astype(BF)
            return key_rel, message

        def scores(u, h, key_rel):
            _, _, d, _ = blocks[u]
            k = key_rel[:, (h % 2) * pair : (h % 2 + 1) * pair]
            zero = jnp.zeros_like(k)
            both = jnp.concatenate([jnp.where(left, k, zero), jnp.where(left, zero, k)], axis=0)
            q = queries[d, h * pair : (h + 1) * pair, :]
            return jnp.dot(both, q, preferred_element_type=F32)

        def weigh(u, h, s):
            _, _, _, r = blocks[u]
            found = []
            for i in range(2):
                scale = prior[r, 2 * h + i] * (LOG2E / float(head_dim) ** 0.5)
                x = s[i * tile : (i + 1) * tile, :] * scale
                m = jnp.max(x, axis=0, keepdims=True)
                p = jnp.exp2(x - m)
                found.append((m, jnp.sum(p, axis=0, keepdims=True), p.astype(BF)))
            return found

        def gather(u, h, message, found):
            valid, _, d, _ = blocks[u]
            for i in range(2):
                row = (h % 2) * pair + i * head_dim
                m, total_w, p = found[i]
                part = jnp.dot(message[row : row + head_dim, :], p, preferred_element_type=F32)
                head = 2 * h + i
                one = slice(head, head + 1)
                rows = slice(head * head_dim, (head + 1) * head_dim)
                old = top[d, one, :]
                new = jnp.where(valid, jnp.maximum(old, m), old)
                keep = jnp.exp2(old - new)
                add = jnp.where(valid, jnp.exp2(m - new), 0.0)
                top[d, one, :] = new
                den[d, one, :] = den[d, one, :] * keep + total_w * add
                acc[d, rows, :] = acc[d, rows, :] * keep + part * add

        items = [(u, h) for u in range(BLOCKS) for h in range(heads // 2)]
        mapped, scored, weighed = {}, {}, {}
        a, b, d = LAGS
        for t in range(len(items) + d):
            if t < len(items) and items[t][1] % 2 == 0:
                u, h = items[t]
                mapped[u, h // 2] = maps(u, h // 2)
            if 0 <= t - a < len(items):
                u, h = items[t - a]
                scored[u, h] = scores(u, h, mapped[u, h // 2][0])
            if 0 <= t - b < len(items):
                u, h = items[t - b]
                weighed[u, h] = weigh(u, h, scored.pop((u, h)))
            if 0 <= t - d < len(items):
                u, h = items[t - d]
                gather(u, h, mapped[u, h // 2][1], weighed.pop((u, h)))
        return 0

    lax.fori_loop(0, (total + BLOCKS - 1) // BLOCKS, some_blocks, 0)


def first_phase(shape, slots, *refs):
    owners, heads, tile, head_dim = shape
    n = len(slots)
    count, b_src, b_dst, b_type, prior = refs[:5]
    tiles = refs[5 : 5 + n]
    wk, wv, att, msg, wq = refs[5 + n : 10 + n]
    hubs = refs[10 + n : 10 + n + owners]
    queries, acc, top, den, order, src, keys, values = refs[10 + n + owners :]
    quad = 4 * head_dim
    acc[...] = jnp.zeros(acc.shape, F32)
    top[...] = jnp.full(top.shape, EMPTY, F32)
    den[...] = jnp.zeros(den.shape, F32)
    for lo in range(0, owners, n):
        some = range(lo, min(lo + n, owners))
        for i, t in enumerate(some):
            src[i * tile : (i + 1) * tile, :] = hubs[t][...]
        for c in range(0, heads * head_dim, quad):
            q = jnp.dot(src[...], wq[:, c : c + quad], preferred_element_type=F32)
            for i, t in enumerate(some):
                queries[t, c : c + quad, :] = q[i * tile : (i + 1) * tile, :].T.astype(BF)
    run_blocks(
        *shape, slots, count, b_src, b_dst, b_type, prior, tiles, wk, wv, att, msg,
        queries, acc, top, den, order, src, keys, values,
    )


def later_phase(shape, slots, last, *refs):
    owners, heads, tile, head_dim = shape
    n = len(slots)
    count, b_src, b_dst, b_type, prior = refs[:5]
    tiles = refs[5 : 5 + n]
    wk, wv, att, msg, queries = refs[5 + n : 10 + n]
    given = refs[10 + n : 13 + n]
    rest = refs[13 + n :]
    if last:
        outs, rest = rest[:owners], rest[owners:]
        order, src, keys, values = rest
        acc, top, den = given
    else:
        acc, top, den, order, src, keys, values = rest
        acc[...], top[...], den[...] = (g[...] for g in given)
    run_blocks(
        *shape, slots, count, b_src, b_dst, b_type, prior, tiles, wk, wv, att, msg,
        queries, acc, top, den, order, src, keys, values,
    )
    if last:
        for t in range(owners):
            total = den[t]
            some = total > 0.0
            safe = jnp.where(some, total, 1.0)
            lse = jnp.where(some, top[t] + jnp.log(safe) * LOG2E, EMPTY)
            inverse = 1.0 / safe
            for h in range(heads):
                rows = slice(h * head_dim, (h + 1) * head_dim)
                outs[t][rows, :] = (acc[t, rows, :] * inverse[h : h + 1, :]).astype(BF)
            parts = split3(lse)
            for k in range(3):
                base = heads * head_dim + k * heads
                outs[t][base : base + heads, :] = parts[k]


def combine(owners, heads, head_dim, *refs):
    parts, w_out, out, agg = refs[:owners], refs[owners], refs[owners + 1], refs[owners + 2]
    base = heads * head_dim
    lse = []
    for r in parts:
        hi, mid, lo = (r[base + k * heads : base + (k + 1) * heads, :].astype(F32) for k in range(3))
        lse.append((hi + mid) + lo)
    best = functools.reduce(jnp.maximum, lse)
    weights = [jnp.exp2(v - best) for v in lse]
    whole = functools.reduce(jnp.add, weights)
    weights = [w / whole for w in weights]
    for h in range(heads):
        rows = slice(h * head_dim, (h + 1) * head_dim)
        total = functools.reduce(
            jnp.add,
            [r[rows, :].astype(F32) * w[h : h + 1, :] for r, w in zip(parts, weights)],
        )
        agg[:, rows] = total.T.astype(BF)
    out[...] = jnp.dot(agg[...], w_out[...], preferred_element_type=F32).astype(BF)


def body(
    node_src,
    hub_feat,
    w_query,
    w_key,
    w_value,
    w_out,
    w_att,
    w_msg,
    relation_prior,
    block_src,
    block_dst,
    block_type,
    block_count,
):
    groups = lax.axis_size("grp")
    owners = lax.axis_size("dev")
    tile, width = hub_feat.shape
    relations, heads = relation_prior.shape
    head_dim = width // heads
    pair, pairs = 2 * head_dim, heads // 2
    quads = heads // 4
    length = block_src.shape[1]
    shape = (owners, heads, tile, head_dim)
    smem = pl.BlockSpec(memory_space=pltpu.SMEM)
    apart = lambda x: pltpu.with_memory_space_constraint(x, pltpu.HBM)
    keep = lambda x: pltpu.with_memory_space_constraint(x, pltpu.VMEM)
    w_out = keep(w_out)
    vmem = pl.BlockSpec(memory_space=pltpu.VMEM)

    def move(x, axis, size, k):
        return lax.ppermute(x, axis, [(i, i ^ k) for i in range(size)])

    hubs = {0: hub_feat}
    for k in range(2, owners, 2):
        hubs[k] = move(hub_feat, "dev", owners, k)
    srcs = {0: node_src}
    if groups == 8:
        steps = [(0, 1), (2, 3), (6, 4), (7, 5)]
        for k in (1, 6, 2, 3):
            srcs[k] = move(node_src, "grp", groups, k)
    else:
        steps = [(k, k + 1) for k in range(0, groups, 2)]
        for k in range(1, groups):
            srcs[k] = move(node_src, "grp", groups, k)

    dense = (w_query, w_key, w_value, node_src, hub_feat)
    maps = [w.reshape(relations, pairs, pair, head_dim) for w in (w_att, w_msg)]
    chunks = 4
    att, msg, w_query, w_key, w_value, own_src, own_hub = pl.pallas_call(
        functools.partial(prepare, chunks),
        in_specs=[pl.BlockSpec(memory_space=pltpu.HBM)] * (2 + len(dense)),
        out_specs=[vmem] * (2 + len(dense)),
        out_shape=[pltpu.VMEM((relations, pairs, pair, pair), BF)] * 2
        + [pltpu.VMEM(x.shape, BF) for x in dense],
        scratch_shapes=[
            pltpu.VMEM((relations, pairs, pair, head_dim), BF),
            pltpu.VMEM((relations, pairs, pair, head_dim), BF),
            pltpu.SemaphoreType.DMA((2, chunks)),
            pltpu.SemaphoreType.DMA((len(dense),)),
        ],
        name="prepare",
        compiler_params=pltpu.CompilerParams(vmem_limit_bytes=LIMIT),
    )(*[apart(x) for x in (*maps, *dense)])
    held = lax.optimization_barrier((att, srcs[1], *[hubs[k] for k in range(0, owners, 2)]))
    att, srcs[1], near = held[0], held[1], held[2:]
    for k in range(0, owners, 2):
        hubs[k] = near[k // 2]
        hubs[k + 1] = move(hubs[k], "dev", owners, 1)
    if groups == 8:
        source, hubs[1] = lax.optimization_barrier((node_src, hubs[1]))
        srcs[4] = move(source, "grp", groups, 4)
    srcs[0], hubs[0] = own_src, own_hub
    att, msg, w_query, w_key, w_value = (keep(x) for x in (att, msg, w_query, w_key, w_value))
    lists = (
        block_count,
        block_src,
        block_dst,
        block_type,
        relation_prior,
    )
    state = [
        pltpu.VMEM((owners, width, tile), F32),
        pltpu.VMEM((owners, heads, tile), F32),
        pltpu.VMEM((owners, heads, tile), F32),
    ]
    rows_out = width + 3 * heads
    sent = [pltpu.VMEM((rows_out, tile), BF)] * owners
    for i, slots in enumerate(steps):
        n = len(slots)
        if groups == 8 and i == 2:
            carry = list(carry)
            held = lax.optimization_barrier((srcs[6], srcs[4], carry[2]))
            srcs[6], srcs[4], carry[2] = held
            for k in (7, 5):
                srcs[k] = move(srcs[k - 1], "grp", groups, 1)
        scratch = [
            pltpu.SMEM((2, length + 2), jnp.int32),
            pltpu.VMEM((n * tile, width), BF),
            pltpu.VMEM((n, quads, tile, 2 * pair), BF),
            pltpu.VMEM((n, quads, 2 * pair, tile), BF),
        ]
        cost = pl.CostEstimate(flops=COST, bytes_accessed=1024, transcendentals=0)
        tiles = [keep(srcs[k]) for k in slots]
        if i == 0:
            queries, *carry = pl.pallas_call(
                functools.partial(first_phase, shape, slots),
                in_specs=[smem] * 5 + [vmem] * (n + 5 + owners),
                out_specs=[vmem] * 4,
                out_shape=[pltpu.VMEM((owners, width, tile), BF)] + state,
                scratch_shapes=scratch,
                cost_estimate=cost,
            compiler_params=pltpu.CompilerParams(vmem_limit_bytes=LIMIT),
                name="phase0",
            )(*lists, *tiles, w_key, w_value, att, msg, w_query, *[keep(hubs[k]) for k in range(owners)])
            continue
        last = i == len(steps) - 1
        base = 10 + n
        aliases = {} if last else {base + k: k for k in range(3)}
        carry = pl.pallas_call(
            functools.partial(later_phase, shape, slots, last),
            in_specs=[smem] * 5 + [vmem] * (n + 8),
            out_specs=[vmem] * (owners if last else 3),
            out_shape=sent if last else state,
            scratch_shapes=scratch,
            input_output_aliases=aliases,
            cost_estimate=cost,
            compiler_params=pltpu.CompilerParams(vmem_limit_bytes=LIMIT),
            name="phase%d" % i,
        )(*lists, *tiles, w_key, w_value, att, msg, queries, *carry)
    parts = [carry[0]] + [move(carry[k], "dev", owners, k) for k in range(1, owners)]
    return pl.pallas_call(
        functools.partial(combine, owners, heads, head_dim),
        out_shape=jax.ShapeDtypeStruct((tile, width), BF),
        scratch_shapes=[pltpu.VMEM((tile, width), BF)],
        compiler_params=pltpu.CompilerParams(vmem_limit_bytes=LIMIT),
        name="combine",
    )(*[keep(p) for p in parts], w_out)


def solution(mesh):
    rows = P(("grp", "dev"), None)
    placed = (rows, rows) + (P(),) * 7 + (rows,) * 3 + (P(("grp", "dev")),)
    return jax.shard_map(body, mesh=mesh, in_specs=placed, out_specs=rows, check_vma=False)
```

```python
import functools

import jax
import jax.numpy as jnp
from jax import lax
from jax.experimental import pallas as pl
from jax.experimental.pallas import tpu as pltpu
from jax.sharding import PartitionSpec as P

BF = jnp.bfloat16
F32 = jnp.float32
LOG2E = 1.4426950408889634
EMPTY = -1e30
BLOCKS = 2
LAGS = (4, 8, 12)
LIMIT = 16 << 20
COST = 10**6


def split3(x):
    hi = x.astype(BF)
    rest = x - hi.astype(F32)
    mid = rest.astype(BF)
    lo = (rest - mid.astype(F32)).astype(BF)
    return hi, mid, lo


def prepare(parts, att, msg, *refs):
    kinds, pairs, pair, head_dim = att.shape
    plain = (len(refs) - 6) // 2
    given, refs = refs[:plain], refs[plain:]
    att_out, msg_out, copies = refs[0], refs[1], refs[2 : 2 + plain]
    att_in, msg_in, sem, plain_sem = refs[2 + plain :]
    size = kinds // parts
    moves = []
    for k in range(parts):
        some = pl.ds(k * size, size)
        moves.append(pltpu.make_async_copy(att.at[some], att_in.at[some], sem.at[0, k]))
        moves.append(pltpu.make_async_copy(msg.at[some], msg_in.at[some], sem.at[1, k]))
    rest = [pltpu.make_async_copy(g, c, plain_sem.at[i]) for i, (g, c) in enumerate(zip(given, copies))]
    for m in moves + rest:
        m.start()
    row = lax.broadcasted_iota(jnp.int32, (pair, head_dim), 0)
    col = lax.broadcasted_iota(jnp.int32, (pair, head_dim), 1)
    twice = jnp.where((row & (head_dim - 1)) == col, 1.0, 0.0).astype(BF)
    r2 = lax.broadcasted_iota(jnp.int32, (pair, 2 * pair), 0)
    c2 = lax.broadcasted_iota(jnp.int32, (pair, 2 * pair), 1)
    same = (r2 < head_dim) == ((c2 & (pair - 1)) < head_dim)
    none = jnp.zeros((head_dim, head_dim), BF)
    for k in range(parts):
        moves[2 * k].wait()
        moves[2 * k + 1].wait()

        def one(i, _):
            r = k * size + i
            for h in range(pairs):
                upper = jnp.concatenate([att_in[r, h, :head_dim, :], none], axis=1)
                lower = jnp.concatenate([none, att_in[r, h, head_dim:, :]], axis=1)
                att_out[r, h] = jnp.concatenate([upper, lower], axis=0)
            for h in range(0, pairs, 2):
                both = msg_in[r, h : h + 2].reshape(2 * pair, head_dim)
                m = lax.dot_general(twice, both, (((1,), (1,)), ((), ())), preferred_element_type=F32)
                m = jnp.where(same, m, 0.0).astype(BF)
                msg_out[r, h] = m[:, :pair]
                msg_out[r, h + 1] = m[:, pair:]
            return 0

        lax.fori_loop(0, size, one, 0)
    for m in rest:
        m.wait()


def run_blocks(
    owners, heads, tile, head_dim, slots, count, b_src, b_dst, b_type, prior, tiles, wk, wv, att, msg,
    queries, acc, top, den, order, src, keys, values,
):
    width = heads * head_dim
    pair, quad = 2 * head_dim, 4 * head_dim
    quads = heads // 4
    for i, ref in enumerate(tiles):
        src[i * tile : (i + 1) * tile, :] = ref[...]
    for q in range(quads):
        cols = slice(q * quad, (q + 1) * quad)
        k = jnp.dot(src[...], wk[:, cols], preferred_element_type=F32)
        v = jnp.dot(src[...], wv[:, cols], preferred_element_type=F32)
        for i in range(len(slots)):
            rows = slice(i * tile, (i + 1) * tile)
            keys[i, q] = k[rows, :].astype(BF)
            values[i, q] = v[rows, :].T.astype(BF)

    my_grp, my_dev = lax.axis_index("grp"), lax.axis_index("dev")

    def pick(j, n):
        s = b_src[0, j] ^ my_grp
        which = jnp.int32(0)
        hit = s == slots[0]
        for i in range(1, len(slots)):
            here = s == slots[i]
            which = jnp.where(here, i, which)
            hit = hit | here
        order[0, n] = j
        order[1, n] = which
        return n + hit.astype(jnp.int32)

    total = lax.fori_loop(0, count[0], pick, jnp.int32(0))
    lane = lax.broadcasted_iota(jnp.int32, (tile, pair), 1)
    left = lane < head_dim
    none = jnp.zeros((pair, pair), BF)

    def diag(w, r, q):
        upper = jnp.concatenate([w[r, 2 * q], none], axis=1)
        lower = jnp.concatenate([none, w[r, 2 * q + 1]], axis=1)
        return jnp.concatenate([upper, lower], axis=0)

    def some_blocks(c, _):
        blocks = []
        for u in range(BLOCKS):
            n = c * BLOCKS + u
            valid = n < total
            j = jnp.where(valid, order[0, n], 0)
            s = jnp.where(valid, order[1, n], 0)
            blocks.append((valid, s, b_dst[0, j] ^ my_dev, b_type[0, j]))

        def maps(u, q):
            _, s, _, r = blocks[u]
            key_rel = jnp.dot(keys[s, q], diag(att, r, q), preferred_element_type=F32).astype(BF)
            message = jnp.dot(diag(msg, r, q), values[s, q], preferred_element_type=F32).astype(BF)
            return key_rel, message

        def scores(u, h, key_rel):
            _, _, d, _ = blocks[u]
            k = key_rel[:, (h % 2) * pair : (h % 2 + 1) * pair]
            zero = jnp.zeros_like(k)
            both = jnp.concatenate([jnp.where(left, k, zero), jnp.where(left, zero, k)], axis=0)
            q = queries[d, h * pair : (h + 1) * pair, :]
            return jnp.dot(both, q, preferred_element_type=F32)

        def weigh(u, h, s):
            _, _, _, r = blocks[u]
            found = []
            for i in range(2):
                scale = prior[r, 2 * h + i] * (LOG2E / float(head_dim) ** 0.5)
                x = s[i * tile : (i + 1) * tile, :] * scale
                m = jnp.max(x, axis=0, keepdims=True)
                p = jnp.exp2(x - m)
                found.append((m, jnp.sum(p, axis=0, keepdims=True), p.astype(BF)))
            return found

        def gather(u, h, message, found):
            valid, _, d, _ = blocks[u]
            for i in range(2):
                row = (h % 2) * pair + i * head_dim
                m, total_w, p = found[i]
                part = jnp.dot(message[row : row + head_dim, :], p, preferred_element_type=F32)
                head = 2 * h + i
                one = slice(head, head + 1)
                rows = slice(head * head_dim, (head + 1) * head_dim)
                old = top[d, one, :]
                new = jnp.where(valid, jnp.maximum(old, m), old)
                keep = jnp.exp2(old - new)
                add = jnp.where(valid, jnp.exp2(m - new), 0.0)
                top[d, one, :] = new
                den[d, one, :] = den[d, one, :] * keep + total_w * add
                acc[d, rows, :] = acc[d, rows, :] * keep + part * add

        items = [(u, h) for u in range(BLOCKS) for h in range(heads // 2)]
        mapped, scored, weighed = {}, {}, {}
        a, b, d = LAGS
        for t in range(len(items) + d):
            if t < len(items) and items[t][1] % 2 == 0:
                u, h = items[t]
                mapped[u, h // 2] = maps(u, h // 2)
            if 0 <= t - a < len(items):
                u, h = items[t - a]
                scored[u, h] = scores(u, h, mapped[u, h // 2][0])
            if 0 <= t - b < len(items):
                u, h = items[t - b]
                weighed[u, h] = weigh(u, h, scored.pop((u, h)))
            if 0 <= t - d < len(items):
                u, h = items[t - d]
                gather(u, h, mapped[u, h // 2][1], weighed.pop((u, h)))
        return 0

    lax.fori_loop(0, (total + BLOCKS - 1) // BLOCKS, some_blocks, 0)


def first_phase(shape, slots, *refs):
    owners, heads, tile, head_dim = shape
    n = len(slots)
    count, b_src, b_dst, b_type, prior = refs[:5]
    tiles = refs[5 : 5 + n]
    wk, wv, att, msg, wq = refs[5 + n : 10 + n]
    hubs = refs[10 + n : 10 + n + owners]
    queries, acc, top, den, order, src, keys, values = refs[10 + n + owners :]
    quad = 4 * head_dim
    acc[...] = jnp.zeros(acc.shape, F32)
    top[...] = jnp.full(top.shape, EMPTY, F32)
    den[...] = jnp.zeros(den.shape, F32)
    for lo in range(0, owners, n):
        some = range(lo, min(lo + n, owners))
        for i, t in enumerate(some):
            src[i * tile : (i + 1) * tile, :] = hubs[t][...]
        for c in range(0, heads * head_dim, quad):
            q = jnp.dot(src[...], wq[:, c : c + quad], preferred_element_type=F32)
            for i, t in enumerate(some):
                queries[t, c : c + quad, :] = q[i * tile : (i + 1) * tile, :].T.astype(BF)
    run_blocks(
        *shape, slots, count, b_src, b_dst, b_type, prior, tiles, wk, wv, att, msg,
        queries, acc, top, den, order, src, keys, values,
    )


def later_phase(shape, slots, last, *refs):
    owners, heads, tile, head_dim = shape
    n = len(slots)
    count, b_src, b_dst, b_type, prior = refs[:5]
    tiles = refs[5 : 5 + n]
    wk, wv, att, msg, queries = refs[5 + n : 10 + n]
    given = refs[10 + n : 13 + n]
    rest = refs[13 + n :]
    if last:
        outs, rest = rest[:owners], rest[owners:]
        order, src, keys, values = rest
        acc, top, den = given
    else:
        acc, top, den, order, src, keys, values = rest
        acc[...], top[...], den[...] = (g[...] for g in given)
    run_blocks(
        *shape, slots, count, b_src, b_dst, b_type, prior, tiles, wk, wv, att, msg,
        queries, acc, top, den, order, src, keys, values,
    )
    if last:
        for t in range(owners):
            total = den[t]
            some = total > 0.0
            safe = jnp.where(some, total, 1.0)
            lse = jnp.where(some, top[t] + jnp.log(safe) * LOG2E, EMPTY)
            inverse = 1.0 / safe
            for h in range(heads):
                rows = slice(h * head_dim, (h + 1) * head_dim)
                outs[t][rows, :] = (acc[t, rows, :] * inverse[h : h + 1, :]).astype(BF)
            parts = split3(lse)
            for k in range(3):
                base = heads * head_dim + k * heads
                outs[t][base : base + heads, :] = parts[k]


def combine(owners, heads, head_dim, *refs):
    parts, w_out, out, agg = refs[:owners], refs[owners], refs[owners + 1], refs[owners + 2]
    base = heads * head_dim
    lse = []
    for r in parts:
        hi, mid, lo = (r[base + k * heads : base + (k + 1) * heads, :].astype(F32) for k in range(3))
        lse.append((hi + mid) + lo)
    best = functools.reduce(jnp.maximum, lse)
    weights = [jnp.exp2(v - best) for v in lse]
    whole = functools.reduce(jnp.add, weights)
    weights = [w / whole for w in weights]
    for h in range(heads):
        rows = slice(h * head_dim, (h + 1) * head_dim)
        total = functools.reduce(
            jnp.add,
            [r[rows, :].astype(F32) * w[h : h + 1, :] for r, w in zip(parts, weights)],
        )
        agg[:, rows] = total.T.astype(BF)
    out[...] = jnp.dot(agg[...], w_out[...], preferred_element_type=F32).astype(BF)


def body(
    node_src,
    hub_feat,
    w_query,
    w_key,
    w_value,
    w_out,
    w_att,
    w_msg,
    relation_prior,
    block_src,
    block_dst,
    block_type,
    block_count,
):
    groups = lax.axis_size("grp")
    owners = lax.axis_size("dev")
    tile, width = hub_feat.shape
    relations, heads = relation_prior.shape
    head_dim = width // heads
    pair, pairs = 2 * head_dim, heads // 2
    quads = heads // 4
    length = block_src.shape[1]
    shape = (owners, heads, tile, head_dim)
    smem = pl.BlockSpec(memory_space=pltpu.SMEM)
    apart = lambda x: pltpu.with_memory_space_constraint(x, pltpu.HBM)
    keep = lambda x: pltpu.with_memory_space_constraint(x, pltpu.VMEM)
    w_out = keep(w_out)
    vmem = pl.BlockSpec(memory_space=pltpu.VMEM)

    def move(x, axis, size, k):
        return lax.ppermute(x, axis, [(i, i ^ k) for i in range(size)])

    hubs = {0: hub_feat}
    for k in range(2, owners):
        hubs[k] = move(hub_feat, "dev", owners, k)
    srcs = {0: node_src}
    if groups == 8:
        steps = [(0, 1), (2, 6), (3, 7), (4, 5)]
        swaps = {1: (2, 6), 2: (4,)}
        for k in (1, 6):
            srcs[k] = move(node_src, "grp", groups, k)
    else:
        steps = [(k, k + 1) for k in range(0, groups, 2)]
        swaps = {}
        for k in range(1, groups):
            srcs[k] = move(node_src, "grp", groups, k)

    dense = (w_query, w_key, w_value, node_src, hub_feat)
    maps = [w.reshape(relations, pairs, pair, head_dim) for w in (w_att, w_msg)]
    chunks = 4
    att, msg, w_query, w_key, w_value, own_src, own_hub = pl.pallas_call(
        functools.partial(prepare, chunks),
        in_specs=[pl.BlockSpec(memory_space=pltpu.HBM)] * (2 + len(dense)),
        out_specs=[vmem] * (2 + len(dense)),
        out_shape=[pltpu.VMEM((relations, pairs, pair, pair), BF)] * 2
        + [pltpu.VMEM(x.shape, BF) for x in dense],
        scratch_shapes=[
            pltpu.VMEM((relations, pairs, pair, head_dim), BF),
            pltpu.VMEM((relations, pairs, pair, head_dim), BF),
            pltpu.SemaphoreType.DMA((2, chunks)),
            pltpu.SemaphoreType.DMA((len(dense),)),
        ],
        name="prepare",
        compiler_params=pltpu.CompilerParams(vmem_limit_bytes=LIMIT),
    )(*[apart(x) for x in (*maps, *dense)])
    hubs[1] = move(hub_feat, "dev", owners, 1)
    if groups == 8:
        source, hubs[1] = lax.optimization_barrier((node_src, hubs[1]))
        srcs[2] = move(source, "grp", groups, 2)
        srcs[4] = move(own_src, "grp", groups, 4)
    srcs[0], hubs[0] = own_src, own_hub
    att, msg, w_query, w_key, w_value = (keep(x) for x in (att, msg, w_query, w_key, w_value))
    lists = (
        block_count,
        block_src,
        block_dst,
        block_type,
        relation_prior,
    )
    state = [
        pltpu.VMEM((owners, width, tile), F32),
        pltpu.VMEM((owners, heads, tile), F32),
        pltpu.VMEM((owners, heads, tile), F32),
    ]
    rows_out = width + 3 * heads
    sent = [pltpu.VMEM((rows_out, tile), BF)] * owners
    for i, slots in enumerate(steps):
        n = len(slots)
        if i in swaps:
            carry = list(carry)
            *held, carry[2] = lax.optimization_barrier((*[srcs[k] for k in swaps[i]], carry[2]))
            for k, tile_k in zip(swaps[i], held):
                srcs[k] = tile_k
                srcs[k + 1] = move(tile_k, "grp", groups, 1)
        scratch = [
            pltpu.SMEM((2, length + 2), jnp.int32),
            pltpu.VMEM((n * tile, width), BF),
            pltpu.VMEM((n, quads, tile, 2 * pair), BF),
            pltpu.VMEM((n, quads, 2 * pair, tile), BF),
        ]
        cost = pl.CostEstimate(flops=COST, bytes_accessed=1024, transcendentals=0)
        tiles = [keep(srcs[k]) for k in slots]
        if i == 0:
            queries, *carry = pl.pallas_call(
                functools.partial(first_phase, shape, slots),
                in_specs=[smem] * 5 + [vmem] * (n + 5 + owners),
                out_specs=[vmem] * 4,
                out_shape=[pltpu.VMEM((owners, width, tile), BF)] + state,
                scratch_shapes=scratch,
                cost_estimate=cost,
            compiler_params=pltpu.CompilerParams(vmem_limit_bytes=LIMIT),
                name="phase0",
            )(*lists, *tiles, w_key, w_value, att, msg, w_query, *[keep(hubs[k]) for k in range(owners)])
            continue
        last = i == len(steps) - 1
        base = 10 + n
        aliases = {} if last else {base + k: k for k in range(3)}
        carry = pl.pallas_call(
            functools.partial(later_phase, shape, slots, last),
            in_specs=[smem] * 5 + [vmem] * (n + 8),
            out_specs=[vmem] * (owners if last else 3),
            out_shape=sent if last else state,
            scratch_shapes=scratch,
            input_output_aliases=aliases,
            cost_estimate=cost,
            compiler_params=pltpu.CompilerParams(vmem_limit_bytes=LIMIT),
            name="phase%d" % i,
        )(*lists, *tiles, w_key, w_value, att, msg, queries, *carry)
    parts = [carry[0]] + [move(carry[k], "dev", owners, k) for k in range(1, owners)]
    return pl.pallas_call(
        functools.partial(combine, owners, heads, head_dim),
        out_shape=jax.ShapeDtypeStruct((tile, width), BF),
        scratch_shapes=[pltpu.VMEM((tile, width), BF)],
        compiler_params=pltpu.CompilerParams(vmem_limit_bytes=LIMIT),
        name="combine",
    )(*[keep(p) for p in parts], w_out)


def solution(mesh):
    rows = P(("grp", "dev"), None)
    placed = (rows, rows) + (P(),) * 7 + (rows,) * 3 + (P(("grp", "dev")),)
    return jax.shard_map(body, mesh=mesh, in_specs=placed, out_specs=rows, check_vma=False)
```

```python
import functools

import jax
import jax.numpy as jnp
from jax import lax
from jax.experimental import pallas as pl
from jax.experimental.pallas import tpu as pltpu
from jax.sharding import PartitionSpec as P

BF = jnp.bfloat16
F32 = jnp.float32
LOG2E = 1.4426950408889634
EMPTY = -1e30
BLOCKS = 2
LAGS = (4, 8, 12)
LIMIT = 16 << 20
COST = 10**6


def split3(x):
    hi = x.astype(BF)
    rest = x - hi.astype(F32)
    mid = rest.astype(BF)
    lo = (rest - mid.astype(F32)).astype(BF)
    return hi, mid, lo


def prepare(parts, att, msg, *refs):
    kinds, pairs, pair, head_dim = att.shape
    plain = (len(refs) - 6) // 2
    given, refs = refs[:plain], refs[plain:]
    att_out, msg_out, copies = refs[0], refs[1], refs[2 : 2 + plain]
    att_in, msg_in, sem, plain_sem = refs[2 + plain :]
    size = kinds // parts
    moves = []
    for k in range(parts):
        some = pl.ds(k * size, size)
        moves.append(pltpu.make_async_copy(att.at[some], att_in.at[some], sem.at[0, k]))
        moves.append(pltpu.make_async_copy(msg.at[some], msg_in.at[some], sem.at[1, k]))
    rest = [pltpu.make_async_copy(g, c, plain_sem.at[i]) for i, (g, c) in enumerate(zip(given, copies))]
    for m in moves + rest:
        m.start()
    row = lax.broadcasted_iota(jnp.int32, (pair, head_dim), 0)
    col = lax.broadcasted_iota(jnp.int32, (pair, head_dim), 1)
    twice = jnp.where((row & (head_dim - 1)) == col, 1.0, 0.0).astype(BF)
    r2 = lax.broadcasted_iota(jnp.int32, (pair, 2 * pair), 0)
    c2 = lax.broadcasted_iota(jnp.int32, (pair, 2 * pair), 1)
    same = (r2 < head_dim) == ((c2 & (pair - 1)) < head_dim)
    none = jnp.zeros((head_dim, head_dim), BF)
    for k in range(parts):
        moves[2 * k].wait()
        moves[2 * k + 1].wait()

        def one(i, _):
            r = k * size + i
            for h in range(pairs):
                upper = jnp.concatenate([att_in[r, h, :head_dim, :], none], axis=1)
                lower = jnp.concatenate([none, att_in[r, h, head_dim:, :]], axis=1)
                att_out[r, h] = jnp.concatenate([upper, lower], axis=0)
            for h in range(0, pairs, 2):
                both = msg_in[r, h : h + 2].reshape(2 * pair, head_dim)
                m = lax.dot_general(twice, both, (((1,), (1,)), ((), ())), preferred_element_type=F32)
                m = jnp.where(same, m, 0.0).astype(BF)
                msg_out[r, h] = m[:, :pair]
                msg_out[r, h + 1] = m[:, pair:]
            return 0

        lax.fori_loop(0, size, one, 0)
    for m in rest:
        m.wait()


def run_blocks(
    owners, heads, tile, head_dim, slots, count, b_src, b_dst, b_type, prior, tiles, wk, wv, att, msg,
    queries, acc, top, den, order, src, keys, values,
):
    width = heads * head_dim
    pair, quad = 2 * head_dim, 4 * head_dim
    quads = heads // 4
    for i, ref in enumerate(tiles):
        src[i * tile : (i + 1) * tile, :] = ref[...]
    for q in range(quads):
        cols = slice(q * quad, (q + 1) * quad)
        k = jnp.dot(src[...], wk[:, cols], preferred_element_type=F32)
        v = jnp.dot(src[...], wv[:, cols], preferred_element_type=F32)
        for i in range(len(slots)):
            rows = slice(i * tile, (i + 1) * tile)
            keys[i, q] = k[rows, :].astype(BF)
            values[i, q] = v[rows, :].T.astype(BF)

    my_grp, my_dev = lax.axis_index("grp"), lax.axis_index("dev")

    def pick(j, n):
        s = b_src[0, j] ^ my_grp
        which = jnp.int32(0)
        hit = (s == slots[0]) & (j < count[0])
        for i in range(1, len(slots)):
            here = s == slots[i]
            which = jnp.where(here, i, which)
            hit = hit | (here & (j < count[0]))
        order[0, n] = j
        order[1, n] = which
        return n + hit.astype(jnp.int32)

    total = lax.fori_loop(0, b_src.shape[1], pick, jnp.int32(0), unroll=8)
    lane = lax.broadcasted_iota(jnp.int32, (tile, pair), 1)
    left = lane < head_dim
    none = jnp.zeros((pair, pair), BF)

    def diag(w, r, q):
        upper = jnp.concatenate([w[r, 2 * q], none], axis=1)
        lower = jnp.concatenate([none, w[r, 2 * q + 1]], axis=1)
        return jnp.concatenate([upper, lower], axis=0)

    def some_blocks(c, _):
        blocks = []
        for u in range(BLOCKS):
            n = c * BLOCKS + u
            valid = n < total
            j = jnp.where(valid, order[0, n], 0)
            s = jnp.where(valid, order[1, n], 0)
            blocks.append((valid, s, b_dst[0, j] ^ my_dev, b_type[0, j]))

        def maps(u, q):
            _, s, _, r = blocks[u]
            key_rel = jnp.dot(keys[s, q], diag(att, r, q), preferred_element_type=F32).astype(BF)
            message = jnp.dot(diag(msg, r, q), values[s, q], preferred_element_type=F32).astype(BF)
            return key_rel, message

        def scores(u, h, key_rel):
            _, _, d, _ = blocks[u]
            k = key_rel[:, (h % 2) * pair : (h % 2 + 1) * pair]
            zero = jnp.zeros_like(k)
            both = jnp.concatenate([jnp.where(left, k, zero), jnp.where(left, zero, k)], axis=0)
            q = queries[d, h * pair : (h + 1) * pair, :]
            return jnp.dot(both, q, preferred_element_type=F32)

        def weigh(u, h, s):
            _, _, _, r = blocks[u]
            found = []
            for i in range(2):
                scale = prior[r, 2 * h + i] * (LOG2E / float(head_dim) ** 0.5)
                x = s[i * tile : (i + 1) * tile, :] * scale
                m = jnp.max(x, axis=0, keepdims=True)
                p = jnp.exp2(x - m)
                found.append((m, jnp.sum(p, axis=0, keepdims=True), p.astype(BF)))
            return found

        def gather(u, h, message, found):
            valid, _, d, _ = blocks[u]
            for i in range(2):
                row = (h % 2) * pair + i * head_dim
                m, total_w, p = found[i]
                part = jnp.dot(message[row : row + head_dim, :], p, preferred_element_type=F32)
                head = 2 * h + i
                one = slice(head, head + 1)
                rows = slice(head * head_dim, (head + 1) * head_dim)
                old = top[d, one, :]
                new = jnp.where(valid, jnp.maximum(old, m), old)
                keep = jnp.exp2(old - new)
                add = jnp.where(valid, jnp.exp2(m - new), 0.0)
                top[d, one, :] = new
                den[d, one, :] = den[d, one, :] * keep + total_w * add
                acc[d, rows, :] = acc[d, rows, :] * keep + part * add

        items = [(u, h) for u in range(BLOCKS) for h in range(heads // 2)]
        mapped, scored, weighed = {}, {}, {}
        a, b, d = LAGS
        for t in range(len(items) + d):
            if t < len(items) and items[t][1] % 2 == 0:
                u, h = items[t]
                mapped[u, h // 2] = maps(u, h // 2)
            if 0 <= t - a < len(items):
                u, h = items[t - a]
                scored[u, h] = scores(u, h, mapped[u, h // 2][0])
            if 0 <= t - b < len(items):
                u, h = items[t - b]
                weighed[u, h] = weigh(u, h, scored.pop((u, h)))
            if 0 <= t - d < len(items):
                u, h = items[t - d]
                gather(u, h, mapped[u, h // 2][1], weighed.pop((u, h)))
        return 0

    lax.fori_loop(0, (total + BLOCKS - 1) // BLOCKS, some_blocks, 0)


def first_phase(shape, slots, *refs):
    owners, heads, tile, head_dim = shape
    n = len(slots)
    count, b_src, b_dst, b_type, prior = refs[:5]
    tiles = refs[5 : 5 + n]
    wk, wv, att, msg, wq = refs[5 + n : 10 + n]
    hubs = refs[10 + n : 10 + n + owners]
    queries, acc, top, den, order, src, keys, values = refs[10 + n + owners :]
    quad = 4 * head_dim
    acc[...] = jnp.zeros(acc.shape, F32)
    top[...] = jnp.full(top.shape, EMPTY, F32)
    den[...] = jnp.zeros(den.shape, F32)
    for lo in range(0, owners, n):
        some = range(lo, min(lo + n, owners))
        for i, t in enumerate(some):
            src[i * tile : (i + 1) * tile, :] = hubs[t][...]
        for c in range(0, heads * head_dim, quad):
            q = jnp.dot(src[...], wq[:, c : c + quad], preferred_element_type=F32)
            for i, t in enumerate(some):
                queries[t, c : c + quad, :] = q[i * tile : (i + 1) * tile, :].T.astype(BF)
    run_blocks(
        *shape, slots, count, b_src, b_dst, b_type, prior, tiles, wk, wv, att, msg,
        queries, acc, top, den, order, src, keys, values,
    )


def later_phase(shape, slots, last, *refs):
    owners, heads, tile, head_dim = shape
    n = len(slots)
    count, b_src, b_dst, b_type, prior = refs[:5]
    tiles = refs[5 : 5 + n]
    wk, wv, att, msg, queries = refs[5 + n : 10 + n]
    acc, top, den, *rest = refs[13 + n :]
    if last:
        outs, rest = rest[:owners], rest[owners:]
    order, src, keys, values = rest
    run_blocks(
        *shape, slots, count, b_src, b_dst, b_type, prior, tiles, wk, wv, att, msg,
        queries, acc, top, den, order, src, keys, values,
    )
    if last:
        for t in range(owners):
            total = den[t]
            some = total > 0.0
            safe = jnp.where(some, total, 1.0)
            lse = jnp.where(some, top[t] + jnp.log(safe) * LOG2E, EMPTY)
            inverse = 1.0 / safe
            for h in range(heads):
                rows = slice(h * head_dim, (h + 1) * head_dim)
                outs[t][rows, :] = (acc[t, rows, :] * inverse[h : h + 1, :]).astype(BF)
            parts = split3(lse)
            for k in range(3):
                base = heads * head_dim + k * heads
                outs[t][base : base + heads, :] = parts[k]


def combine(owners, heads, head_dim, *refs):
    parts, w_out, out, agg = refs[:owners], refs[owners], refs[owners + 1], refs[owners + 2]
    base = heads * head_dim
    lse = []
    for r in parts:
        hi, mid, lo = (r[base + k * heads : base + (k + 1) * heads, :].astype(F32) for k in range(3))
        lse.append((hi + mid) + lo)
    best = functools.reduce(jnp.maximum, lse)
    weights = [jnp.exp2(v - best) for v in lse]
    whole = functools.reduce(jnp.add, weights)
    weights = [w / whole for w in weights]
    for h in range(heads):
        rows = slice(h * head_dim, (h + 1) * head_dim)
        total = functools.reduce(
            jnp.add,
            [r[rows, :].astype(F32) * w[h : h + 1, :] for r, w in zip(parts, weights)],
        )
        agg[:, rows] = total.T.astype(BF)
    out[...] = jnp.dot(agg[...], w_out[...], preferred_element_type=F32).astype(BF)


def body(
    node_src,
    hub_feat,
    w_query,
    w_key,
    w_value,
    w_out,
    w_att,
    w_msg,
    relation_prior,
    block_src,
    block_dst,
    block_type,
    block_count,
):
    groups = lax.axis_size("grp")
    owners = lax.axis_size("dev")
    tile, width = hub_feat.shape
    relations, heads = relation_prior.shape
    head_dim = width // heads
    pair, pairs = 2 * head_dim, heads // 2
    quads = heads // 4
    length = block_src.shape[1]
    shape = (owners, heads, tile, head_dim)
    smem = pl.BlockSpec(memory_space=pltpu.SMEM)
    apart = lambda x: pltpu.with_memory_space_constraint(x, pltpu.HBM)
    keep = lambda x: pltpu.with_memory_space_constraint(x, pltpu.VMEM)
    w_out = keep(w_out)
    vmem = pl.BlockSpec(memory_space=pltpu.VMEM)

    def move(x, axis, size, k):
        return lax.ppermute(x, axis, [(i, i ^ k) for i in range(size)])

    hubs = {0: hub_feat}
    for k in range(2, owners):
        hubs[k] = move(hub_feat, "dev", owners, k)
    srcs = {0: node_src}
    if groups == 8:
        steps = [(0, 1), (2, 6), (3, 7), (4, 5)]
        swaps = {1: (2, 6), 2: (4,)}
        for k in (1, 6):
            srcs[k] = move(node_src, "grp", groups, k)
    else:
        steps = [(k, k + 1) for k in range(0, groups, 2)]
        swaps = {}
        for k in range(1, groups):
            srcs[k] = move(node_src, "grp", groups, k)

    dense = (w_query, w_key, w_value, node_src, hub_feat)
    maps = [w.reshape(relations, pairs, pair, head_dim) for w in (w_att, w_msg)]
    chunks = 4
    att, msg, w_query, w_key, w_value, own_src, own_hub = pl.pallas_call(
        functools.partial(prepare, chunks),
        in_specs=[pl.BlockSpec(memory_space=pltpu.HBM)] * (2 + len(dense)),
        out_specs=[vmem] * (2 + len(dense)),
        out_shape=[pltpu.VMEM((relations, pairs, pair, pair), BF)] * 2
        + [pltpu.VMEM(x.shape, BF) for x in dense],
        scratch_shapes=[
            pltpu.VMEM((relations, pairs, pair, head_dim), BF),
            pltpu.VMEM((relations, pairs, pair, head_dim), BF),
            pltpu.SemaphoreType.DMA((2, chunks)),
            pltpu.SemaphoreType.DMA((len(dense),)),
        ],
        name="prepare",
        compiler_params=pltpu.CompilerParams(vmem_limit_bytes=LIMIT),
    )(*[apart(x) for x in (*maps, *dense)])
    hubs[1] = move(hub_feat, "dev", owners, 1)
    if groups == 8:
        source, hubs[1] = lax.optimization_barrier((node_src, hubs[1]))
        srcs[2] = move(source, "grp", groups, 2)
        srcs[4] = move(own_src, "grp", groups, 4)
    srcs[0], hubs[0] = own_src, own_hub
    att, msg, w_query, w_key, w_value = (keep(x) for x in (att, msg, w_query, w_key, w_value))
    lists = (
        block_count,
        block_src,
        block_dst,
        block_type,
        relation_prior,
    )
    state = [
        pltpu.VMEM((owners, width, tile), F32),
        pltpu.VMEM((owners, heads, tile), F32),
        pltpu.VMEM((owners, heads, tile), F32),
    ]
    rows_out = width + 3 * heads
    sent = [pltpu.VMEM((rows_out, tile), BF)] * owners
    for i, slots in enumerate(steps):
        n = len(slots)
        if i in swaps:
            carry = list(carry)
            *held, carry[2] = lax.optimization_barrier((*[srcs[k] for k in swaps[i]], carry[2]))
            for k, tile_k in zip(swaps[i], held):
                srcs[k] = tile_k
                srcs[k + 1] = move(tile_k, "grp", groups, 1)
        scratch = [
            pltpu.SMEM((2, length + 2), jnp.int32),
            pltpu.VMEM((n * tile, width), BF),
            pltpu.VMEM((n, quads, tile, 2 * pair), BF),
            pltpu.VMEM((n, quads, 2 * pair, tile), BF),
        ]
        cost = pl.CostEstimate(flops=COST, bytes_accessed=1024, transcendentals=0)
        tiles = [keep(srcs[k]) for k in slots]
        if i == 0:
            queries, *carry = pl.pallas_call(
                functools.partial(first_phase, shape, slots),
                in_specs=[smem] * 5 + [vmem] * (n + 5 + owners),
                out_specs=[vmem] * 4,
                out_shape=[pltpu.VMEM((owners, width, tile), BF)] + state,
                scratch_shapes=scratch,
                cost_estimate=cost,
            compiler_params=pltpu.CompilerParams(vmem_limit_bytes=LIMIT),
                name="phase0",
            )(*lists, *tiles, w_key, w_value, att, msg, w_query, *[keep(hubs[k]) for k in range(owners)])
            continue
        last = i == len(steps) - 1
        base = 10 + n
        aliases = {base + k: k for k in range(3)}
        carry = pl.pallas_call(
            functools.partial(later_phase, shape, slots, last),
            in_specs=[smem] * 5 + [vmem] * (n + 8),
            out_specs=[vmem] * (3 + owners if last else 3),
            out_shape=state + sent if last else state,
            scratch_shapes=scratch,
            input_output_aliases=aliases,
            cost_estimate=cost,
            compiler_params=pltpu.CompilerParams(vmem_limit_bytes=LIMIT),
            name="phase%d" % i,
        )(*lists, *tiles, w_key, w_value, att, msg, queries, *carry)
    tiles = carry[3:]
    parts = [tiles[0]] + [move(tiles[k], "dev", owners, k) for k in range(1, owners)]
    return pl.pallas_call(
        functools.partial(combine, owners, heads, head_dim),
        out_shape=jax.ShapeDtypeStruct((tile, width), BF),
        scratch_shapes=[pltpu.VMEM((tile, width), BF)],
        compiler_params=pltpu.CompilerParams(vmem_limit_bytes=LIMIT),
        name="combine",
    )(*[keep(p) for p in parts], w_out)


def solution(mesh):
    rows = P(("grp", "dev"), None)
    placed = (rows, rows) + (P(),) * 7 + (rows,) * 3 + (P(("grp", "dev")),)
    return jax.shard_map(body, mesh=mesh, in_specs=placed, out_specs=rows, check_vma=False)
```

```python
import functools

import jax
import jax.numpy as jnp
from jax import lax
from jax.experimental import pallas as pl
from jax.experimental.pallas import tpu as pltpu
from jax.sharding import PartitionSpec as P

BF = jnp.bfloat16
F32 = jnp.float32
LOG2E = 1.4426950408889634
EMPTY = -1e30
BLOCKS = 2
LAGS = (4, 8, 12)
LIMIT = 16 << 20
COST = 10**6


def split3(x):
    hi = x.astype(BF)
    rest = x - hi.astype(F32)
    mid = rest.astype(BF)
    lo = (rest - mid.astype(F32)).astype(BF)
    return hi, mid, lo


def prepare(parts, att, msg, *refs):
    kinds, pairs, pair, head_dim = att.shape
    plain = (len(refs) - 6) // 2
    given, refs = refs[:plain], refs[plain:]
    att_out, msg_out, copies = refs[0], refs[1], refs[2 : 2 + plain]
    att_in, msg_in, sem, plain_sem = refs[2 + plain :]
    size = kinds // parts
    moves = []
    for k in range(parts):
        some = pl.ds(k * size, size)
        moves.append(pltpu.make_async_copy(att.at[some], att_in.at[some], sem.at[0, k]))
        moves.append(pltpu.make_async_copy(msg.at[some], msg_in.at[some], sem.at[1, k]))
    rest = [pltpu.make_async_copy(g, c, plain_sem.at[i]) for i, (g, c) in enumerate(zip(given, copies))]
    for m in moves + rest:
        m.start()
    row = lax.broadcasted_iota(jnp.int32, (pair, head_dim), 0)
    col = lax.broadcasted_iota(jnp.int32, (pair, head_dim), 1)
    twice = jnp.where((row & (head_dim - 1)) == col, 1.0, 0.0).astype(BF)
    r2 = lax.broadcasted_iota(jnp.int32, (pair, 2 * pair), 0)
    c2 = lax.broadcasted_iota(jnp.int32, (pair, 2 * pair), 1)
    same = (r2 < head_dim) == ((c2 & (pair - 1)) < head_dim)
    none = jnp.zeros((head_dim, head_dim), BF)
    for k in range(parts):
        moves[2 * k].wait()
        moves[2 * k + 1].wait()

        def one(i, _):
            r = k * size + i
            for h in range(pairs):
                upper = jnp.concatenate([att_in[r, h, :head_dim, :], none], axis=1)
                lower = jnp.concatenate([none, att_in[r, h, head_dim:, :]], axis=1)
                att_out[r, h] = jnp.concatenate([upper, lower], axis=0)
            for h in range(0, pairs, 2):
                both = msg_in[r, h : h + 2].reshape(2 * pair, head_dim)
                m = lax.dot_general(twice, both, (((1,), (1,)), ((), ())), preferred_element_type=F32)
                m = jnp.where(same, m, 0.0).astype(BF)
                msg_out[r, h] = m[:, :pair]
                msg_out[r, h + 1] = m[:, pair:]
            return 0

        lax.fori_loop(0, size, one, 0)
    for m in rest:
        m.wait()


def run_blocks(
    owners, heads, tile, head_dim, slots, count, b_src, b_dst, b_type, prior, tiles, wk, wv, att, msg,
    queries, acc, top, den, order, src, keys, values,
):
    width = heads * head_dim
    pair, quad = 2 * head_dim, 4 * head_dim
    quads = heads // 4
    for i, ref in enumerate(tiles):
        src[i * tile : (i + 1) * tile, :] = ref[...]
    for q in range(quads):
        cols = slice(q * quad, (q + 1) * quad)
        k = jnp.dot(src[...], wk[:, cols], preferred_element_type=F32)
        v = jnp.dot(src[...], wv[:, cols], preferred_element_type=F32)
        for i in range(len(slots)):
            rows = slice(i * tile, (i + 1) * tile)
            keys[i, q] = k[rows, :].astype(BF)
            values[i, q] = v[rows, :].T.astype(BF)

    my_grp, my_dev = lax.axis_index("grp"), lax.axis_index("dev")

    def pick(j, n):
        s = b_src[0, j] ^ my_grp
        which = jnp.int32(0)
        hit = (s == slots[0]) & (j < count[0])
        for i in range(1, len(slots)):
            here = s == slots[i]
            which = jnp.where(here, i, which)
            hit = hit | (here & (j < count[0]))
        order[0, n] = j
        order[1, n] = which
        return n + hit.astype(jnp.int32)

    total = lax.fori_loop(0, b_src.shape[1], pick, jnp.int32(0), unroll=8)
    lane = lax.broadcasted_iota(jnp.int32, (tile, pair), 1)
    left = lane < head_dim
    none = jnp.zeros((pair, pair), BF)

    def diag(w, r, q):
        upper = jnp.concatenate([w[r, 2 * q], none], axis=1)
        lower = jnp.concatenate([none, w[r, 2 * q + 1]], axis=1)
        return jnp.concatenate([upper, lower], axis=0)

    def some_blocks(c, _):
        blocks = []
        for u in range(BLOCKS):
            n = c * BLOCKS + u
            valid = n < total
            j = jnp.where(valid, order[0, n], 0)
            s = jnp.where(valid, order[1, n], 0)
            blocks.append((valid, s, b_dst[0, j] ^ my_dev, b_type[0, j]))

        def maps(u, q):
            _, s, _, r = blocks[u]
            key_rel = jnp.dot(keys[s, q], diag(att, r, q), preferred_element_type=F32).astype(BF)
            message = jnp.dot(diag(msg, r, q), values[s, q], preferred_element_type=F32).astype(BF)
            return key_rel, message

        def scores(u, h, key_rel):
            _, _, d, _ = blocks[u]
            k = key_rel[:, (h % 2) * pair : (h % 2 + 1) * pair]
            zero = jnp.zeros_like(k)
            both = jnp.concatenate([jnp.where(left, k, zero), jnp.where(left, zero, k)], axis=0)
            q = queries[d, h * pair : (h + 1) * pair, :]
            return jnp.dot(both, q, preferred_element_type=F32)

        def weigh(u, h, s):
            _, _, _, r = blocks[u]
            found = []
            for i in range(2):
                scale = prior[r, 2 * h + i] * (LOG2E / float(head_dim) ** 0.5)
                x = s[i * tile : (i + 1) * tile, :] * scale
                m = jnp.max(x, axis=0, keepdims=True)
                p = jnp.exp2(x - m)
                found.append((m, jnp.sum(p, axis=0, keepdims=True), p.astype(BF)))
            return found

        def gather(u, h, message, found):
            valid, _, d, _ = blocks[u]
            for i in range(2):
                row = (h % 2) * pair + i * head_dim
                m, total_w, p = found[i]
                part = jnp.dot(message[row : row + head_dim, :], p, preferred_element_type=F32)
                head = 2 * h + i
                one = slice(head, head + 1)
                rows = slice(head * head_dim, (head + 1) * head_dim)
                old = top[d, one, :]
                new = jnp.where(valid, jnp.maximum(old, m), old)
                keep = jnp.exp2(old - new)
                add = jnp.where(valid, jnp.exp2(m - new), 0.0)
                top[d, one, :] = new
                den[d, one, :] = den[d, one, :] * keep + total_w * add
                acc[d, rows, :] = acc[d, rows, :] * keep + part * add

        items = [(u, h) for u in range(BLOCKS) for h in range(heads // 2)]
        mapped, scored, weighed = {}, {}, {}
        a, b, d = LAGS
        for t in range(len(items) + d):
            if t < len(items) and items[t][1] % 2 == 0:
                u, h = items[t]
                mapped[u, h // 2] = maps(u, h // 2)
            if 0 <= t - a < len(items):
                u, h = items[t - a]
                scored[u, h] = scores(u, h, mapped[u, h // 2][0])
            if 0 <= t - b < len(items):
                u, h = items[t - b]
                weighed[u, h] = weigh(u, h, scored.pop((u, h)))
            if 0 <= t - d < len(items):
                u, h = items[t - d]
                gather(u, h, mapped[u, h // 2][1], weighed.pop((u, h)))
        return 0

    lax.fori_loop(0, (total + BLOCKS - 1) // BLOCKS, some_blocks, 0)


def first_phase(shape, slots, *refs):
    owners, heads, tile, head_dim = shape
    n = len(slots)
    count, b_src, b_dst, b_type, prior = refs[:5]
    tiles = refs[5 : 5 + n]
    wk, wv, att, msg, wq = refs[5 + n : 10 + n]
    hubs = refs[10 + n : 10 + n + owners]
    queries, acc, top, den, order, src, keys, values = refs[10 + n + owners :]
    quad = 4 * head_dim
    acc[...] = jnp.zeros(acc.shape, F32)
    top[...] = jnp.full(top.shape, EMPTY, F32)
    den[...] = jnp.zeros(den.shape, F32)
    for lo in range(0, owners, n):
        some = range(lo, min(lo + n, owners))
        for i, t in enumerate(some):
            src[i * tile : (i + 1) * tile, :] = hubs[t][...]
        for c in range(0, heads * head_dim, quad):
            q = jnp.dot(src[...], wq[:, c : c + quad], preferred_element_type=F32)
            for i, t in enumerate(some):
                queries[t, c : c + quad, :] = q[i * tile : (i + 1) * tile, :].T.astype(BF)
    run_blocks(
        *shape, slots, count, b_src, b_dst, b_type, prior, tiles, wk, wv, att, msg,
        queries, acc, top, den, order, src, keys, values,
    )


def later_phase(shape, slots, last, *refs):
    owners, heads, tile, head_dim = shape
    n = len(slots)
    count, b_src, b_dst, b_type, prior = refs[:5]
    tiles = refs[5 : 5 + n]
    wk, wv, att, msg, queries = refs[5 + n : 10 + n]
    acc, top, den, *rest = refs[13 + n :]
    if last:
        outs, rest = rest[:owners], rest[owners:]
    order, src, keys, values = rest
    run_blocks(
        *shape, slots, count, b_src, b_dst, b_type, prior, tiles, wk, wv, att, msg,
        queries, acc, top, den, order, src, keys, values,
    )
    if last:
        for t in range(owners):
            total = den[t]
            some = total > 0.0
            safe = jnp.where(some, total, 1.0)
            lse = jnp.where(some, top[t] + jnp.log(safe) * LOG2E, EMPTY)
            inverse = 1.0 / safe
            for h in range(heads):
                rows = slice(h * head_dim, (h + 1) * head_dim)
                outs[t][rows, :] = (acc[t, rows, :] * inverse[h : h + 1, :]).astype(BF)
            parts = split3(lse)
            for k in range(3):
                base = heads * head_dim + k * heads
                outs[t][base : base + heads, :] = parts[k]


def combine(owners, heads, head_dim, *refs):
    parts, w_out, out, agg = refs[:owners], refs[owners], refs[owners + 1], refs[owners + 2]
    base = heads * head_dim
    lse = []
    for r in parts:
        hi, mid, lo = (r[base + k * heads : base + (k + 1) * heads, :].astype(F32) for k in range(3))
        lse.append((hi + mid) + lo)
    best = functools.reduce(jnp.maximum, lse)
    weights = [jnp.exp2(v - best) for v in lse]
    whole = functools.reduce(jnp.add, weights)
    weights = [w / whole for w in weights]
    for h in range(heads):
        rows = slice(h * head_dim, (h + 1) * head_dim)
        total = functools.reduce(
            jnp.add,
            [r[rows, :].astype(F32) * w[h : h + 1, :] for r, w in zip(parts, weights)],
        )
        agg[:, rows] = total.T.astype(BF)
    out[...] = jnp.dot(agg[...], w_out[...], preferred_element_type=F32).astype(BF)


def body(
    node_src,
    hub_feat,
    w_query,
    w_key,
    w_value,
    w_out,
    w_att,
    w_msg,
    relation_prior,
    block_src,
    block_dst,
    block_type,
    block_count,
):
    groups = lax.axis_size("grp")
    owners = lax.axis_size("dev")
    tile, width = hub_feat.shape
    relations, heads = relation_prior.shape
    head_dim = width // heads
    pair, pairs = 2 * head_dim, heads // 2
    quads = heads // 4
    length = block_src.shape[1]
    shape = (owners, heads, tile, head_dim)
    smem = pl.BlockSpec(memory_space=pltpu.SMEM)
    apart = lambda x: pltpu.with_memory_space_constraint(x, pltpu.HBM)
    keep = lambda x: pltpu.with_memory_space_constraint(x, pltpu.VMEM)
    w_out = keep(w_out)
    vmem = pl.BlockSpec(memory_space=pltpu.VMEM)

    def move(x, axis, size, k):
        return lax.ppermute(x, axis, [(i, i ^ k) for i in range(size)])

    hubs = {0: hub_feat}
    for k in range(2, owners):
        hubs[k] = move(hub_feat, "dev", owners, k)
    srcs = {0: node_src}
    if groups == 8:
        steps = [(0, 1), (2, 6), (3, 4), (7, 5)]
        swaps = {2: (4,)}
        for k in (1, 6):
            srcs[k] = move(node_src, "grp", groups, k)
    else:
        steps = [(k, k + 1) for k in range(0, groups, 2)]
        swaps = {}
        for k in range(1, groups):
            srcs[k] = move(node_src, "grp", groups, k)

    dense = (w_query, w_key, w_value, node_src, hub_feat)
    maps = [w.reshape(relations, pairs, pair, head_dim) for w in (w_att, w_msg)]
    chunks = 4
    att, msg, w_query, w_key, w_value, own_src, own_hub = pl.pallas_call(
        functools.partial(prepare, chunks),
        in_specs=[pl.BlockSpec(memory_space=pltpu.HBM)] * (2 + len(dense)),
        out_specs=[vmem] * (2 + len(dense)),
        out_shape=[pltpu.VMEM((relations, pairs, pair, pair), BF)] * 2
        + [pltpu.VMEM(x.shape, BF) for x in dense],
        scratch_shapes=[
            pltpu.VMEM((relations, pairs, pair, head_dim), BF),
            pltpu.VMEM((relations, pairs, pair, head_dim), BF),
            pltpu.SemaphoreType.DMA((2, chunks)),
            pltpu.SemaphoreType.DMA((len(dense),)),
        ],
        name="prepare",
        compiler_params=pltpu.CompilerParams(vmem_limit_bytes=LIMIT),
    )(*[apart(x) for x in (*maps, *dense)])
    hubs[1] = move(hub_feat, "dev", owners, 1)
    if groups == 8:
        source, hubs[1] = lax.optimization_barrier((node_src, hubs[1]))
        srcs[2] = move(source, "grp", groups, 2)
        srcs[4] = move(own_src, "grp", groups, 4)
        srcs[3] = move(own_src, "grp", groups, 3)
    srcs[0], hubs[0] = own_src, own_hub
    att, msg, w_query, w_key, w_value = (keep(x) for x in (att, msg, w_query, w_key, w_value))
    lists = (
        block_count,
        block_src,
        block_dst,
        block_type,
        relation_prior,
    )
    state = [
        pltpu.VMEM((owners, width, tile), F32),
        pltpu.VMEM((owners, heads, tile), F32),
        pltpu.VMEM((owners, heads, tile), F32),
    ]
    rows_out = width + 3 * heads
    sent = [pltpu.VMEM((rows_out, tile), BF)] * owners
    for i, slots in enumerate(steps):
        n = len(slots)
        if groups == 8 and i == 1:
            carry = list(carry)
            source, carry[2] = lax.optimization_barrier((own_src, carry[2]))
            srcs[7] = move(source, "grp", groups, 7)
        if i in swaps:
            carry = list(carry)
            *held, carry[2] = lax.optimization_barrier((*[srcs[k] for k in swaps[i]], carry[2]))
            for k, tile_k in zip(swaps[i], held):
                srcs[k] = tile_k
                srcs[k + 1] = move(tile_k, "grp", groups, 1)
        scratch = [
            pltpu.SMEM((2, length + 2), jnp.int32),
            pltpu.VMEM((n * tile, width), BF),
            pltpu.VMEM((n, quads, tile, 2 * pair), BF),
            pltpu.VMEM((n, quads, 2 * pair, tile), BF),
        ]
        cost = pl.CostEstimate(flops=COST, bytes_accessed=1024, transcendentals=0)
        tiles = [keep(srcs[k]) for k in slots]
        if i == 0:
            queries, *carry = pl.pallas_call(
                functools.partial(first_phase, shape, slots),
                in_specs=[smem] * 5 + [vmem] * (n + 5 + owners),
                out_specs=[vmem] * 4,
                out_shape=[pltpu.VMEM((owners, width, tile), BF)] + state,
                scratch_shapes=scratch,
                cost_estimate=cost,
            compiler_params=pltpu.CompilerParams(vmem_limit_bytes=LIMIT),
                name="phase0",
            )(*lists, *tiles, w_key, w_value, att, msg, w_query, *[keep(hubs[k]) for k in range(owners)])
            continue
        last = i == len(steps) - 1
        base = 10 + n
        aliases = {base + k: k for k in range(3)}
        carry = pl.pallas_call(
            functools.partial(later_phase, shape, slots, last),
            in_specs=[smem] * 5 + [vmem] * (n + 8),
            out_specs=[vmem] * (3 + owners if last else 3),
            out_shape=state + sent if last else state,
            scratch_shapes=scratch,
            input_output_aliases=aliases,
            cost_estimate=cost,
            compiler_params=pltpu.CompilerParams(vmem_limit_bytes=LIMIT),
            name="phase%d" % i,
        )(*lists, *tiles, w_key, w_value, att, msg, queries, *carry)
    tiles = carry[3:]
    parts = [tiles[0]] + [move(tiles[k], "dev", owners, k) for k in range(1, owners)]
    return pl.pallas_call(
        functools.partial(combine, owners, heads, head_dim),
        out_shape=jax.ShapeDtypeStruct((tile, width), BF),
        scratch_shapes=[pltpu.VMEM((tile, width), BF)],
        compiler_params=pltpu.CompilerParams(vmem_limit_bytes=LIMIT),
        name="combine",
    )(*[keep(p) for p in parts], w_out)


def solution(mesh):
    rows = P(("grp", "dev"), None)
    placed = (rows, rows) + (P(),) * 7 + (rows,) * 3 + (P(("grp", "dev")),)
    return jax.shard_map(body, mesh=mesh, in_specs=placed, out_specs=rows, check_vma=False)
```

```python
import functools

import jax
import jax.numpy as jnp
from jax import lax
from jax.experimental import pallas as pl
from jax.experimental.pallas import tpu as pltpu
from jax.sharding import PartitionSpec as P

BF = jnp.bfloat16
F32 = jnp.float32
LOG2E = 1.4426950408889634
EMPTY = -1e30
BLOCKS = 2
LAGS = (4, 8, 12)
LIMIT = 16 << 20
COST = 10**6


def split3(x):
    hi = x.astype(BF)
    rest = x - hi.astype(F32)
    mid = rest.astype(BF)
    lo = (rest - mid.astype(F32)).astype(BF)
    return hi, mid, lo


def prepare(parts, att, msg, *refs):
    kinds, pairs, pair, head_dim = att.shape
    plain = (len(refs) - 6) // 2
    given, refs = refs[:plain], refs[plain:]
    att_out, msg_out, copies = refs[0], refs[1], refs[2 : 2 + plain]
    att_in, msg_in, sem, plain_sem = refs[2 + plain :]
    size = kinds // parts
    moves = []
    for k in range(parts):
        some = pl.ds(k * size, size)
        moves.append(pltpu.make_async_copy(att.at[some], att_in.at[some], sem.at[0, k]))
        moves.append(pltpu.make_async_copy(msg.at[some], msg_in.at[some], sem.at[1, k]))
    rest = [pltpu.make_async_copy(g, c, plain_sem.at[i]) for i, (g, c) in enumerate(zip(given, copies))]
    for m in moves + rest:
        m.start()
    row = lax.broadcasted_iota(jnp.int32, (pair, head_dim), 0)
    col = lax.broadcasted_iota(jnp.int32, (pair, head_dim), 1)
    twice = jnp.where((row & (head_dim - 1)) == col, 1.0, 0.0).astype(BF)
    r2 = lax.broadcasted_iota(jnp.int32, (pair, 2 * pair), 0)
    c2 = lax.broadcasted_iota(jnp.int32, (pair, 2 * pair), 1)
    same = (r2 < head_dim) == ((c2 & (pair - 1)) < head_dim)
    none = jnp.zeros((head_dim, head_dim), BF)
    for k in range(parts):
        moves[2 * k].wait()
        moves[2 * k + 1].wait()

        def one(i, _):
            r = k * size + i
            for h in range(pairs):
                upper = jnp.concatenate([att_in[r, h, :head_dim, :], none], axis=1)
                lower = jnp.concatenate([none, att_in[r, h, head_dim:, :]], axis=1)
                att_out[r, h] = jnp.concatenate([upper, lower], axis=0)
            for h in range(0, pairs, 2):
                both = msg_in[r, h : h + 2].reshape(2 * pair, head_dim)
                m = lax.dot_general(twice, both, (((1,), (1,)), ((), ())), preferred_element_type=F32)
                m = jnp.where(same, m, 0.0).astype(BF)
                msg_out[r, h] = m[:, :pair]
                msg_out[r, h + 1] = m[:, pair:]
            return 0

        lax.fori_loop(0, size, one, 0)
    for m in rest:
        m.wait()


def run_blocks(
    owners, heads, tile, head_dim, slots, count, b_src, b_dst, b_type, prior, tiles, wk, wv, att, msg,
    queries, acc, top, den, order, src, keys, values,
):
    width = heads * head_dim
    pair, quad = 2 * head_dim, 4 * head_dim
    quads = heads // 4
    for i, ref in enumerate(tiles):
        src[i * tile : (i + 1) * tile, :] = ref[...]
    for q in range(quads):
        cols = slice(q * quad, (q + 1) * quad)
        k = jnp.dot(src[...], wk[:, cols], preferred_element_type=F32)
        v = jnp.dot(src[...], wv[:, cols], preferred_element_type=F32)
        for i in range(len(slots)):
            rows = slice(i * tile, (i + 1) * tile)
            keys[i, q] = k[rows, :].astype(BF)
            values[i, q] = v[rows, :].T.astype(BF)

    my_grp, my_dev = lax.axis_index("grp"), lax.axis_index("dev")

    def pick(j, n):
        s = b_src[0, j] ^ my_grp
        which = jnp.int32(0)
        hit = (s == slots[0]) & (j < count[0])
        for i in range(1, len(slots)):
            here = s == slots[i]
            which = jnp.where(here, i, which)
            hit = hit | (here & (j < count[0]))
        order[0, n] = j
        order[1, n] = which
        return n + hit.astype(jnp.int32)

    total = lax.fori_loop(0, b_src.shape[1], pick, jnp.int32(0), unroll=8)
    lane = lax.broadcasted_iota(jnp.int32, (tile, pair), 1)
    left = lane < head_dim
    none = jnp.zeros((pair, pair), BF)

    def diag(w, r, q):
        upper = jnp.concatenate([w[r, 2 * q], none], axis=1)
        lower = jnp.concatenate([none, w[r, 2 * q + 1]], axis=1)
        return jnp.concatenate([upper, lower], axis=0)

    def some_blocks(c, _):
        blocks = []
        for u in range(BLOCKS):
            n = c * BLOCKS + u
            valid = n < total
            j = jnp.where(valid, order[0, n], 0)
            s = jnp.where(valid, order[1, n], 0)
            blocks.append((valid, s, b_dst[0, j] ^ my_dev, b_type[0, j]))

        def maps(u, q):
            _, s, _, r = blocks[u]
            key_rel = jnp.dot(keys[s, q], diag(att, r, q), preferred_element_type=F32).astype(BF)
            message = jnp.dot(diag(msg, r, q), values[s, q], preferred_element_type=F32).astype(BF)
            return key_rel, message

        def scores(u, h, key_rel):
            _, _, d, _ = blocks[u]
            k = key_rel[:, (h % 2) * pair : (h % 2 + 1) * pair]
            zero = jnp.zeros_like(k)
            both = jnp.concatenate([jnp.where(left, k, zero), jnp.where(left, zero, k)], axis=0)
            q = queries[d, h * pair : (h + 1) * pair, :]
            return jnp.dot(both, q, preferred_element_type=F32)

        def weigh(u, h, s):
            _, _, _, r = blocks[u]
            found = []
            for i in range(2):
                scale = prior[r, 2 * h + i] * (LOG2E / float(head_dim) ** 0.5)
                x = s[i * tile : (i + 1) * tile, :] * scale
                m = jnp.max(x, axis=0, keepdims=True)
                p = jnp.exp2(x - m)
                found.append((m, jnp.sum(p, axis=0, keepdims=True), p.astype(BF)))
            return found

        def gather(u, h, message, found):
            valid, _, d, _ = blocks[u]
            for i in range(2):
                row = (h % 2) * pair + i * head_dim
                m, total_w, p = found[i]
                part = jnp.dot(message[row : row + head_dim, :], p, preferred_element_type=F32)
                head = 2 * h + i
                one = slice(head, head + 1)
                rows = slice(head * head_dim, (head + 1) * head_dim)
                old = top[d, one, :]
                new = jnp.where(valid, jnp.maximum(old, m), old)
                keep = jnp.exp2(old - new)
                add = jnp.where(valid, jnp.exp2(m - new), 0.0)
                top[d, one, :] = new
                den[d, one, :] = den[d, one, :] * keep + total_w * add
                acc[d, rows, :] = acc[d, rows, :] * keep + part * add

        items = [(u, h) for u in range(BLOCKS) for h in range(heads // 2)]
        mapped, scored, weighed = {}, {}, {}
        a, b, d = LAGS
        for t in range(len(items) + d):
            if t < len(items) and items[t][1] % 2 == 0:
                u, h = items[t]
                mapped[u, h // 2] = maps(u, h // 2)
            if 0 <= t - a < len(items):
                u, h = items[t - a]
                scored[u, h] = scores(u, h, mapped[u, h // 2][0])
            if 0 <= t - b < len(items):
                u, h = items[t - b]
                weighed[u, h] = weigh(u, h, scored.pop((u, h)))
            if 0 <= t - d < len(items):
                u, h = items[t - d]
                gather(u, h, mapped[u, h // 2][1], weighed.pop((u, h)))
        return 0

    lax.fori_loop(0, (total + BLOCKS - 1) // BLOCKS, some_blocks, 0)


def first_phase(shape, slots, *refs):
    owners, heads, tile, head_dim = shape
    n = len(slots)
    count, b_src, b_dst, b_type, prior = refs[:5]
    tiles = refs[5 : 5 + n]
    wk, wv, att, msg, wq = refs[5 + n : 10 + n]
    hubs = refs[10 + n : 10 + n + owners]
    queries, acc, top, den, order, src, keys, values = refs[10 + n + owners :]
    quad = 4 * head_dim
    acc[...] = jnp.zeros(acc.shape, F32)
    top[...] = jnp.full(top.shape, EMPTY, F32)
    den[...] = jnp.zeros(den.shape, F32)
    for lo in range(0, owners, n):
        some = range(lo, min(lo + n, owners))
        for i, t in enumerate(some):
            src[i * tile : (i + 1) * tile, :] = hubs[t][...]
        for c in range(0, heads * head_dim, quad):
            q = jnp.dot(src[...], wq[:, c : c + quad], preferred_element_type=F32)
            for i, t in enumerate(some):
                queries[t, c : c + quad, :] = q[i * tile : (i + 1) * tile, :].T.astype(BF)
    run_blocks(
        *shape, slots, count, b_src, b_dst, b_type, prior, tiles, wk, wv, att, msg,
        queries, acc, top, den, order, src, keys, values,
    )


def later_phase(shape, slots, last, *refs):
    owners, heads, tile, head_dim = shape
    n = len(slots)
    count, b_src, b_dst, b_type, prior = refs[:5]
    tiles = refs[5 : 5 + n]
    wk, wv, att, msg, queries = refs[5 + n : 10 + n]
    acc, top, den, *rest = refs[13 + n :]
    if last:
        outs, rest = rest[:owners], rest[owners:]
    order, src, keys, values = rest
    run_blocks(
        *shape, slots, count, b_src, b_dst, b_type, prior, tiles, wk, wv, att, msg,
        queries, acc, top, den, order, src, keys, values,
    )
    if last:
        for t in range(owners):
            total = den[t]
            some = total > 0.0
            safe = jnp.where(some, total, 1.0)
            lse = jnp.where(some, top[t] + jnp.log(safe) * LOG2E, EMPTY)
            inverse = 1.0 / safe
            for h in range(heads):
                rows = slice(h * head_dim, (h + 1) * head_dim)
                outs[t][rows, :] = (acc[t, rows, :] * inverse[h : h + 1, :]).astype(BF)
            parts = split3(lse)
            for k in range(3):
                base = heads * head_dim + k * heads
                outs[t][base : base + heads, :] = parts[k]


def combine(owners, heads, head_dim, *refs):
    parts, w_out, out, agg = refs[:owners], refs[owners], refs[owners + 1], refs[owners + 2]
    base = heads * head_dim
    lse = []
    for r in parts:
        hi, mid, lo = (r[base + k * heads : base + (k + 1) * heads, :].astype(F32) for k in range(3))
        lse.append((hi + mid) + lo)
    best = functools.reduce(jnp.maximum, lse)
    weights = [jnp.exp2(v - best) for v in lse]
    whole = functools.reduce(jnp.add, weights)
    weights = [w / whole for w in weights]
    for h in range(heads):
        rows = slice(h * head_dim, (h + 1) * head_dim)
        total = functools.reduce(
            jnp.add,
            [r[rows, :].astype(F32) * w[h : h + 1, :] for r, w in zip(parts, weights)],
        )
        agg[:, rows] = total.T.astype(BF)
    out[...] = jnp.dot(agg[...], w_out[...], preferred_element_type=F32).astype(BF)


def body(
    node_src,
    hub_feat,
    w_query,
    w_key,
    w_value,
    w_out,
    w_att,
    w_msg,
    relation_prior,
    block_src,
    block_dst,
    block_type,
    block_count,
):
    groups = lax.axis_size("grp")
    owners = lax.axis_size("dev")
    tile, width = hub_feat.shape
    relations, heads = relation_prior.shape
    head_dim = width // heads
    pair, pairs = 2 * head_dim, heads // 2
    quads = heads // 4
    length = block_src.shape[1]
    shape = (owners, heads, tile, head_dim)
    smem = pl.BlockSpec(memory_space=pltpu.SMEM)
    apart = lambda x: pltpu.with_memory_space_constraint(x, pltpu.HBM)
    keep = lambda x: pltpu.with_memory_space_constraint(x, pltpu.VMEM)
    w_out = keep(w_out)
    vmem = pl.BlockSpec(memory_space=pltpu.VMEM)

    def move(x, axis, size, k):
        return lax.ppermute(x, axis, [(i, i ^ k) for i in range(size)])

    hubs = {0: hub_feat}
    for k in range(2, owners):
        hubs[k] = move(hub_feat, "dev", owners, k)
    srcs = {0: node_src}
    if groups == 8:
        steps = [(0, 1), (2, 6), (3, 4), (7, 5)]
        swaps = {2: (4,)}
        for k in (1, 6):
            srcs[k] = move(node_src, "grp", groups, k)
    else:
        steps = [(k, k + 1) for k in range(0, groups, 2)]
        swaps = {}
        for k in range(1, groups):
            srcs[k] = move(node_src, "grp", groups, k)

    dense = (w_query, w_key, w_value, node_src, hub_feat)
    maps = [w.reshape(relations, pairs, pair, head_dim) for w in (w_att, w_msg)]
    chunks = 4
    att, msg, w_query, w_key, w_value, own_src, own_hub = pl.pallas_call(
        functools.partial(prepare, chunks),
        in_specs=[pl.BlockSpec(memory_space=pltpu.HBM)] * (2 + len(dense)),
        out_specs=[vmem] * (2 + len(dense)),
        out_shape=[pltpu.VMEM((relations, pairs, pair, pair), BF)] * 2
        + [pltpu.VMEM(x.shape, BF) for x in dense],
        scratch_shapes=[
            pltpu.VMEM((relations, pairs, pair, head_dim), BF),
            pltpu.VMEM((relations, pairs, pair, head_dim), BF),
            pltpu.SemaphoreType.DMA((2, chunks)),
            pltpu.SemaphoreType.DMA((len(dense),)),
        ],
        name="prepare",
        compiler_params=pltpu.CompilerParams(vmem_limit_bytes=LIMIT),
    )(*[apart(x) for x in (*maps, *dense)])
    hubs[1] = move(hub_feat, "dev", owners, 1)
    if groups == 8:
        source, hubs[1] = lax.optimization_barrier((node_src, hubs[1]))
        srcs[2] = move(source, "grp", groups, 2)
        srcs[4] = move(own_src, "grp", groups, 4)
        for k in (3, 7):
            srcs[k] = move(own_src, "grp", groups, k)
    srcs[0], hubs[0] = own_src, own_hub
    att, msg, w_query, w_key, w_value = (keep(x) for x in (att, msg, w_query, w_key, w_value))
    lists = (
        block_count,
        block_src,
        block_dst,
        block_type,
        relation_prior,
    )
    state = [
        pltpu.VMEM((owners, width, tile), F32),
        pltpu.VMEM((owners, heads, tile), F32),
        pltpu.VMEM((owners, heads, tile), F32),
    ]
    rows_out = width + 3 * heads
    sent = [pltpu.VMEM((rows_out, tile), BF)] * owners
    for i, slots in enumerate(steps):
        n = len(slots)
        if i in swaps:
            carry = list(carry)
            *held, carry[2] = lax.optimization_barrier((*[srcs[k] for k in swaps[i]], carry[2]))
            for k, tile_k in zip(swaps[i], held):
                srcs[k] = tile_k
                srcs[k + 1] = move(tile_k, "grp", groups, 1)
        scratch = [
            pltpu.SMEM((2, length + 2), jnp.int32),
            pltpu.VMEM((n * tile, width), BF),
            pltpu.VMEM((n, quads, tile, 2 * pair), BF),
            pltpu.VMEM((n, quads, 2 * pair, tile), BF),
        ]
        cost = pl.CostEstimate(flops=COST, bytes_accessed=1024, transcendentals=0)
        tiles = [keep(srcs[k]) for k in slots]
        if i == 0:
            queries, *carry = pl.pallas_call(
                functools.partial(first_phase, shape, slots),
                in_specs=[smem] * 5 + [vmem] * (n + 5 + owners),
                out_specs=[vmem] * 4,
                out_shape=[pltpu.VMEM((owners, width, tile), BF)] + state,
                scratch_shapes=scratch,
                cost_estimate=cost,
            compiler_params=pltpu.CompilerParams(vmem_limit_bytes=LIMIT),
                name="phase0",
            )(*lists, *tiles, w_key, w_value, att, msg, w_query, *[keep(hubs[k]) for k in range(owners)])
            continue
        last = i == len(steps) - 1
        base = 10 + n
        aliases = {base + k: k for k in range(3)}
        carry = pl.pallas_call(
            functools.partial(later_phase, shape, slots, last),
            in_specs=[smem] * 5 + [vmem] * (n + 8),
            out_specs=[vmem] * (3 + owners if last else 3),
            out_shape=state + sent if last else state,
            scratch_shapes=scratch,
            input_output_aliases=aliases,
            cost_estimate=cost,
            compiler_params=pltpu.CompilerParams(vmem_limit_bytes=LIMIT),
            name="phase%d" % i,
        )(*lists, *tiles, w_key, w_value, att, msg, queries, *carry)
    tiles = carry[3:]
    parts = [tiles[0]] + [move(tiles[k], "dev", owners, k) for k in range(1, owners)]
    return pl.pallas_call(
        functools.partial(combine, owners, heads, head_dim),
        out_shape=jax.ShapeDtypeStruct((tile, width), BF),
        scratch_shapes=[pltpu.VMEM((tile, width), BF)],
        compiler_params=pltpu.CompilerParams(vmem_limit_bytes=LIMIT),
        name="combine",
    )(*[keep(p) for p in parts], w_out)


def solution(mesh):
    rows = P(("grp", "dev"), None)
    placed = (rows, rows) + (P(),) * 7 + (rows,) * 3 + (P(("grp", "dev")),)
    return jax.shard_map(body, mesh=mesh, in_specs=placed, out_specs=rows, check_vma=False)
```

```python
import functools

import jax
import jax.numpy as jnp
from jax import lax
from jax.experimental import pallas as pl
from jax.experimental.pallas import tpu as pltpu
from jax.sharding import PartitionSpec as P

BF = jnp.bfloat16
F32 = jnp.float32
LOG2E = 1.4426950408889634
EMPTY = -1e30
BLOCKS = 2
LAGS = (4, 8, 12)
LIMIT = 16 << 20
COST = 10**6


def split3(x):
    hi = x.astype(BF)
    rest = x - hi.astype(F32)
    mid = rest.astype(BF)
    lo = (rest - mid.astype(F32)).astype(BF)
    return hi, mid, lo


def prepare(parts, att, msg, *refs):
    kinds, pairs, pair, head_dim = att.shape
    plain = (len(refs) - 6) // 2
    given, refs = refs[:plain], refs[plain:]
    att_out, msg_out, copies = refs[0], refs[1], refs[2 : 2 + plain]
    att_in, msg_in, sem, plain_sem = refs[2 + plain :]
    size = kinds // parts
    moves = []
    for k in range(parts):
        some = pl.ds(k * size, size)
        moves.append(pltpu.make_async_copy(att.at[some], att_in.at[some], sem.at[0, k]))
        moves.append(pltpu.make_async_copy(msg.at[some], msg_in.at[some], sem.at[1, k]))
    rest = [pltpu.make_async_copy(g, c, plain_sem.at[i]) for i, (g, c) in enumerate(zip(given, copies))]
    for m in moves + rest:
        m.start()
    row = lax.broadcasted_iota(jnp.int32, (pair, head_dim), 0)
    col = lax.broadcasted_iota(jnp.int32, (pair, head_dim), 1)
    twice = jnp.where((row & (head_dim - 1)) == col, 1.0, 0.0).astype(BF)
    r2 = lax.broadcasted_iota(jnp.int32, (pair, 2 * pair), 0)
    c2 = lax.broadcasted_iota(jnp.int32, (pair, 2 * pair), 1)
    same = (r2 < head_dim) == ((c2 & (pair - 1)) < head_dim)
    none = jnp.zeros((head_dim, head_dim), BF)
    for k in range(parts):
        moves[2 * k].wait()
        moves[2 * k + 1].wait()

        def one(i, _):
            r = k * size + i
            for h in range(pairs):
                upper = jnp.concatenate([att_in[r, h, :head_dim, :], none], axis=1)
                lower = jnp.concatenate([none, att_in[r, h, head_dim:, :]], axis=1)
                att_out[r, h] = jnp.concatenate([upper, lower], axis=0)
            for h in range(0, pairs, 2):
                both = msg_in[r, h : h + 2].reshape(2 * pair, head_dim)
                m = lax.dot_general(twice, both, (((1,), (1,)), ((), ())), preferred_element_type=F32)
                m = jnp.where(same, m, 0.0).astype(BF)
                msg_out[r, h] = m[:, :pair]
                msg_out[r, h + 1] = m[:, pair:]
            return 0

        lax.fori_loop(0, size, one, 0)
    for m in rest:
        m.wait()


def run_blocks(
    owners, heads, tile, head_dim, slots, count, b_src, b_dst, b_type, prior, tiles, wk, wv, att, msg,
    queries, acc, top, den, order, src, keys, values,
):
    width = heads * head_dim
    pair, quad = 2 * head_dim, 4 * head_dim
    quads = heads // 4
    for i, ref in enumerate(tiles):
        src[i * tile : (i + 1) * tile, :] = ref[...]
    for q in range(quads):
        cols = slice(q * quad, (q + 1) * quad)
        k = jnp.dot(src[...], wk[:, cols], preferred_element_type=F32)
        v = jnp.dot(src[...], wv[:, cols], preferred_element_type=F32)
        for i in range(len(slots)):
            rows = slice(i * tile, (i + 1) * tile)
            keys[i, q] = k[rows, :].astype(BF)
            values[i, q] = v[rows, :].T.astype(BF)

    my_grp, my_dev = lax.axis_index("grp"), lax.axis_index("dev")

    def pick(j, n):
        s = b_src[0, j] ^ my_grp
        which = jnp.int32(0)
        hit = (s == slots[0]) & (j < count[0])
        for i in range(1, len(slots)):
            here = s == slots[i]
            which = jnp.where(here, i, which)
            hit = hit | (here & (j < count[0]))
        order[0, n] = j
        order[1, n] = which
        return n + hit.astype(jnp.int32)

    total = lax.fori_loop(0, b_src.shape[1], pick, jnp.int32(0), unroll=8)
    lane = lax.broadcasted_iota(jnp.int32, (tile, pair), 1)
    left = lane < head_dim
    none = jnp.zeros((pair, pair), BF)

    def diag(w, r, q):
        upper = jnp.concatenate([w[r, 2 * q], none], axis=1)
        lower = jnp.concatenate([none, w[r, 2 * q + 1]], axis=1)
        return jnp.concatenate([upper, lower], axis=0)

    def some_blocks(c, _):
        blocks = []
        for u in range(BLOCKS):
            n = c * BLOCKS + u
            valid = n < total
            j = jnp.where(valid, order[0, n], 0)
            s = jnp.where(valid, order[1, n], 0)
            blocks.append((valid, s, b_dst[0, j] ^ my_dev, b_type[0, j]))

        def maps(u, q):
            _, s, _, r = blocks[u]
            key_rel = jnp.dot(keys[s, q], diag(att, r, q), preferred_element_type=F32).astype(BF)
            message = jnp.dot(diag(msg, r, q), values[s, q], preferred_element_type=F32).astype(BF)
            return key_rel, message

        def scores(u, h, key_rel):
            _, _, d, _ = blocks[u]
            k = key_rel[:, (h % 2) * pair : (h % 2 + 1) * pair]
            zero = jnp.zeros_like(k)
            both = jnp.concatenate([jnp.where(left, k, zero), jnp.where(left, zero, k)], axis=0)
            q = queries[d, h * pair : (h + 1) * pair, :]
            return jnp.dot(both, q, preferred_element_type=F32)

        def weigh(u, h, s):
            _, _, _, r = blocks[u]
            found = []
            for i in range(2):
                scale = prior[r, 2 * h + i] * (LOG2E / float(head_dim) ** 0.5)
                x = s[i * tile : (i + 1) * tile, :] * scale
                m = jnp.max(x, axis=0, keepdims=True)
                p = jnp.exp2(x - m)
                found.append((m, jnp.sum(p, axis=0, keepdims=True), p.astype(BF)))
            return found

        def gather(u, h, message, found):
            valid, _, d, _ = blocks[u]
            for i in range(2):
                row = (h % 2) * pair + i * head_dim
                m, total_w, p = found[i]
                part = jnp.dot(message[row : row + head_dim, :], p, preferred_element_type=F32)
                head = 2 * h + i
                one = slice(head, head + 1)
                rows = slice(head * head_dim, (head + 1) * head_dim)
                old = top[d, one, :]
                new = jnp.where(valid, jnp.maximum(old, m), old)
                keep = jnp.exp2(old - new)
                add = jnp.where(valid, jnp.exp2(m - new), 0.0)
                top[d, one, :] = new
                den[d, one, :] = den[d, one, :] * keep + total_w * add
                acc[d, rows, :] = acc[d, rows, :] * keep + part * add

        items = [(u, h) for u in range(BLOCKS) for h in range(heads // 2)]
        mapped, scored, weighed = {}, {}, {}
        a, b, d = LAGS
        for t in range(len(items) + d):
            if t < len(items) and items[t][1] % 2 == 0:
                u, h = items[t]
                mapped[u, h // 2] = maps(u, h // 2)
            if 0 <= t - a < len(items):
                u, h = items[t - a]
                scored[u, h] = scores(u, h, mapped[u, h // 2][0])
            if 0 <= t - b < len(items):
                u, h = items[t - b]
                weighed[u, h] = weigh(u, h, scored.pop((u, h)))
            if 0 <= t - d < len(items):
                u, h = items[t - d]
                gather(u, h, mapped[u, h // 2][1], weighed.pop((u, h)))
        return 0

    lax.fori_loop(0, (total + BLOCKS - 1) // BLOCKS, some_blocks, 0)


def first_phase(shape, slots, *refs):
    owners, heads, tile, head_dim = shape
    n = len(slots)
    count, b_src, b_dst, b_type, prior = refs[:5]
    tiles = refs[5 : 5 + n]
    wk, wv, att, msg, wq = refs[5 + n : 10 + n]
    hubs = refs[10 + n : 10 + n + owners]
    queries, acc, top, den, order, src, keys, values = refs[10 + n + owners :]
    quad = 4 * head_dim
    acc[...] = jnp.zeros(acc.shape, F32)
    top[...] = jnp.full(top.shape, EMPTY, F32)
    den[...] = jnp.zeros(den.shape, F32)
    for lo in range(0, owners, n):
        some = range(lo, min(lo + n, owners))
        for i, t in enumerate(some):
            src[i * tile : (i + 1) * tile, :] = hubs[t][...]
        for c in range(0, heads * head_dim, quad):
            q = jnp.dot(src[...], wq[:, c : c + quad], preferred_element_type=F32)
            for i, t in enumerate(some):
                queries[t, c : c + quad, :] = q[i * tile : (i + 1) * tile, :].T.astype(BF)
    run_blocks(
        *shape, slots, count, b_src, b_dst, b_type, prior, tiles, wk, wv, att, msg,
        queries, acc, top, den, order, src, keys, values,
    )


def later_phase(shape, slots, last, *refs):
    owners, heads, tile, head_dim = shape
    n = len(slots)
    count, b_src, b_dst, b_type, prior = refs[:5]
    tiles = refs[5 : 5 + n]
    wk, wv, att, msg, queries = refs[5 + n : 10 + n]
    acc, top, den, *rest = refs[13 + n :]
    if last:
        outs, rest = rest[:owners], rest[owners:]
    order, src, keys, values = rest
    run_blocks(
        *shape, slots, count, b_src, b_dst, b_type, prior, tiles, wk, wv, att, msg,
        queries, acc, top, den, order, src, keys, values,
    )
    if last:
        for t in range(owners):
            total = den[t]
            some = total > 0.0
            safe = jnp.where(some, total, 1.0)
            lse = jnp.where(some, top[t] + jnp.log(safe) * LOG2E, EMPTY)
            inverse = 1.0 / safe
            for h in range(heads):
                rows = slice(h * head_dim, (h + 1) * head_dim)
                outs[t][rows, :] = (acc[t, rows, :] * inverse[h : h + 1, :]).astype(BF)
            parts = split3(lse)
            for k in range(3):
                base = heads * head_dim + k * heads
                outs[t][base : base + heads, :] = parts[k]


def combine(owners, heads, head_dim, *refs):
    parts, w_out, out, agg = refs[:owners], refs[owners], refs[owners + 1], refs[owners + 2]
    base = heads * head_dim
    lse = []
    for r in parts:
        hi, mid, lo = (r[base + k * heads : base + (k + 1) * heads, :].astype(F32) for k in range(3))
        lse.append((hi + mid) + lo)
    best = functools.reduce(jnp.maximum, lse)
    weights = [jnp.exp2(v - best) for v in lse]
    whole = functools.reduce(jnp.add, weights)
    weights = [w / whole for w in weights]
    for h in range(heads):
        rows = slice(h * head_dim, (h + 1) * head_dim)
        total = functools.reduce(
            jnp.add,
            [r[rows, :].astype(F32) * w[h : h + 1, :] for r, w in zip(parts, weights)],
        )
        agg[:, rows] = total.T.astype(BF)
    out[...] = jnp.dot(agg[...], w_out[...], preferred_element_type=F32).astype(BF)


def body(
    node_src,
    hub_feat,
    w_query,
    w_key,
    w_value,
    w_out,
    w_att,
    w_msg,
    relation_prior,
    block_src,
    block_dst,
    block_type,
    block_count,
):
    groups = lax.axis_size("grp")
    owners = lax.axis_size("dev")
    tile, width = hub_feat.shape
    relations, heads = relation_prior.shape
    head_dim = width // heads
    pair, pairs = 2 * head_dim, heads // 2
    quads = heads // 4
    length = block_src.shape[1]
    shape = (owners, heads, tile, head_dim)
    smem = pl.BlockSpec(memory_space=pltpu.SMEM)
    apart = lambda x: pltpu.with_memory_space_constraint(x, pltpu.HBM)
    keep = lambda x: pltpu.with_memory_space_constraint(x, pltpu.VMEM)
    w_out = keep(w_out)
    vmem = pl.BlockSpec(memory_space=pltpu.VMEM)

    def move(x, axis, size, k):
        return lax.ppermute(x, axis, [(i, i ^ k) for i in range(size)])

    hubs = {0: hub_feat}
    for k in range(2, owners):
        hubs[k] = move(hub_feat, "dev", owners, k)
    srcs = {0: node_src}
    if groups == 8:
        steps = [(0, 1), (2, 6), (3, 4), (7, 5)]
        swaps = {2: (4,)}
        for k in (1, 6):
            srcs[k] = move(node_src, "grp", groups, k)
    else:
        steps = [(k, k + 1) for k in range(0, groups, 2)]
        swaps = {}
        for k in range(1, groups):
            srcs[k] = move(node_src, "grp", groups, k)

    dense = (w_query, w_key, w_value, node_src, hub_feat)
    maps = [w.reshape(relations, pairs, pair, head_dim) for w in (w_att, w_msg)]
    chunks = 16
    att, msg, w_query, w_key, w_value, own_src, own_hub = pl.pallas_call(
        functools.partial(prepare, chunks),
        in_specs=[pl.BlockSpec(memory_space=pltpu.HBM)] * (2 + len(dense)),
        out_specs=[vmem] * (2 + len(dense)),
        out_shape=[pltpu.VMEM((relations, pairs, pair, pair), BF)] * 2
        + [pltpu.VMEM(x.shape, BF) for x in dense],
        scratch_shapes=[
            pltpu.VMEM((relations, pairs, pair, head_dim), BF),
            pltpu.VMEM((relations, pairs, pair, head_dim), BF),
            pltpu.SemaphoreType.DMA((2, chunks)),
            pltpu.SemaphoreType.DMA((len(dense),)),
        ],
        name="prepare",
        compiler_params=pltpu.CompilerParams(vmem_limit_bytes=LIMIT),
    )(*[apart(x) for x in (*maps, *dense)])
    hubs[1] = move(hub_feat, "dev", owners, 1)
    if groups == 8:
        source, hubs[1] = lax.optimization_barrier((node_src, hubs[1]))
        srcs[2] = move(source, "grp", groups, 2)
        srcs[4] = move(own_src, "grp", groups, 4)
        for k in (3, 7):
            srcs[k] = move(own_src, "grp", groups, k)
    srcs[0], hubs[0] = own_src, own_hub
    att, msg, w_query, w_key, w_value = (keep(x) for x in (att, msg, w_query, w_key, w_value))
    if groups == 8:
        srcs[6], hubs[2] = lax.optimization_barrier((srcs[6], hubs[2]))
    lists = (
        block_count,
        block_src,
        block_dst,
        block_type,
        relation_prior,
    )
    state = [
        pltpu.VMEM((owners, width, tile), F32),
        pltpu.VMEM((owners, heads, tile), F32),
        pltpu.VMEM((owners, heads, tile), F32),
    ]
    rows_out = width + 3 * heads
    sent = [pltpu.VMEM((rows_out, tile), BF)] * owners
    for i, slots in enumerate(steps):
        n = len(slots)
        if i in swaps:
            carry = list(carry)
            *held, carry[2] = lax.optimization_barrier((*[srcs[k] for k in swaps[i]], carry[2]))
            for k, tile_k in zip(swaps[i], held):
                srcs[k] = tile_k
                srcs[k + 1] = move(tile_k, "grp", groups, 1)
        scratch = [
            pltpu.SMEM((2, length + 2), jnp.int32),
            pltpu.VMEM((n * tile, width), BF),
            pltpu.VMEM((n, quads, tile, 2 * pair), BF),
            pltpu.VMEM((n, quads, 2 * pair, tile), BF),
        ]
        cost = pl.CostEstimate(flops=COST, bytes_accessed=1024, transcendentals=0)
        tiles = [keep(srcs[k]) for k in slots]
        if i == 0:
            queries, *carry = pl.pallas_call(
                functools.partial(first_phase, shape, slots),
                in_specs=[smem] * 5 + [vmem] * (n + 5 + owners),
                out_specs=[vmem] * 4,
                out_shape=[pltpu.VMEM((owners, width, tile), BF)] + state,
                scratch_shapes=scratch,
                cost_estimate=cost,
            compiler_params=pltpu.CompilerParams(vmem_limit_bytes=LIMIT),
                name="phase0",
            )(*lists, *tiles, w_key, w_value, att, msg, w_query, *[keep(hubs[k]) for k in range(owners)])
            continue
        last = i == len(steps) - 1
        base = 10 + n
        aliases = {base + k: k for k in range(3)}
        carry = pl.pallas_call(
            functools.partial(later_phase, shape, slots, last),
            in_specs=[smem] * 5 + [vmem] * (n + 8),
            out_specs=[vmem] * (3 + owners if last else 3),
            out_shape=state + sent if last else state,
            scratch_shapes=scratch,
            input_output_aliases=aliases,
            cost_estimate=cost,
            compiler_params=pltpu.CompilerParams(vmem_limit_bytes=LIMIT),
            name="phase%d" % i,
        )(*lists, *tiles, w_key, w_value, att, msg, queries, *carry)
    tiles = carry[3:]
    parts = [tiles[0]] + [move(tiles[k], "dev", owners, k) for k in range(1, owners)]
    return pl.pallas_call(
        functools.partial(combine, owners, heads, head_dim),
        out_shape=jax.ShapeDtypeStruct((tile, width), BF),
        scratch_shapes=[pltpu.VMEM((tile, width), BF)],
        compiler_params=pltpu.CompilerParams(vmem_limit_bytes=LIMIT),
        name="combine",
    )(*[keep(p) for p in parts], w_out)


def solution(mesh):
    rows = P(("grp", "dev"), None)
    placed = (rows, rows) + (P(),) * 7 + (rows,) * 3 + (P(("grp", "dev")),)
    return jax.shard_map(body, mesh=mesh, in_specs=placed, out_specs=rows, check_vma=False)
```

```python
import functools

import jax
import jax.numpy as jnp
from jax import lax
from jax.experimental import pallas as pl
from jax.experimental.pallas import tpu as pltpu
from jax.sharding import PartitionSpec as P

BF = jnp.bfloat16
F32 = jnp.float32
LOG2E = 1.4426950408889634
EMPTY = -1e30
BLOCKS = 2
LAGS = (4, 8, 12)
LIMIT = 16 << 20
COST = 10**6


def split3(x):
    hi = x.astype(BF)
    rest = x - hi.astype(F32)
    mid = rest.astype(BF)
    lo = (rest - mid.astype(F32)).astype(BF)
    return hi, mid, lo


def prepare(parts, att, msg, *refs):
    kinds, pairs, pair, head_dim = att.shape
    plain = (len(refs) - 6) // 2
    given, refs = refs[:plain], refs[plain:]
    att_out, msg_out, copies = refs[0], refs[1], refs[2 : 2 + plain]
    att_in, msg_in, sem, plain_sem = refs[2 + plain :]
    size = kinds // parts
    moves = []
    for k in range(parts):
        some = pl.ds(k * size, size)
        moves.append(pltpu.make_async_copy(att.at[some], att_in.at[some], sem.at[0, k]))
        moves.append(pltpu.make_async_copy(msg.at[some], msg_in.at[some], sem.at[1, k]))
    rest = [pltpu.make_async_copy(g, c, plain_sem.at[i]) for i, (g, c) in enumerate(zip(given, copies))]
    for m in moves + rest:
        m.start()
    row = lax.broadcasted_iota(jnp.int32, (pair, head_dim), 0)
    col = lax.broadcasted_iota(jnp.int32, (pair, head_dim), 1)
    twice = jnp.where((row & (head_dim - 1)) == col, 1.0, 0.0).astype(BF)
    r2 = lax.broadcasted_iota(jnp.int32, (pair, 2 * pair), 0)
    c2 = lax.broadcasted_iota(jnp.int32, (pair, 2 * pair), 1)
    same = (r2 < head_dim) == ((c2 & (pair - 1)) < head_dim)
    none = jnp.zeros((head_dim, head_dim), BF)
    for k in range(parts):
        moves[2 * k].wait()
        moves[2 * k + 1].wait()

        def one(i, _):
            r = k * size + i
            for h in range(pairs):
                upper = jnp.concatenate([att_in[r, h, :head_dim, :], none], axis=1)
                lower = jnp.concatenate([none, att_in[r, h, head_dim:, :]], axis=1)
                att_out[r, h] = jnp.concatenate([upper, lower], axis=0)
            for h in range(0, pairs, 2):
                both = msg_in[r, h : h + 2].reshape(2 * pair, head_dim)
                m = lax.dot_general(twice, both, (((1,), (1,)), ((), ())), preferred_element_type=F32)
                m = jnp.where(same, m, 0.0).astype(BF)
                msg_out[r, h] = m[:, :pair]
                msg_out[r, h + 1] = m[:, pair:]
            return 0

        lax.fori_loop(0, size, one, 0)
    for m in rest:
        m.wait()


def run_blocks(
    owners, heads, tile, head_dim, slots, count, b_src, b_dst, b_type, prior, tiles, wk, wv, att, msg,
    queries, acc, top, den, order, src, keys, values,
):
    width = heads * head_dim
    pair, quad = 2 * head_dim, 4 * head_dim
    quads = heads // 4
    for i, ref in enumerate(tiles):
        src[i * tile : (i + 1) * tile, :] = ref[...]
    for q in range(quads):
        cols = slice(q * quad, (q + 1) * quad)
        k = jnp.dot(src[...], wk[:, cols], preferred_element_type=F32)
        v = jnp.dot(src[...], wv[:, cols], preferred_element_type=F32)
        for i in range(len(slots)):
            rows = slice(i * tile, (i + 1) * tile)
            keys[i, q] = k[rows, :].astype(BF)
            values[i, q] = v[rows, :].T.astype(BF)

    my_grp, my_dev = lax.axis_index("grp"), lax.axis_index("dev")

    def pick(j, n):
        s = b_src[0, j] ^ my_grp
        which = jnp.int32(0)
        hit = (s == slots[0]) & (j < count[0])
        for i in range(1, len(slots)):
            here = s == slots[i]
            which = jnp.where(here, i, which)
            hit = hit | (here & (j < count[0]))
        order[0, n] = j
        order[1, n] = which
        return n + hit.astype(jnp.int32)

    total = lax.fori_loop(0, b_src.shape[1], pick, jnp.int32(0), unroll=8)
    lane = lax.broadcasted_iota(jnp.int32, (tile, pair), 1)
    left = lane < head_dim
    none = jnp.zeros((pair, pair), BF)

    def diag(w, r, q):
        upper = jnp.concatenate([w[r, 2 * q], none], axis=1)
        lower = jnp.concatenate([none, w[r, 2 * q + 1]], axis=1)
        return jnp.concatenate([upper, lower], axis=0)

    def some_blocks(c, _):
        blocks = []
        for u in range(BLOCKS):
            n = c * BLOCKS + u
            valid = n < total
            j = jnp.where(valid, order[0, n], 0)
            s = jnp.where(valid, order[1, n], 0)
            blocks.append((valid, s, b_dst[0, j] ^ my_dev, b_type[0, j]))

        def maps(u, q):
            _, s, _, r = blocks[u]
            key_rel = jnp.dot(keys[s, q], diag(att, r, q), preferred_element_type=F32).astype(BF)
            message = jnp.dot(diag(msg, r, q), values[s, q], preferred_element_type=F32).astype(BF)
            return key_rel, message

        def scores(u, h, key_rel):
            _, _, d, _ = blocks[u]
            k = key_rel[:, (h % 2) * pair : (h % 2 + 1) * pair]
            zero = jnp.zeros_like(k)
            both = jnp.concatenate([jnp.where(left, k, zero), jnp.where(left, zero, k)], axis=0)
            q = queries[d, h * pair : (h + 1) * pair, :]
            return jnp.dot(both, q, preferred_element_type=F32)

        def weigh(u, h, s):
            _, _, _, r = blocks[u]
            found = []
            for i in range(2):
                scale = prior[r, 2 * h + i] * (LOG2E / float(head_dim) ** 0.5)
                x = s[i * tile : (i + 1) * tile, :] * scale
                m = jnp.max(x, axis=0, keepdims=True)
                p = jnp.exp2(x - m)
                found.append((m, jnp.sum(p, axis=0, keepdims=True), p.astype(BF)))
            return found

        def gather(u, h, message, found):
            valid, _, d, _ = blocks[u]
            for i in range(2):
                row = (h % 2) * pair + i * head_dim
                m, total_w, p = found[i]
                part = jnp.dot(message[row : row + head_dim, :], p, preferred_element_type=F32)
                head = 2 * h + i
                one = slice(head, head + 1)
                rows = slice(head * head_dim, (head + 1) * head_dim)
                old = top[d, one, :]
                new = jnp.where(valid, jnp.maximum(old, m), old)
                keep = jnp.exp2(old - new)
                add = jnp.where(valid, jnp.exp2(m - new), 0.0)
                top[d, one, :] = new
                den[d, one, :] = den[d, one, :] * keep + total_w * add
                acc[d, rows, :] = acc[d, rows, :] * keep + part * add

        items = [(u, h) for u in range(BLOCKS) for h in range(heads // 2)]
        mapped, scored, weighed = {}, {}, {}
        a, b, d = LAGS
        for t in range(len(items) + d):
            if t < len(items) and items[t][1] % 2 == 0:
                u, h = items[t]
                mapped[u, h // 2] = maps(u, h // 2)
            if 0 <= t - a < len(items):
                u, h = items[t - a]
                scored[u, h] = scores(u, h, mapped[u, h // 2][0])
            if 0 <= t - b < len(items):
                u, h = items[t - b]
                weighed[u, h] = weigh(u, h, scored.pop((u, h)))
            if 0 <= t - d < len(items):
                u, h = items[t - d]
                gather(u, h, mapped[u, h // 2][1], weighed.pop((u, h)))
        return 0

    lax.fori_loop(0, (total + BLOCKS - 1) // BLOCKS, some_blocks, 0)


def first_phase(shape, slots, *refs):
    owners, heads, tile, head_dim = shape
    n = len(slots)
    count, b_src, b_dst, b_type, prior = refs[:5]
    tiles = refs[5 : 5 + n]
    wk, wv, att, msg, wq = refs[5 + n : 10 + n]
    hubs = refs[10 + n : 10 + n + owners]
    queries, acc, top, den, order, src, keys, values = refs[10 + n + owners :]
    quad = 4 * head_dim
    acc[...] = jnp.zeros(acc.shape, F32)
    top[...] = jnp.full(top.shape, EMPTY, F32)
    den[...] = jnp.zeros(den.shape, F32)
    for lo in range(0, owners, n):
        some = range(lo, min(lo + n, owners))
        for i, t in enumerate(some):
            src[i * tile : (i + 1) * tile, :] = hubs[t][...]
        for c in range(0, heads * head_dim, quad):
            q = jnp.dot(src[...], wq[:, c : c + quad], preferred_element_type=F32)
            for i, t in enumerate(some):
                queries[t, c : c + quad, :] = q[i * tile : (i + 1) * tile, :].T.astype(BF)
    run_blocks(
        *shape, slots, count, b_src, b_dst, b_type, prior, tiles, wk, wv, att, msg,
        queries, acc, top, den, order, src, keys, values,
    )


def later_phase(shape, slots, last, *refs):
    owners, heads, tile, head_dim = shape
    n = len(slots)
    count, b_src, b_dst, b_type, prior = refs[:5]
    tiles = refs[5 : 5 + n]
    wk, wv, att, msg, queries = refs[5 + n : 10 + n]
    acc, top, den, *rest = refs[13 + n :]
    if last:
        outs, rest = rest[:owners], rest[owners:]
    order, src, keys, values = rest
    run_blocks(
        *shape, slots, count, b_src, b_dst, b_type, prior, tiles, wk, wv, att, msg,
        queries, acc, top, den, order, src, keys, values,
    )
    if last:
        for t in range(owners):
            total = den[t]
            some = total > 0.0
            safe = jnp.where(some, total, 1.0)
            lse = jnp.where(some, top[t] + jnp.log(safe) * LOG2E, EMPTY)
            inverse = 1.0 / safe
            for h in range(heads):
                rows = slice(h * head_dim, (h + 1) * head_dim)
                outs[t][rows, :] = (acc[t, rows, :] * inverse[h : h + 1, :]).astype(BF)
            parts = split3(lse)
            for k in range(3):
                base = heads * head_dim + k * heads
                outs[t][base : base + heads, :] = parts[k]


def combine(owners, heads, head_dim, *refs):
    parts, w_out, out, agg = refs[:owners], refs[owners], refs[owners + 1], refs[owners + 2]
    base = heads * head_dim
    lse = []
    for r in parts:
        hi, mid, lo = (r[base + k * heads : base + (k + 1) * heads, :].astype(F32) for k in range(3))
        lse.append((hi + mid) + lo)
    best = functools.reduce(jnp.maximum, lse)
    weights = [jnp.exp2(v - best) for v in lse]
    whole = functools.reduce(jnp.add, weights)
    weights = [w / whole for w in weights]
    for h in range(heads):
        rows = slice(h * head_dim, (h + 1) * head_dim)
        total = functools.reduce(
            jnp.add,
            [r[rows, :].astype(F32) * w[h : h + 1, :] for r, w in zip(parts, weights)],
        )
        agg[:, rows] = total.T.astype(BF)
    out[...] = jnp.dot(agg[...], w_out[...], preferred_element_type=F32).astype(BF)


def body(
    node_src,
    hub_feat,
    w_query,
    w_key,
    w_value,
    w_out,
    w_att,
    w_msg,
    relation_prior,
    block_src,
    block_dst,
    block_type,
    block_count,
):
    groups = lax.axis_size("grp")
    owners = lax.axis_size("dev")
    tile, width = hub_feat.shape
    relations, heads = relation_prior.shape
    head_dim = width // heads
    pair, pairs = 2 * head_dim, heads // 2
    quads = heads // 4
    length = block_src.shape[1]
    shape = (owners, heads, tile, head_dim)
    smem = pl.BlockSpec(memory_space=pltpu.SMEM)
    apart = lambda x: pltpu.with_memory_space_constraint(x, pltpu.HBM)
    keep = lambda x: pltpu.with_memory_space_constraint(x, pltpu.VMEM)
    w_out = keep(w_out)
    vmem = pl.BlockSpec(memory_space=pltpu.VMEM)

    def move(x, axis, size, k):
        return lax.ppermute(x, axis, [(i, i ^ k) for i in range(size)])

    hubs = {0: hub_feat}
    for k in range(2, owners):
        hubs[k] = move(hub_feat, "dev", owners, k)
    srcs = {0: node_src}
    if groups == 8:
        steps = [(0, 1), (2, 6), (3, 4), (7,), (5,)]
        swaps = {2: (4,)}
        for k in (1, 6):
            srcs[k] = move(node_src, "grp", groups, k)
    else:
        steps = [(k, k + 1) for k in range(0, groups, 2)]
        swaps = {}
        for k in range(1, groups):
            srcs[k] = move(node_src, "grp", groups, k)

    dense = (w_query, w_key, w_value, node_src, hub_feat)
    maps = [w.reshape(relations, pairs, pair, head_dim) for w in (w_att, w_msg)]
    chunks = 16
    att, msg, w_query, w_key, w_value, own_src, own_hub = pl.pallas_call(
        functools.partial(prepare, chunks),
        in_specs=[pl.BlockSpec(memory_space=pltpu.HBM)] * (2 + len(dense)),
        out_specs=[vmem] * (2 + len(dense)),
        out_shape=[pltpu.VMEM((relations, pairs, pair, pair), BF)] * 2
        + [pltpu.VMEM(x.shape, BF) for x in dense],
        scratch_shapes=[
            pltpu.VMEM((relations, pairs, pair, head_dim), BF),
            pltpu.VMEM((relations, pairs, pair, head_dim), BF),
            pltpu.SemaphoreType.DMA((2, chunks)),
            pltpu.SemaphoreType.DMA((len(dense),)),
        ],
        name="prepare",
        compiler_params=pltpu.CompilerParams(vmem_limit_bytes=LIMIT),
    )(*[apart(x) for x in (*maps, *dense)])
    hubs[1] = move(hub_feat, "dev", owners, 1)
    if groups == 8:
        source, hubs[1] = lax.optimization_barrier((node_src, hubs[1]))
        srcs[2] = move(source, "grp", groups, 2)
        srcs[4] = move(own_src, "grp", groups, 4)
        for k in (3, 7):
            srcs[k] = move(own_src, "grp", groups, k)
    srcs[0], hubs[0] = own_src, own_hub
    att, msg, w_query, w_key, w_value = (keep(x) for x in (att, msg, w_query, w_key, w_value))
    lists = (
        block_count,
        block_src,
        block_dst,
        block_type,
        relation_prior,
    )
    state = [
        pltpu.VMEM((owners, width, tile), F32),
        pltpu.VMEM((owners, heads, tile), F32),
        pltpu.VMEM((owners, heads, tile), F32),
    ]
    rows_out = width + 3 * heads
    sent = [pltpu.VMEM((rows_out, tile), BF)] * owners
    for i, slots in enumerate(steps):
        n = len(slots)
        if i in swaps:
            carry = list(carry)
            *held, carry[2] = lax.optimization_barrier((*[srcs[k] for k in swaps[i]], carry[2]))
            for k, tile_k in zip(swaps[i], held):
                srcs[k] = tile_k
                srcs[k + 1] = move(tile_k, "grp", groups, 1)
        scratch = [
            pltpu.SMEM((2, length + 2), jnp.int32),
            pltpu.VMEM((n * tile, width), BF),
            pltpu.VMEM((n, quads, tile, 2 * pair), BF),
            pltpu.VMEM((n, quads, 2 * pair, tile), BF),
        ]
        cost = pl.CostEstimate(flops=COST, bytes_accessed=1024, transcendentals=0)
        tiles = [keep(srcs[k]) for k in slots]
        if i == 0:
            queries, *carry = pl.pallas_call(
                functools.partial(first_phase, shape, slots),
                in_specs=[smem] * 5 + [vmem] * (n + 5 + owners),
                out_specs=[vmem] * 4,
                out_shape=[pltpu.VMEM((owners, width, tile), BF)] + state,
                scratch_shapes=scratch,
                cost_estimate=cost,
            compiler_params=pltpu.CompilerParams(vmem_limit_bytes=LIMIT),
                name="phase0",
            )(*lists, *tiles, w_key, w_value, att, msg, w_query, *[keep(hubs[k]) for k in range(owners)])
            continue
        last = i == len(steps) - 1
        base = 10 + n
        aliases = {base + k: k for k in range(3)}
        carry = pl.pallas_call(
            functools.partial(later_phase, shape, slots, last),
            in_specs=[smem] * 5 + [vmem] * (n + 8),
            out_specs=[vmem] * (3 + owners if last else 3),
            out_shape=state + sent if last else state,
            scratch_shapes=scratch,
            input_output_aliases=aliases,
            cost_estimate=cost,
            compiler_params=pltpu.CompilerParams(vmem_limit_bytes=LIMIT),
            name="phase%d" % i,
        )(*lists, *tiles, w_key, w_value, att, msg, queries, *carry)
    tiles = carry[3:]
    parts = [tiles[0]] + [move(tiles[k], "dev", owners, k) for k in range(1, owners)]
    return pl.pallas_call(
        functools.partial(combine, owners, heads, head_dim),
        out_shape=jax.ShapeDtypeStruct((tile, width), BF),
        scratch_shapes=[pltpu.VMEM((tile, width), BF)],
        compiler_params=pltpu.CompilerParams(vmem_limit_bytes=LIMIT),
        name="combine",
    )(*[keep(p) for p in parts], w_out)


def solution(mesh):
    rows = P(("grp", "dev"), None)
    placed = (rows, rows) + (P(),) * 7 + (rows,) * 3 + (P(("grp", "dev")),)
    return jax.shard_map(body, mesh=mesh, in_specs=placed, out_specs=rows, check_vma=False)
```

```python
import functools

import jax
import jax.numpy as jnp
from jax import lax
from jax.experimental import pallas as pl
from jax.experimental.pallas import tpu as pltpu
from jax.sharding import PartitionSpec as P

BF = jnp.bfloat16
F32 = jnp.float32
LOG2E = 1.4426950408889634
EMPTY = -1e30
BLOCKS = 4
LAGS = (4, 8, 12)
LIMIT = 16 << 20
COST = 10**6


def split3(x):
    hi = x.astype(BF)
    rest = x - hi.astype(F32)
    mid = rest.astype(BF)
    lo = (rest - mid.astype(F32)).astype(BF)
    return hi, mid, lo


def prepare(parts, att, msg, *refs):
    kinds, pairs, pair, head_dim = att.shape
    plain = (len(refs) - 6) // 2
    given, refs = refs[:plain], refs[plain:]
    att_out, msg_out, copies = refs[0], refs[1], refs[2 : 2 + plain]
    att_in, msg_in, sem, plain_sem = refs[2 + plain :]
    size = kinds // parts
    moves = []
    for k in range(parts):
        some = pl.ds(k * size, size)
        moves.append(pltpu.make_async_copy(att.at[some], att_in.at[some], sem.at[0, k]))
        moves.append(pltpu.make_async_copy(msg.at[some], msg_in.at[some], sem.at[1, k]))
    rest = [pltpu.make_async_copy(g, c, plain_sem.at[i]) for i, (g, c) in enumerate(zip(given, copies))]
    for m in moves + rest:
        m.start()
    row = lax.broadcasted_iota(jnp.int32, (pair, head_dim), 0)
    col = lax.broadcasted_iota(jnp.int32, (pair, head_dim), 1)
    twice = jnp.where((row & (head_dim - 1)) == col, 1.0, 0.0).astype(BF)
    r2 = lax.broadcasted_iota(jnp.int32, (pair, 2 * pair), 0)
    c2 = lax.broadcasted_iota(jnp.int32, (pair, 2 * pair), 1)
    same = (r2 < head_dim) == ((c2 & (pair - 1)) < head_dim)
    none = jnp.zeros((head_dim, head_dim), BF)
    for k in range(parts):
        moves[2 * k].wait()
        moves[2 * k + 1].wait()

        def one(i, _):
            r = k * size + i
            for h in range(pairs):
                upper = jnp.concatenate([att_in[r, h, :head_dim, :], none], axis=1)
                lower = jnp.concatenate([none, att_in[r, h, head_dim:, :]], axis=1)
                att_out[r, h] = jnp.concatenate([upper, lower], axis=0)
            for h in range(0, pairs, 2):
                both = msg_in[r, h : h + 2].reshape(2 * pair, head_dim)
                m = lax.dot_general(twice, both, (((1,), (1,)), ((), ())), preferred_element_type=F32)
                m = jnp.where(same, m, 0.0).astype(BF)
                msg_out[r, h] = m[:, :pair]
                msg_out[r, h + 1] = m[:, pair:]
            return 0

        lax.fori_loop(0, size, one, 0)
    for m in rest:
        m.wait()


def run_blocks(
    owners, heads, tile, head_dim, slots, count, b_src, b_dst, b_type, prior, tiles, wk, wv, att, msg,
    queries, acc, top, den, order, src, keys, values,
):
    width = heads * head_dim
    pair, quad = 2 * head_dim, 4 * head_dim
    quads = heads // 4
    for i, ref in enumerate(tiles):
        src[i * tile : (i + 1) * tile, :] = ref[...]
    for q in range(quads):
        cols = slice(q * quad, (q + 1) * quad)
        k = jnp.dot(src[...], wk[:, cols], preferred_element_type=F32)
        v = jnp.dot(src[...], wv[:, cols], preferred_element_type=F32)
        for i in range(len(slots)):
            rows = slice(i * tile, (i + 1) * tile)
            keys[i, q] = k[rows, :].astype(BF)
            values[i, q] = v[rows, :].T.astype(BF)

    my_grp, my_dev = lax.axis_index("grp"), lax.axis_index("dev")

    def pick(j, n):
        s = b_src[0, j] ^ my_grp
        which = jnp.int32(0)
        hit = (s == slots[0]) & (j < count[0])
        for i in range(1, len(slots)):
            here = s == slots[i]
            which = jnp.where(here, i, which)
            hit = hit | (here & (j < count[0]))
        order[0, n] = j
        order[1, n] = which
        return n + hit.astype(jnp.int32)

    total = lax.fori_loop(0, b_src.shape[1], pick, jnp.int32(0), unroll=8)
    lane = lax.broadcasted_iota(jnp.int32, (tile, pair), 1)
    left = lane < head_dim
    none = jnp.zeros((pair, pair), BF)

    def diag(w, r, q):
        upper = jnp.concatenate([w[r, 2 * q], none], axis=1)
        lower = jnp.concatenate([none, w[r, 2 * q + 1]], axis=1)
        return jnp.concatenate([upper, lower], axis=0)

    def some_blocks(size, start, c, _):
        blocks = []
        for u in range(size):
            n = start + c * size + u
            valid = n < total
            j = jnp.where(valid, order[0, n], 0)
            s = jnp.where(valid, order[1, n], 0)
            blocks.append((valid, s, b_dst[0, j] ^ my_dev, b_type[0, j]))

        def maps(u, q):
            _, s, _, r = blocks[u]
            key_rel = jnp.dot(keys[s, q], diag(att, r, q), preferred_element_type=F32).astype(BF)
            message = jnp.dot(diag(msg, r, q), values[s, q], preferred_element_type=F32).astype(BF)
            return key_rel, message

        def scores(u, h, key_rel):
            _, _, d, _ = blocks[u]
            k = key_rel[:, (h % 2) * pair : (h % 2 + 1) * pair]
            zero = jnp.zeros_like(k)
            both = jnp.concatenate([jnp.where(left, k, zero), jnp.where(left, zero, k)], axis=0)
            q = queries[d, h * pair : (h + 1) * pair, :]
            return jnp.dot(both, q, preferred_element_type=F32)

        def weigh(u, h, s):
            _, _, _, r = blocks[u]
            found = []
            for i in range(2):
                scale = prior[r, 2 * h + i] * (LOG2E / float(head_dim) ** 0.5)
                x = s[i * tile : (i + 1) * tile, :] * scale
                m = jnp.max(x, axis=0, keepdims=True)
                p = jnp.exp2(x - m)
                found.append((m, jnp.sum(p, axis=0, keepdims=True), p.astype(BF)))
            return found

        def gather(u, h, message, found):
            valid, _, d, _ = blocks[u]
            for i in range(2):
                row = (h % 2) * pair + i * head_dim
                m, total_w, p = found[i]
                part = jnp.dot(message[row : row + head_dim, :], p, preferred_element_type=F32)
                head = 2 * h + i
                one = slice(head, head + 1)
                rows = slice(head * head_dim, (head + 1) * head_dim)
                old = top[d, one, :]
                new = jnp.where(valid, jnp.maximum(old, m), old)
                keep = jnp.exp2(old - new)
                add = jnp.where(valid, jnp.exp2(m - new), 0.0)
                top[d, one, :] = new
                den[d, one, :] = den[d, one, :] * keep + total_w * add
                acc[d, rows, :] = acc[d, rows, :] * keep + part * add

        items = [(u, h) for u in range(size) for h in range(heads // 2)]
        mapped, scored, weighed = {}, {}, {}
        a, b, d = LAGS
        for t in range(len(items) + d):
            if t < len(items) and items[t][1] % 2 == 0:
                u, h = items[t]
                mapped[u, h // 2] = maps(u, h // 2)
            if 0 <= t - a < len(items):
                u, h = items[t - a]
                scored[u, h] = scores(u, h, mapped[u, h // 2][0])
            if 0 <= t - b < len(items):
                u, h = items[t - b]
                weighed[u, h] = weigh(u, h, scored.pop((u, h)))
            if 0 <= t - d < len(items):
                u, h = items[t - d]
                gather(u, h, mapped[u, h // 2][1], weighed.pop((u, h)))
        return 0

    half = BLOCKS // 2
    full = (total + half - 1) // BLOCKS
    done = full * BLOCKS
    lax.fori_loop(0, full, functools.partial(some_blocks, BLOCKS, 0), 0)
    lax.fori_loop(0, (total > done).astype(jnp.int32), functools.partial(some_blocks, half, done), 0)


def first_phase(shape, slots, *refs):
    owners, heads, tile, head_dim = shape
    n = len(slots)
    count, b_src, b_dst, b_type, prior = refs[:5]
    tiles = refs[5 : 5 + n]
    wk, wv, att, msg, wq = refs[5 + n : 10 + n]
    hubs = refs[10 + n : 10 + n + owners]
    queries, acc, top, den, order, src, keys, values = refs[10 + n + owners :]
    quad = 4 * head_dim
    acc[...] = jnp.zeros(acc.shape, F32)
    top[...] = jnp.full(top.shape, EMPTY, F32)
    den[...] = jnp.zeros(den.shape, F32)
    for lo in range(0, owners, n):
        some = range(lo, min(lo + n, owners))
        for i, t in enumerate(some):
            src[i * tile : (i + 1) * tile, :] = hubs[t][...]
        for c in range(0, heads * head_dim, quad):
            q = jnp.dot(src[...], wq[:, c : c + quad], preferred_element_type=F32)
            for i, t in enumerate(some):
                queries[t, c : c + quad, :] = q[i * tile : (i + 1) * tile, :].T.astype(BF)
    run_blocks(
        *shape, slots, count, b_src, b_dst, b_type, prior, tiles, wk, wv, att, msg,
        queries, acc, top, den, order, src, keys, values,
    )


def later_phase(shape, slots, last, *refs):
    owners, heads, tile, head_dim = shape
    n = len(slots)
    count, b_src, b_dst, b_type, prior = refs[:5]
    tiles = refs[5 : 5 + n]
    wk, wv, att, msg, queries = refs[5 + n : 10 + n]
    acc, top, den, *rest = refs[13 + n :]
    if last:
        outs, rest = rest[:owners], rest[owners:]
    order, src, keys, values = rest
    run_blocks(
        *shape, slots, count, b_src, b_dst, b_type, prior, tiles, wk, wv, att, msg,
        queries, acc, top, den, order, src, keys, values,
    )
    if last:
        for t in range(owners):
            total = den[t]
            some = total > 0.0
            safe = jnp.where(some, total, 1.0)
            lse = jnp.where(some, top[t] + jnp.log(safe) * LOG2E, EMPTY)
            inverse = 1.0 / safe
            for h in range(heads):
                rows = slice(h * head_dim, (h + 1) * head_dim)
                outs[t][rows, :] = (acc[t, rows, :] * inverse[h : h + 1, :]).astype(BF)
            parts = split3(lse)
            for k in range(3):
                base = heads * head_dim + k * heads
                outs[t][base : base + heads, :] = parts[k]


def combine(owners, heads, head_dim, *refs):
    parts, w_out, out, agg = refs[:owners], refs[owners], refs[owners + 1], refs[owners + 2]
    base = heads * head_dim
    lse = []
    for r in parts:
        hi, mid, lo = (r[base + k * heads : base + (k + 1) * heads, :].astype(F32) for k in range(3))
        lse.append((hi + mid) + lo)
    best = functools.reduce(jnp.maximum, lse)
    weights = [jnp.exp2(v - best) for v in lse]
    whole = functools.reduce(jnp.add, weights)
    weights = [w / whole for w in weights]
    for h in range(heads):
        rows = slice(h * head_dim, (h + 1) * head_dim)
        total = functools.reduce(
            jnp.add,
            [r[rows, :].astype(F32) * w[h : h + 1, :] for r, w in zip(parts, weights)],
        )
        agg[:, rows] = total.T.astype(BF)
    out[...] = jnp.dot(agg[...], w_out[...], preferred_element_type=F32).astype(BF)


def body(
    node_src,
    hub_feat,
    w_query,
    w_key,
    w_value,
    w_out,
    w_att,
    w_msg,
    relation_prior,
    block_src,
    block_dst,
    block_type,
    block_count,
):
    groups = lax.axis_size("grp")
    owners = lax.axis_size("dev")
    tile, width = hub_feat.shape
    relations, heads = relation_prior.shape
    head_dim = width // heads
    pair, pairs = 2 * head_dim, heads // 2
    quads = heads // 4
    length = block_src.shape[1]
    shape = (owners, heads, tile, head_dim)
    smem = pl.BlockSpec(memory_space=pltpu.SMEM)
    apart = lambda x: pltpu.with_memory_space_constraint(x, pltpu.HBM)
    keep = lambda x: pltpu.with_memory_space_constraint(x, pltpu.VMEM)
    w_out = keep(w_out)
    vmem = pl.BlockSpec(memory_space=pltpu.VMEM)

    def move(x, axis, size, k):
        return lax.ppermute(x, axis, [(i, i ^ k) for i in range(size)])

    hubs = {0: hub_feat}
    for k in range(2, owners):
        hubs[k] = move(hub_feat, "dev", owners, k)
    srcs = {0: node_src}
    if groups == 8:
        steps = [(0, 1), (2, 6), (3, 4), (7,), (5,)]
        swaps = {2: (4,)}
        for k in (1, 6):
            srcs[k] = move(node_src, "grp", groups, k)
    else:
        steps = [(k, k + 1) for k in range(0, groups, 2)]
        swaps = {}
        for k in range(1, groups):
            srcs[k] = move(node_src, "grp", groups, k)

    dense = (w_query, w_key, w_value, node_src, hub_feat)
    maps = [w.reshape(relations, pairs, pair, head_dim) for w in (w_att, w_msg)]
    chunks = 16
    att, msg, w_query, w_key, w_value, own_src, own_hub = pl.pallas_call(
        functools.partial(prepare, chunks),
        in_specs=[pl.BlockSpec(memory_space=pltpu.HBM)] * (2 + len(dense)),
        out_specs=[vmem] * (2 + len(dense)),
        out_shape=[pltpu.VMEM((relations, pairs, pair, pair), BF)] * 2
        + [pltpu.VMEM(x.shape, BF) for x in dense],
        scratch_shapes=[
            pltpu.VMEM((relations, pairs, pair, head_dim), BF),
            pltpu.VMEM((relations, pairs, pair, head_dim), BF),
            pltpu.SemaphoreType.DMA((2, chunks)),
            pltpu.SemaphoreType.DMA((len(dense),)),
        ],
        name="prepare",
        compiler_params=pltpu.CompilerParams(vmem_limit_bytes=LIMIT),
    )(*[apart(x) for x in (*maps, *dense)])
    hubs[1] = move(hub_feat, "dev", owners, 1)
    if groups == 8:
        source, hubs[1] = lax.optimization_barrier((node_src, hubs[1]))
        srcs[2] = move(source, "grp", groups, 2)
        srcs[4] = move(own_src, "grp", groups, 4)
        for k in (3, 7):
            srcs[k] = move(own_src, "grp", groups, k)
    srcs[0], hubs[0] = own_src, own_hub
    att, msg, w_query, w_key, w_value = (keep(x) for x in (att, msg, w_query, w_key, w_value))
    lists = (
        block_count,
        block_src,
        block_dst,
        block_type,
        relation_prior,
    )
    state = [
        pltpu.VMEM((owners, width, tile), F32),
        pltpu.VMEM((owners, heads, tile), F32),
        pltpu.VMEM((owners, heads, tile), F32),
    ]
    rows_out = width + 3 * heads
    sent = [pltpu.VMEM((rows_out, tile), BF)] * owners
    for i, slots in enumerate(steps):
        n = len(slots)
        if i in swaps:
            carry = list(carry)
            *held, carry[2] = lax.optimization_barrier((*[srcs[k] for k in swaps[i]], carry[2]))
            for k, tile_k in zip(swaps[i], held):
                srcs[k] = tile_k
                srcs[k + 1] = move(tile_k, "grp", groups, 1)
        scratch = [
            pltpu.SMEM((2, length + BLOCKS), jnp.int32),
            pltpu.VMEM((n * tile, width), BF),
            pltpu.VMEM((n, quads, tile, 2 * pair), BF),
            pltpu.VMEM((n, quads, 2 * pair, tile), BF),
        ]
        cost = pl.CostEstimate(flops=COST, bytes_accessed=1024, transcendentals=0)
        tiles = [keep(srcs[k]) for k in slots]
        if i == 0:
            queries, *carry = pl.pallas_call(
                functools.partial(first_phase, shape, slots),
                in_specs=[smem] * 5 + [vmem] * (n + 5 + owners),
                out_specs=[vmem] * 4,
                out_shape=[pltpu.VMEM((owners, width, tile), BF)] + state,
                scratch_shapes=scratch,
                cost_estimate=cost,
            compiler_params=pltpu.CompilerParams(vmem_limit_bytes=LIMIT),
                name="phase0",
            )(*lists, *tiles, w_key, w_value, att, msg, w_query, *[keep(hubs[k]) for k in range(owners)])
            continue
        last = i == len(steps) - 1
        base = 10 + n
        aliases = {base + k: k for k in range(3)}
        carry = pl.pallas_call(
            functools.partial(later_phase, shape, slots, last),
            in_specs=[smem] * 5 + [vmem] * (n + 8),
            out_specs=[vmem] * (3 + owners if last else 3),
            out_shape=state + sent if last else state,
            scratch_shapes=scratch,
            input_output_aliases=aliases,
            cost_estimate=cost,
            compiler_params=pltpu.CompilerParams(vmem_limit_bytes=LIMIT),
            name="phase%d" % i,
        )(*lists, *tiles, w_key, w_value, att, msg, queries, *carry)
    tiles = carry[3:]
    parts = [tiles[0]] + [move(tiles[k], "dev", owners, k) for k in range(1, owners)]
    return pl.pallas_call(
        functools.partial(combine, owners, heads, head_dim),
        out_shape=jax.ShapeDtypeStruct((tile, width), BF),
        scratch_shapes=[pltpu.VMEM((tile, width), BF)],
        compiler_params=pltpu.CompilerParams(vmem_limit_bytes=LIMIT),
        name="combine",
    )(*[keep(p) for p in parts], w_out)


def solution(mesh):
    rows = P(("grp", "dev"), None)
    placed = (rows, rows) + (P(),) * 7 + (rows,) * 3 + (P(("grp", "dev")),)
    return jax.shard_map(body, mesh=mesh, in_specs=placed, out_specs=rows, check_vma=False)
```

```python
import functools

import jax
import jax.numpy as jnp
from jax import lax
from jax.experimental import pallas as pl
from jax.experimental.pallas import tpu as pltpu
from jax.sharding import PartitionSpec as P

BF = jnp.bfloat16
F32 = jnp.float32
LOG2E = 1.4426950408889634
EMPTY = -1e30
BLOCKS = 4
LAGS = (4, 8, 12)
LIMIT = 16 << 20
COST = 10**6


def split3(x):
    hi = x.astype(BF)
    rest = x - hi.astype(F32)
    mid = rest.astype(BF)
    lo = (rest - mid.astype(F32)).astype(BF)
    return hi, mid, lo


def prepare(parts, att, msg, *refs):
    kinds, pairs, pair, head_dim = att.shape
    plain = (len(refs) - 6) // 2
    given, refs = refs[:plain], refs[plain:]
    att_out, msg_out, copies = refs[0], refs[1], refs[2 : 2 + plain]
    att_in, msg_in, sem, plain_sem = refs[2 + plain :]
    size = kinds // parts
    moves = []
    for k in range(parts):
        some = pl.ds(k * size, size)
        moves.append(pltpu.make_async_copy(att.at[some], att_in.at[some], sem.at[0, k]))
        moves.append(pltpu.make_async_copy(msg.at[some], msg_in.at[some], sem.at[1, k]))
    rest = [pltpu.make_async_copy(g, c, plain_sem.at[i]) for i, (g, c) in enumerate(zip(given, copies))]
    for m in moves + rest:
        m.start()
    row = lax.broadcasted_iota(jnp.int32, (pair, head_dim), 0)
    col = lax.broadcasted_iota(jnp.int32, (pair, head_dim), 1)
    twice = jnp.where((row & (head_dim - 1)) == col, 1.0, 0.0).astype(BF)
    r2 = lax.broadcasted_iota(jnp.int32, (pair, 2 * pair), 0)
    c2 = lax.broadcasted_iota(jnp.int32, (pair, 2 * pair), 1)
    same = (r2 < head_dim) == ((c2 & (pair - 1)) < head_dim)
    none = jnp.zeros((head_dim, head_dim), BF)
    for k in range(parts):
        moves[2 * k].wait()
        moves[2 * k + 1].wait()

        def one(i, _):
            r = k * size + i
            for h in range(pairs):
                upper = jnp.concatenate([att_in[r, h, :head_dim, :], none], axis=1)
                lower = jnp.concatenate([none, att_in[r, h, head_dim:, :]], axis=1)
                att_out[r, h] = jnp.concatenate([upper, lower], axis=0)
            for h in range(0, pairs, 2):
                both = msg_in[r, h : h + 2].reshape(2 * pair, head_dim)
                m = lax.dot_general(twice, both, (((1,), (1,)), ((), ())), preferred_element_type=F32)
                m = jnp.where(same, m, 0.0).astype(BF)
                msg_out[r, h] = m[:, :pair]
                msg_out[r, h + 1] = m[:, pair:]
            return 0

        lax.fori_loop(0, size, one, 0)
    for m in rest:
        m.wait()


def run_blocks(
    owners, heads, tile, head_dim, slots, count, b_src, b_dst, b_type, prior, tiles, wk, wv, att, msg,
    queries, acc, top, den, order, src, keys, values,
):
    width = heads * head_dim
    pair, quad = 2 * head_dim, 4 * head_dim
    quads = heads // 4
    for i, ref in enumerate(tiles):
        src[i * tile : (i + 1) * tile, :] = ref[...]
    for q in range(quads):
        cols = slice(q * quad, (q + 1) * quad)
        k = jnp.dot(src[...], wk[:, cols], preferred_element_type=F32)
        v = jnp.dot(src[...], wv[:, cols], preferred_element_type=F32)
        for i in range(len(slots)):
            rows = slice(i * tile, (i + 1) * tile)
            keys[i, q] = k[rows, :].astype(BF)
            values[i, q] = v[rows, :].T.astype(BF)

    my_grp, my_dev = lax.axis_index("grp"), lax.axis_index("dev")

    def pick(j, n):
        s = b_src[0, j] ^ my_grp
        which = jnp.int32(0)
        hit = (s == slots[0]) & (j < count[0])
        for i in range(1, len(slots)):
            here = s == slots[i]
            which = jnp.where(here, i, which)
            hit = hit | (here & (j < count[0]))
        order[0, n] = j
        order[1, n] = which
        return n + hit.astype(jnp.int32)

    total = lax.fori_loop(0, b_src.shape[1], pick, jnp.int32(0), unroll=8)
    lane = lax.broadcasted_iota(jnp.int32, (tile, pair), 1)
    left = lane < head_dim
    none = jnp.zeros((pair, pair), BF)

    def diag(w, r, q):
        upper = jnp.concatenate([w[r, 2 * q], none], axis=1)
        lower = jnp.concatenate([none, w[r, 2 * q + 1]], axis=1)
        return jnp.concatenate([upper, lower], axis=0)

    def some_blocks(size, start, c, _):
        blocks = []
        for u in range(size):
            n = start + c * size + u
            valid = n < total
            j = jnp.where(valid, order[0, n], 0)
            s = jnp.where(valid, order[1, n], 0)
            blocks.append((valid, s, b_dst[0, j] ^ my_dev, b_type[0, j]))

        def maps(u, q):
            _, s, _, r = blocks[u]
            key_rel = jnp.dot(keys[s, q], diag(att, r, q), preferred_element_type=F32).astype(BF)
            message = jnp.dot(diag(msg, r, q), values[s, q], preferred_element_type=F32).astype(BF)
            return key_rel, message

        def scores(u, h, key_rel):
            _, _, d, _ = blocks[u]
            k = key_rel[:, (h % 2) * pair : (h % 2 + 1) * pair]
            zero = jnp.zeros_like(k)
            both = jnp.concatenate([jnp.where(left, k, zero), jnp.where(left, zero, k)], axis=0)
            q = queries[d, h * pair : (h + 1) * pair, :]
            return jnp.dot(both, q, preferred_element_type=F32)

        def weigh(u, h, s):
            _, _, _, r = blocks[u]
            found = []
            for i in range(2):
                scale = prior[r, 2 * h + i] * (LOG2E / float(head_dim) ** 0.5)
                x = s[i * tile : (i + 1) * tile, :] * scale
                m = jnp.max(x, axis=0, keepdims=True)
                p = jnp.exp2(x - m)
                found.append((m, jnp.sum(p, axis=0, keepdims=True), p.astype(BF)))
            return found

        def gather(u, h, message, found):
            valid, _, d, _ = blocks[u]
            for i in range(2):
                row = (h % 2) * pair + i * head_dim
                m, total_w, p = found[i]
                part = jnp.dot(message[row : row + head_dim, :], p, preferred_element_type=F32)
                head = 2 * h + i
                one = slice(head, head + 1)
                rows = slice(head * head_dim, (head + 1) * head_dim)
                old = top[d, one, :]
                new = jnp.where(valid, jnp.maximum(old, m), old)
                keep = jnp.exp2(old - new)
                add = jnp.where(valid, jnp.exp2(m - new), 0.0)
                top[d, one, :] = new
                den[d, one, :] = den[d, one, :] * keep + total_w * add
                acc[d, rows, :] = acc[d, rows, :] * keep + part * add

        items = [(u, h) for u in range(size) for h in range(heads // 2)]
        mapped, scored, weighed = {}, {}, {}
        a, b, d = LAGS
        for t in range(len(items) + d):
            if t < len(items) and items[t][1] % 2 == 0:
                u, h = items[t]
                mapped[u, h // 2] = maps(u, h // 2)
            if 0 <= t - a < len(items):
                u, h = items[t - a]
                scored[u, h] = scores(u, h, mapped[u, h // 2][0])
            if 0 <= t - b < len(items):
                u, h = items[t - b]
                weighed[u, h] = weigh(u, h, scored.pop((u, h)))
            if 0 <= t - d < len(items):
                u, h = items[t - d]
                gather(u, h, mapped[u, h // 2][1], weighed.pop((u, h)))
        return 0

    half = BLOCKS // 2
    full = (total + half - 1) // BLOCKS
    done = full * BLOCKS
    lax.fori_loop(0, full, functools.partial(some_blocks, BLOCKS, 0), 0)
    lax.fori_loop(0, (total > done).astype(jnp.int32), functools.partial(some_blocks, half, done), 0)


def first_phase(shape, slots, *refs):
    owners, heads, tile, head_dim = shape
    n = len(slots)
    count, b_src, b_dst, b_type, prior = refs[:5]
    tiles = refs[5 : 5 + n]
    wk, wv, att, msg, wq = refs[5 + n : 10 + n]
    hubs = refs[10 + n : 10 + n + owners]
    queries, acc, top, den, order, src, keys, values = refs[10 + n + owners :]
    quad = 4 * head_dim
    acc[...] = jnp.zeros(acc.shape, F32)
    top[...] = jnp.full(top.shape, EMPTY, F32)
    den[...] = jnp.zeros(den.shape, F32)
    for lo in range(0, owners, n):
        some = range(lo, min(lo + n, owners))
        for i, t in enumerate(some):
            src[i * tile : (i + 1) * tile, :] = hubs[t][...]
        for c in range(0, heads * head_dim, quad):
            q = jnp.dot(src[...], wq[:, c : c + quad], preferred_element_type=F32)
            for i, t in enumerate(some):
                queries[t, c : c + quad, :] = q[i * tile : (i + 1) * tile, :].T.astype(BF)
    run_blocks(
        *shape, slots, count, b_src, b_dst, b_type, prior, tiles, wk, wv, att, msg,
        queries, acc, top, den, order, src, keys, values,
    )


def later_phase(shape, slots, last, *refs):
    owners, heads, tile, head_dim = shape
    n = len(slots)
    count, b_src, b_dst, b_type, prior = refs[:5]
    tiles = refs[5 : 5 + n]
    wk, wv, att, msg, queries = refs[5 + n : 10 + n]
    acc, top, den, *rest = refs[13 + n :]
    if last:
        outs, rest = rest[:owners], rest[owners:]
    order, src, keys, values = rest
    run_blocks(
        *shape, slots, count, b_src, b_dst, b_type, prior, tiles, wk, wv, att, msg,
        queries, acc, top, den, order, src, keys, values,
    )
    if last:
        for t in range(owners):
            total = den[t]
            some = total > 0.0
            safe = jnp.where(some, total, 1.0)
            lse = jnp.where(some, top[t] + jnp.log(safe) * LOG2E, EMPTY)
            inverse = 1.0 / safe
            for h in range(heads):
                rows = slice(h * head_dim, (h + 1) * head_dim)
                outs[t][rows, :] = (acc[t, rows, :] * inverse[h : h + 1, :]).astype(BF)
            parts = split3(lse)
            for k in range(3):
                base = heads * head_dim + k * heads
                outs[t][base : base + heads, :] = parts[k]


def combine(owners, heads, head_dim, *refs):
    parts, w_out, out, agg = refs[:owners], refs[owners], refs[owners + 1], refs[owners + 2]
    base = heads * head_dim
    lse = []
    for r in parts:
        hi, mid, lo = (r[base + k * heads : base + (k + 1) * heads, :].astype(F32) for k in range(3))
        lse.append((hi + mid) + lo)
    best = functools.reduce(jnp.maximum, lse)
    weights = [jnp.exp2(v - best) for v in lse]
    whole = functools.reduce(jnp.add, weights)
    weights = [w / whole for w in weights]
    for h in range(heads):
        rows = slice(h * head_dim, (h + 1) * head_dim)
        total = functools.reduce(
            jnp.add,
            [r[rows, :].astype(F32) * w[h : h + 1, :] for r, w in zip(parts, weights)],
        )
        agg[:, rows] = total.T.astype(BF)
    out[...] = jnp.dot(agg[...], w_out[...], preferred_element_type=F32).astype(BF)


def body(
    node_src,
    hub_feat,
    w_query,
    w_key,
    w_value,
    w_out,
    w_att,
    w_msg,
    relation_prior,
    block_src,
    block_dst,
    block_type,
    block_count,
):
    groups = lax.axis_size("grp")
    owners = lax.axis_size("dev")
    tile, width = hub_feat.shape
    relations, heads = relation_prior.shape
    head_dim = width // heads
    pair, pairs = 2 * head_dim, heads // 2
    quads = heads // 4
    length = block_src.shape[1]
    shape = (owners, heads, tile, head_dim)
    smem = pl.BlockSpec(memory_space=pltpu.SMEM)
    apart = lambda x: pltpu.with_memory_space_constraint(x, pltpu.HBM)
    keep = lambda x: pltpu.with_memory_space_constraint(x, pltpu.VMEM)
    w_out = keep(w_out)
    vmem = pl.BlockSpec(memory_space=pltpu.VMEM)

    def move(x, axis, size, k):
        return lax.ppermute(x, axis, [(i, i ^ k) for i in range(size)])

    hubs = {0: hub_feat}
    for k in range(2, owners):
        hubs[k] = move(hub_feat, "dev", owners, k)
    srcs = {0: node_src}
    if groups == 8:
        steps = [(0, 1), (2, 6), (3, 4), (7, 5)]
        swaps = {2: (4,)}
        for k in (1, 6):
            srcs[k] = move(node_src, "grp", groups, k)
    else:
        steps = [(k, k + 1) for k in range(0, groups, 2)]
        swaps = {}
        for k in range(1, groups):
            srcs[k] = move(node_src, "grp", groups, k)

    dense = (w_query, w_key, w_value, node_src, hub_feat)
    maps = [w.reshape(relations, pairs, pair, head_dim) for w in (w_att, w_msg)]
    chunks = 16
    att, msg, w_query, w_key, w_value, own_src, own_hub = pl.pallas_call(
        functools.partial(prepare, chunks),
        in_specs=[pl.BlockSpec(memory_space=pltpu.HBM)] * (2 + len(dense)),
        out_specs=[vmem] * (2 + len(dense)),
        out_shape=[pltpu.VMEM((relations, pairs, pair, pair), BF)] * 2
        + [pltpu.VMEM(x.shape, BF) for x in dense],
        scratch_shapes=[
            pltpu.VMEM((relations, pairs, pair, head_dim), BF),
            pltpu.VMEM((relations, pairs, pair, head_dim), BF),
            pltpu.SemaphoreType.DMA((2, chunks)),
            pltpu.SemaphoreType.DMA((len(dense),)),
        ],
        name="prepare",
        compiler_params=pltpu.CompilerParams(vmem_limit_bytes=LIMIT),
    )(*[apart(x) for x in (*maps, *dense)])
    hubs[1] = move(hub_feat, "dev", owners, 1)
    if groups == 8:
        source, hubs[1] = lax.optimization_barrier((node_src, hubs[1]))
        srcs[2] = move(source, "grp", groups, 2)
        srcs[4] = move(own_src, "grp", groups, 4)
        for k in (3, 7):
            srcs[k] = move(own_src, "grp", groups, k)
    srcs[0], hubs[0] = own_src, own_hub
    att, msg, w_query, w_key, w_value = (keep(x) for x in (att, msg, w_query, w_key, w_value))
    lists = (
        block_count,
        block_src,
        block_dst,
        block_type,
        relation_prior,
    )
    state = [
        pltpu.VMEM((owners, width, tile), F32),
        pltpu.VMEM((owners, heads, tile), F32),
        pltpu.VMEM((owners, heads, tile), F32),
    ]
    rows_out = width + 3 * heads
    sent = [pltpu.VMEM((rows_out, tile), BF)] * owners
    for i, slots in enumerate(steps):
        n = len(slots)
        if i in swaps:
            carry = list(carry)
            *held, carry[2] = lax.optimization_barrier((*[srcs[k] for k in swaps[i]], carry[2]))
            for k, tile_k in zip(swaps[i], held):
                srcs[k] = tile_k
                srcs[k + 1] = move(tile_k, "grp", groups, 1)
        scratch = [
            pltpu.SMEM((2, length + BLOCKS), jnp.int32),
            pltpu.VMEM((n * tile, width), BF),
            pltpu.VMEM((n, quads, tile, 2 * pair), BF),
            pltpu.VMEM((n, quads, 2 * pair, tile), BF),
        ]
        cost = pl.CostEstimate(flops=COST, bytes_accessed=1024, transcendentals=0)
        tiles = [keep(srcs[k]) for k in slots]
        if i == 0:
            queries, *carry = pl.pallas_call(
                functools.partial(first_phase, shape, slots),
                in_specs=[smem] * 5 + [vmem] * (n + 5 + owners),
                out_specs=[vmem] * 4,
                out_shape=[pltpu.VMEM((owners, width, tile), BF)] + state,
                scratch_shapes=scratch,
                cost_estimate=cost,
            compiler_params=pltpu.CompilerParams(vmem_limit_bytes=LIMIT),
                name="phase0",
            )(*lists, *tiles, w_key, w_value, att, msg, w_query, *[keep(hubs[k]) for k in range(owners)])
            continue
        last = i == len(steps) - 1
        base = 10 + n
        aliases = {base + k: k for k in range(3)}
        carry = pl.pallas_call(
            functools.partial(later_phase, shape, slots, last),
            in_specs=[smem] * 5 + [vmem] * (n + 8),
            out_specs=[vmem] * (3 + owners if last else 3),
            out_shape=state + sent if last else state,
            scratch_shapes=scratch,
            input_output_aliases=aliases,
            cost_estimate=cost,
            compiler_params=pltpu.CompilerParams(vmem_limit_bytes=LIMIT),
            name="phase%d" % i,
        )(*lists, *tiles, w_key, w_value, att, msg, queries, *carry)
    tiles = carry[3:]
    parts = [tiles[0]] + [move(tiles[k], "dev", owners, k) for k in range(1, owners)]
    return pl.pallas_call(
        functools.partial(combine, owners, heads, head_dim),
        out_shape=jax.ShapeDtypeStruct((tile, width), BF),
        scratch_shapes=[pltpu.VMEM((tile, width), BF)],
        compiler_params=pltpu.CompilerParams(vmem_limit_bytes=LIMIT),
        name="combine",
    )(*[keep(p) for p in parts], w_out)


def solution(mesh):
    rows = P(("grp", "dev"), None)
    placed = (rows, rows) + (P(),) * 7 + (rows,) * 3 + (P(("grp", "dev")),)
    return jax.shard_map(body, mesh=mesh, in_specs=placed, out_specs=rows, check_vma=False)
```
